32 devices in a mesh: dp: 8 (over z, x), tensor: 4 (over y, core).
Axes of the slice: x: 2, y: 2, z: 4, core: 2. Of those that a mesh axis runs over, the one named last changes fastest.
Arguments:
- hidden_in: bfloat16 [16384, 768], P('dp'), may hold values from -6 to 6
- seq_lengths: int32 [32, 4], P('dp'), may hold values from 0 to 512, as said below
- out_grad: bfloat16 [16384, 768], P('dp'), may hold values from -6 to 6
- query_weight: float32 [768, 768], P('dp', 'tensor'), may hold values from -0.3125 to 0.3125
- key_weight: float32 [768, 768], P('dp', 'tensor'), may hold values from -0.21875 to 0.21875
- value_weight: float32 [768, 768], P('dp', 'tensor'), may hold values from -0.21875 to 0.21875
- output_weight: float32 [768, 768], P('tensor', 'dp'), may hold values from -1.75 to 1.75
- up_weight: float32 [768, 3072], P('dp', 'tensor'), may hold values from -0.21875 to 0.21875
- down_weight: float32 [3072, 768], P('tensor', 'dp'), may hold values from -0.15625 to 0.15625
- query_bias: float32 [12, 64], P('tensor', 'dp'), may hold values from -1.5 to 1.5
- value_bias: float32 [12, 64], P('tensor', 'dp'), may hold values from -1.5 to 1.5
- inner_bias: float32 [4, 768], P('tensor', 'dp'), may hold values from -1.5 to 1.5
- output_bias: float32 [768], P('dp'), may hold values from -1.5 to 1.5
- down_bias: float32 [768], P('dp'), may hold values from -1.5 to 1.5
- first_gain: float32 [768], P('dp'), may hold values from 0.5 to 1.5
- first_shift: float32 [768], P('dp'), may hold values from -1.5 to 1.5
- second_gain: float32 [768], P('dp'), may hold values from 0.5 to 1.5
- second_shift: float32 [768], P('dp'), may hold values from -1.5 to 1.5
Outputs:
- hidden_out: bfloat16 [16384, 768], P(('dp', 'tensor'))
- grad_hidden: bfloat16 [16384, 768], P(('dp', 'tensor'))
- grad_query_weight: float32 [768, 768], P('dp', 'tensor')
- grad_key_weight: float32 [768, 768], P('dp', 'tensor')
- grad_value_weight: float32 [768, 768], P('dp', 'tensor')
- grad_output_weight: float32 [768, 768], P('tensor', 'dp')
- grad_up_weight: float32 [768, 3072], P('dp', 'tensor')
- grad_down_weight: float32 [3072, 768], P('tensor', 'dp')
- grad_query_bias: float32 [12, 64], P('tensor', 'dp')
- grad_value_bias: float32 [12, 64], P('tensor', 'dp')
- grad_inner_bias: float32 [4, 768], P('tensor', 'dp')
- grad_output_bias: float32 [768], P('dp')
- grad_down_bias: float32 [768], P('dp')
- grad_first_gain: float32 [768], P('dp')
- grad_first_shift: float32 [768], P('dp')
- grad_second_gain: float32 [768], P('dp')
- grad_second_shift: float32 [768], P('dp')
The draws below stay inside these ranges and needn't reach their ends.
Inputs may be any that keep to these rules, and one draw needn't show every extreme that they name: `seq_lengths`: each row holds 1 to 4 sequences in its leading slots, each of 128 to 512 tokens, together at most 512; unused slots hold 0; some row holds one sequence of 512 tokens.
All inputs are finite; a program needn't handle non-finite values.
Results may differ from the reference program's by a relative error of at most 0.023.
Values may be sent and summed in bfloat16 or wider, within the bound.
A program may use at most 128 MiB of HBM per device.

```python
import math
import jax
import jax.numpy as jnp
from jax import lax

D = 768
H = 12
DH = 64
FF = 3072
SEQ = 512
MIN_LEN = 128
SLOTS = 4
ROWS = 32
TOKENS = 16384
N_TENSOR = 4


def draw_seq_lengths(key, part):
    key_count, key_fill, key_cut = jax.random.split(jax.random.fold_in(key, 17), 3)
    count = jax.random.randint(key_count, (ROWS,), 1, SLOTS + 1)
    count = count.at[0].set(1)
    slack = SEQ - MIN_LEN * count
    fill = jax.random.randint(key_fill, (ROWS,), 0, slack + 1)
    fill = fill.at[0].set(slack[0])
    slot_index = jnp.arange(SLOTS, dtype=jnp.int32)[None, :]
    cuts = jax.random.randint(key_cut, (ROWS, SLOTS - 1), 0, fill[:, None] + 1)
    cuts = jnp.where(slot_index[:, :SLOTS - 1] >= count[:, None] - 1, fill[:, None], cuts)
    cuts = jnp.sort(cuts, axis=1)
    bounds = jnp.concatenate([jnp.zeros((ROWS, 1), jnp.int32), cuts.astype(jnp.int32), fill[:, None].astype(jnp.int32)], axis=1)
    extra = bounds[:, 1:] - bounds[:, :-1]
    lengths = jnp.where(slot_index < count[:, None], MIN_LEN + extra, 0)
    return lengths.astype(jnp.int32)


def steps_of(own_key, dims, cuts, smallest, top_value):
    def one(axis_at, shards_of):
        steps = jax.random.uniform(jax.random.fold_in(jax.random.fold_in(own_key, 6), axis_at), (shards_of,), jnp.float32, smallest / len(cuts), top_value / len(cuts))
        return jnp.repeat(jnp.exp(steps), dims[axis_at] // shards_of).reshape((-1,) + (1,) * (len(dims) - axis_at - 1))

    factor_of = one(*cuts[0])
    for cut in cuts[1:]:
        factor_of = factor_of * one(*cut)
    return factor_of


def normal_values(rng, extent, scale, limit, pieces=(), kind=jnp.bfloat16):
    level = steps_of(rng, extent, pieces, -0.22, 0.18) if pieces else 1.0
    drawn = jax.random.normal(rng, extent, jnp.float32) * scale * level
    return jnp.minimum(jnp.maximum(drawn, -limit), limit).astype(kind)


def setup_inputs(seed: int = 0) -> dict:
    arg_keys = jax.random.split(jax.random.key(seed), 19)
    hidden_in = normal_values(arg_keys[0], (TOKENS, D), 1.0, 6.0, ((0, 8),))
    seq_lengths = draw_seq_lengths(jax.random.fold_in(arg_keys[18], 71), 0)
    out_grad = normal_values(arg_keys[2], (TOKENS, D), 1.0, 6.0, ((0, 8),))
    query_weight = normal_values(arg_keys[3], (D, D), (D // 2) ** -0.5, 0.3125, ((0, 8), (1, 4)), jnp.float32)
    key_weight = normal_values(arg_keys[4], (D, D), D ** -0.5, 0.21875, ((0, 8), (1, 4)), jnp.float32)
    value_weight = normal_values(arg_keys[5], (D, D), D ** -0.5, 0.21875, ((0, 8), (1, 4)), jnp.float32)
    output_weight = normal_values(arg_keys[6], (D, D), (D // 64) ** -0.5, 1.75, ((0, 4), (1, 8)), jnp.float32)
    up_weight = normal_values(arg_keys[7], (D, FF), D ** -0.5, 0.21875, ((0, 8), (1, 4)), jnp.float32)
    down_weight = normal_values(arg_keys[8], (FF, D), (FF // 2) ** -0.5, 0.15625, ((0, 4), (1, 8)), jnp.float32)
    query_bias = normal_values(arg_keys[9], (H, DH), 0.3, 1.5, ((0, 4), (1, 8)), jnp.float32)
    value_bias = normal_values(arg_keys[10], (H, DH), 0.3, 1.5, ((0, 4), (1, 8)), jnp.float32)
    inner_bias = normal_values(arg_keys[11], (N_TENSOR, FF // N_TENSOR), 0.3, 1.5, ((0, 4), (1, 8)), jnp.float32)
    output_bias = normal_values(arg_keys[12], (D,), 0.3, 1.5, ((0, 8),), jnp.float32)
    down_bias = normal_values(arg_keys[13], (D,), 0.3, 1.5, ((0, 8),), jnp.float32)
    first_gain = jnp.clip(1.0 + 0.1 * jax.random.normal(arg_keys[14], (D,), jnp.float32), 0.5, 1.5)
    first_shift = normal_values(arg_keys[15], (D,), 0.3, 1.5, ((0, 8),), jnp.float32)
    second_gain = jnp.clip(1.0 + 0.1 * jax.random.normal(arg_keys[16], (D,), jnp.float32), 0.5, 1.5)
    second_shift = normal_values(arg_keys[17], (D,), 0.3, 1.5, ((0, 8),), jnp.float32)
    return {"hidden_in": hidden_in, "seq_lengths": seq_lengths, "out_grad": out_grad, "query_weight": query_weight, "key_weight": key_weight, "value_weight": value_weight, "output_weight": output_weight, "up_weight": up_weight, "down_weight": down_weight, "query_bias": query_bias, "value_bias": value_bias, "inner_bias": inner_bias, "output_bias": output_bias, "down_bias": down_bias, "first_gain": first_gain, "first_shift": first_shift, "second_gain": second_gain, "second_shift": second_shift}


EPS = 1e-12
NEGATIVE = -1000000000.0

@jax.custom_vjp
def low(v):
    return lax.optimization_barrier(v.astype(jnp.bfloat16)).astype(jnp.float32)

@jax.custom_vjp
def low_back(v):
    return v

def low_keep(v):
    return (low(v), None)

def low_pass(kept, grad):
    return (grad,)

def back_keep(v):
    return (v, None)

def back_low(kept, grad):
    return (low(grad),)
low.defvjp(low_keep, low_pass)
low_back.defvjp(back_keep, back_low)

def highest(left, right):
    return jnp.dot(left, right, precision=lax.Precision.HIGHEST)

def layer_norm(values, gain, shift):
    centred = values - lax.optimization_barrier(jnp.mean(values, axis=-1, keepdims=True))
    spread = lax.optimization_barrier(jnp.mean(centred * centred, axis=-1, keepdims=True))
    return centred * lax.rsqrt(spread + EPS) * gain + shift

def row_masks(lengths):
    ends = jnp.cumsum(lengths, axis=1).astype(jnp.int32)
    places = jnp.arange(SEQ, dtype=jnp.int32)
    segment = lax.optimization_barrier(jnp.sum((places[None, :, None] >= ends[:, None, :]).astype(jnp.int32), axis=2))
    valid = places[None, :] < ends[:, -1:]
    same = segment[:, :, None] == segment[:, None, :]
    diagonal = places[:, None] == places[None, :]
    allowed = jnp.where(valid[:, :, None], same, diagonal[None])
    return (allowed, valid)

def attend_group(inputs):
    queries, keys, values, allowed = inputs
    group = queries.shape[0]
    query_heads = queries.reshape(group, SEQ, H, DH)
    key_heads = keys.reshape(group, SEQ, H, DH)
    value_heads = values.reshape(group, SEQ, H, DH)
    scores = jnp.einsum('gqhd,gkhd->ghqk', query_heads, key_heads, precision=lax.Precision.HIGHEST) * DH ** (-0.5)
    scores = low_back(jnp.where(allowed[:, None], scores, NEGATIVE))
    weights = low(jax.nn.softmax(scores, axis=-1))
    mixed = jnp.einsum('ghqk,gkhd->gqhd', weights, value_heads, precision=lax.Precision.HIGHEST)
    return mixed.reshape(group, SEQ, D)

def layer(hidden, params, allowed):
    rounded = [low(item) for item in params]
    query_w, key_w, value_w, output_w, up_w, down_w = rounded[0:6]
    query_b, value_b, inner_b, output_b, down_b = rounded[6:11]
    gain_one, shift_one, gain_two, shift_two = rounded[11:15]
    queries = low_back(low(highest(hidden, query_w) + query_b.reshape(-1)))
    keys = low_back(low(highest(hidden, key_w)))
    values = low_back(low(highest(hidden, value_w) + value_b.reshape(-1)))
    group = math.gcd(ROWS, 8)
    blocks = ROWS // group
    mixed = lax.map(jax.checkpoint(attend_group), (queries.reshape(blocks, group, SEQ, D), keys.reshape(blocks, group, SEQ, D), values.reshape(blocks, group, SEQ, D), allowed.reshape(blocks, group, SEQ, SEQ)))
    mixed = low_back(low(mixed.reshape(TOKENS, D)))
    attn_out = low_back(highest(mixed, output_w) + output_b)
    normed = layer_norm(hidden + attn_out, gain_one, shift_one)
    inner = low_back(highest(low(normed), up_w) + inner_b.reshape(-1))
    activated = low(jax.nn.gelu(inner, approximate=False))
    down_out = low_back(highest(activated, down_w) + down_b)
    return layer_norm(normed + down_out, gain_two, shift_two)

def reference(hidden_in, seq_lengths, out_grad, query_weight, key_weight, value_weight, output_weight, up_weight, down_weight, query_bias, value_bias, inner_bias, output_bias, down_bias, first_gain, first_shift, second_gain, second_shift):
    allowed, valid = row_masks(seq_lengths)
    params = (query_weight, key_weight, value_weight, output_weight, up_weight, down_weight, query_bias, value_bias, inner_bias, output_bias, down_bias, first_gain, first_shift, second_gain, second_shift)
    hidden = hidden_in.astype(jnp.float32)

    def forward(state, weights):
        return layer(state, weights, allowed)
    final, pullback = jax.vjp(forward, hidden, params)
    cotangent = out_grad.astype(jnp.float32) * valid.reshape(TOKENS, 1).astype(jnp.float32)
    hidden_grad, grads = pullback(cotangent)
    return (final.astype(jnp.bfloat16), hidden_grad.astype(jnp.bfloat16), grads[0], grads[1], grads[2], grads[3], grads[4], grads[5], grads[6], grads[7], grads[8], grads[9], grads[10], grads[11], grads[12], grads[13], grads[14])
```

```python
import functools

import jax
import jax.numpy as jnp
from jax import lax
from jax.experimental import pallas as pl
from jax.experimental.pallas import tpu as pltpu
from jax.sharding import PartitionSpec as P

H = 12
DH = 64
SEQ = 512
D = 768
EPS = 1e-12
NEGATIVE = -1000000000.0
MESH = pl.DeviceIdType.MESH
BF = jnp.bfloat16
F32 = jnp.float32
DMA = pltpu.SemaphoreType.DMA


class Place:
    def __init__(self, r):
        dp = lax.axis_index("dp")
        t = lax.axis_index("tensor")
        g = lax.div(dp, r)
        self.r, self.q = r, lax.rem(dp, r)
        self.z, self.x = lax.div(g, 2), lax.rem(g, 2)
        self.y, self.c = lax.div(t, 2), lax.rem(t, 2)
        self.xn, self.yn, self.cn = 1 - self.x, 1 - self.y, 1 - self.c
        self.zs = [lax.rem(self.z + i, 4) for i in range(4)]

    def dev(self, z, x, y, c):
        return {"dp": (2 * z + x) * self.r + self.q, "tensor": 2 * y + c}

    def across_z(self, i):
        return self.dev(self.zs[i], self.x, self.y, self.c)

    def across_x(self):
        return self.dev(self.z, self.xn, self.y, self.c)

    def across_y(self):
        return self.dev(self.z, self.x, self.yn, self.c)

    def partner(self):
        return self.dev(self.z, self.x, self.y, self.cn)

    def barrier(self):
        peers = [self.across_z(i) for i in (1, 2, 3)]
        peers += [self.across_x(), self.across_y(), self.partner()]
        bar = pltpu.get_barrier_semaphore()
        for peer in peers:
            pl.semaphore_signal(bar, inc=1, device_id=peer, device_id_type=MESH)
        pl.semaphore_wait(bar, len(peers))


class Sender:
    def __init__(self):
        self.sent = []

    def __call__(self, src, dst, ss, rs, to):
        cp = pltpu.make_async_remote_copy(
            src_ref=src, dst_ref=dst, send_sem=ss, recv_sem=rs, device_id=to, device_id_type=MESH
        )
        cp.start()
        self.sent.append(cp)

    def finish(self):
        for cp in self.sent:
            cp.wait_send()


def arrived(ref, sem):
    pltpu.make_async_copy(ref, ref, sem).wait()


def rows(z, x):
    return pl.ds(pl.multiple_of((2 * z + x) * 96, 96), 96)


def gather_kernel(
    r, own_ref, small_ref, w_ref, s_ref, vbuf, sbuf,
    lsem, sz, sx, sy, sfx, sfy, sp, rz, rx, ry, rfx, rfy, rp, ssend, srecv,
):
    me = Place(r)
    z, x, y, c, xn, yn, cn, zs = me.z, me.x, me.y, me.c, me.xn, me.yn, me.cn, me.zs
    sbuf[c, x, y, z] = small_ref[...]
    me.barrier()
    send = Sender()

    def unit(k, z, x, y, c, half=None):
        if half is None:
            return vbuf.at[k, 2 * y + c, rows(z, x)]
        return vbuf.at[k, 2 * y + c, rows(z, x), pl.ds(384 * half, 384)]

    def own(k):
        src, dst = own_ref.at[k], unit(k, z, x, y, c)
        for i in (1, 3, 2):
            send(src, dst, sz.at[k, i], rz.at[k, z], me.across_z(i))
        send(src, dst, sx.at[k, 0], rx.at[k, z], me.across_x())
        send(src, dst, sy.at[k, 0], ry.at[k, z], me.across_y())
        send(src, dst, sp.at[k, 0, 0], rp.at[k, z, 0], me.partner())
        cp = pltpu.make_async_copy(src, dst, lsem.at[k])
        cp.start()
        return cp

    def from_z(k):
        for i in (1, 3, 2):
            u = unit(k, zs[i], x, y, c)
            arrived(u, rz.at[k, zs[i]])
            send(u, u, sx.at[k, i], rx.at[k, zs[i]], me.across_x())
            send(u, u, sy.at[k, i], ry.at[k, zs[i]], me.across_y())
            send(u, u, sp.at[k, i, 0], rp.at[k, zs[i], 0], me.partner())

    def from_xy(k):
        for i in (0, 1, 3, 2):
            u = unit(k, zs[i], xn, y, c)
            arrived(u, rx.at[k, zs[i]])
            h = unit(k, zs[i], xn, y, c, 0)
            send(h, h, sfy.at[k, i], rfy.at[k, zs[i]], me.across_y())
            send(u, u, sp.at[k, i, 1], rp.at[k, zs[i], 1], me.partner())
            u = unit(k, zs[i], x, yn, c)
            arrived(u, ry.at[k, zs[i]])
            h = unit(k, zs[i], x, yn, c, 1)
            send(h, h, sfx.at[k, i], rfx.at[k, zs[i]], me.across_x())
            send(u, u, sp.at[k, i, 2], rp.at[k, zs[i], 2], me.partner())

    def from_far(k):
        for i in (0, 1, 3, 2):
            arrived(unit(k, zs[i], xn, yn, c, 0), rfy.at[k, zs[i]])
            arrived(unit(k, zs[i], xn, yn, c, 1), rfx.at[k, zs[i]])
            u = unit(k, zs[i], xn, yn, c)
            send(u, u, sp.at[k, i, 3], rp.at[k, zs[i], 3], me.partner())

    def from_partner(k):
        for i in range(4):
            for j, (a, b) in enumerate(((x, y), (xn, y), (x, yn), (xn, yn))):
                arrived(unit(k, zs[i], a, b, cn), rp.at[k, zs[i], j])

    mine = sbuf.at[c, x, y, z]
    for i in (1, 2, 3):
        send(mine, mine, ssend.at[i], srecv.at[z], me.across_z(i))
    local = [own(0)]
    from_z(0)
    for i in (1, 2, 3):
        arrived(mine, srecv.at[zs[i]])
    mine = sbuf.at[c, x, y]
    send(mine, mine, ssend.at[4], srecv.at[4], me.across_x())
    local.append(own(1))
    arrived(mine, srecv.at[4])
    for b in range(2):
        mine = sbuf.at[c, b, y]
        send(mine, mine, ssend.at[5 + b], srecv.at[5 + b], me.across_y())
    from_xy(0)
    from_z(1)
    for b in range(2):
        arrived(mine, srecv.at[5 + b])
    send(sbuf.at[c], sbuf.at[c], ssend.at[7], srecv.at[7], me.partner())
    local.append(own(2))
    from_xy(1)
    from_far(0)
    from_z(2)
    from_far(1)
    from_xy(2)
    from_far(2)
    arrived(sbuf.at[c], srecv.at[7])
    from_partner(0)
    from_partner(1)
    from_partner(2)
    for cp in local:
        cp.wait()
    send.finish()
    cp = pltpu.make_async_copy(vbuf, w_ref, lsem.at[0])
    cp.start()
    s_ref[...] = sbuf[...]
    cp.wait()


def gather(r, own, small):
    return pl.pallas_call(
        functools.partial(gather_kernel, r),
        out_shape=(
            jax.ShapeDtypeStruct((3, 4, D, D), BF),
            jax.ShapeDtypeStruct((2, 2, 2, 4, 8, 128), F32),
        ),
        in_specs=[pl.BlockSpec(memory_space=pltpu.VMEM)] * 2,
        out_specs=(pl.BlockSpec(memory_space=pl.ANY), pl.BlockSpec(memory_space=pltpu.VMEM)),
        scratch_shapes=[
            pltpu.VMEM((3, 4, D, D), BF),
            pltpu.VMEM((2, 2, 2, 4, 8, 128), F32),
            DMA((3,)), DMA((3, 4)), DMA((3, 4)), DMA((3, 4)), DMA((3, 4)), DMA((3, 4)), DMA((3, 4, 4)),
            DMA((3, 4)), DMA((3, 4)), DMA((3, 4)), DMA((3, 4)), DMA((3, 4)), DMA((3, 4, 4)),
            DMA((8,)), DMA((8,)),
        ],
        compiler_params=pltpu.CompilerParams(
            collective_id=0, has_side_effects=True, vmem_limit_bytes=60 * 2**20
        ),
    )(own, small)


def reduce_kernel(
    r, g_ref, small_ref, o_ref, so_ref, gbuf, pbuf, dx, dy, ex, ey, zb, sbuf, s1, s2, s3, s4,
    lsem, sp, s_dx, s_dy, s_ex, s_ey, s_z, rp, r_dx, r_dy, r_ex, r_ey, r_z, ssend, srecv,
):
    me = Place(r)
    z, x, y, c, xn, yn, cn, zs = me.z, me.x, me.y, me.c, me.xn, me.yn, me.cn, me.zs
    order = (1, 2, 0)
    loads = {}
    for k in order:
        for j, b in enumerate((2 * yn + cn, 2 * yn + c, 2 * y + cn, 2 * y + c)):
            cp = pltpu.make_async_copy(g_ref.at[k, b], gbuf.at[k, b], lsem.at[k, j])
            cp.start()
            loads[k, j] = cp
    sbuf[...] = small_ref[...]
    me.barrier()
    send = Sender()
    send(sbuf.at[cn], s1, ssend.at[0], srecv.at[0], me.partner())

    def pair(k):
        for j, yy in ((0, yn), (2, y)):
            loads[k, j].wait()
            send(gbuf.at[k, 2 * yy + cn], pbuf.at[k, yy], sp.at[k, j], rp.at[k, yy], me.partner())
        for j, yy in ((1, yn), (3, y)):
            loads[k, j].wait()
            arrived(pbuf.at[k, yy], rp.at[k, yy])

            def add(i, _, yy=yy):
                s = pl.ds(pl.multiple_of(i * 96, 96), 96)
                gbuf[k, 2 * yy + c, s] = gbuf[k, 2 * yy + c, s] + pbuf[k, yy, s]
                return 0

            lax.fori_loop(0, 8, add, 0)

    def first(k):
        for i in (2, 1, 3, 0):
            u = gbuf.at[k, 2 * yn + c, rows(zs[i], xn)]
            send(u.at[:, pl.ds(0, 384)], dx.at[k, zs[i]], s_dx.at[k, i], r_dx.at[k, zs[i]], me.across_x())
            send(u.at[:, pl.ds(384, 384)], dy.at[k, zs[i]], s_dy.at[k, i], r_dy.at[k, zs[i]], me.across_y())

    def second(k):
        for i in (2, 1, 3, 0):
            u = gbuf.at[k, 2 * yn + c, rows(zs[i], x)]
            arrived(dx.at[k, zs[i]], r_dx.at[k, zs[i]])
            u[:, 0:384] = u[:, 0:384] + dx[k, zs[i]]
            send(u, ey.at[k, zs[i]], s_ey.at[k, i], r_ey.at[k, zs[i]], me.across_y())
            u = gbuf.at[k, 2 * y + c, rows(zs[i], xn)]
            arrived(dy.at[k, zs[i]], r_dy.at[k, zs[i]])
            u[:, 384:768] = u[:, 384:768] + dy[k, zs[i]]
            send(u, ex.at[k, zs[i]], s_ex.at[k, i], r_ex.at[k, zs[i]], me.across_x())

    def third(k):
        for i in (2, 1, 3, 0):
            u = gbuf.at[k, 2 * y + c, rows(zs[i], x)]
            arrived(ex.at[k, zs[i]], r_ex.at[k, zs[i]])
            arrived(ey.at[k, zs[i]], r_ey.at[k, zs[i]])
            s = u[...].astype(F32) + ex[k, zs[i]].astype(F32) + ey[k, zs[i]].astype(F32)
            if i:
                u[...] = s.astype(BF)
                send(u, zb.at[k, z], s_z.at[k, i], r_z.at[k, z], me.across_z(i))
            else:
                o_ref[k] = s

    def last(k):
        for i in (1, 3, 2):
            arrived(zb.at[k, zs[i]], r_z.at[k, zs[i]])
            o_ref[k] = o_ref[k] + zb[k, zs[i]].astype(F32)

    a, b, d = order
    pair(a)
    first(a)
    pair(b)
    first(b)
    second(a)
    arrived(s1, srecv.at[0])
    sbuf[c] = sbuf[c] + s1[...]
    send(sbuf.at[c, xn], s2, ssend.at[1], srecv.at[1], me.across_x())
    pair(d)
    first(d)
    second(b)
    arrived(s2, srecv.at[1])
    sbuf[c, x] = sbuf[c, x] + s2[...]
    send(sbuf.at[c, x, yn], s3, ssend.at[2], srecv.at[2], me.across_y())
    third(a)
    second(d)
    arrived(s3, srecv.at[2])
    sbuf[c, x, y] = sbuf[c, x, y] + s3[...]
    for i in (1, 2, 3):
        send(sbuf.at[c, x, y, zs[i]], s4.at[z], ssend.at[2 + i], srecv.at[3 + z], me.across_z(i))
    third(b)
    third(d)
    last(a)
    last(b)
    last(d)
    total = sbuf[c, x, y, z]
    for i in (1, 2, 3):
        arrived(s4.at[zs[i]], srecv.at[3 + zs[i]])
        total = total + s4[zs[i]]
    so_ref[...] = total
    send.finish()


def reduce(r, grads, small):
    unit = (96, D)
    half = (96, 384)
    return pl.pallas_call(
        functools.partial(reduce_kernel, r),
        out_shape=(
            jax.ShapeDtypeStruct((3, 96, D), F32),
            jax.ShapeDtypeStruct((8, 128), F32),
        ),
        in_specs=[pl.BlockSpec(memory_space=pl.ANY), pl.BlockSpec(memory_space=pltpu.VMEM)],
        out_specs=(pl.BlockSpec(memory_space=pltpu.VMEM),) * 2,
        scratch_shapes=[
            pltpu.VMEM((3, 4, D, D), BF),
            pltpu.VMEM((3, 2, D, D), BF),
            pltpu.VMEM((3, 4) + half, BF), pltpu.VMEM((3, 4) + half, BF),
            pltpu.VMEM((3, 4) + unit, BF), pltpu.VMEM((3, 4) + unit, BF), pltpu.VMEM((3, 4) + unit, BF),
            pltpu.VMEM((2, 2, 2, 4, 8, 128), F32),
            pltpu.VMEM((2, 2, 4, 8, 128), F32), pltpu.VMEM((2, 4, 8, 128), F32),
            pltpu.VMEM((4, 8, 128), F32), pltpu.VMEM((4, 8, 128), F32),
            DMA((3, 4)), DMA((3, 4)), DMA((3, 4)), DMA((3, 4)), DMA((3, 4)), DMA((3, 4)), DMA((3, 4)),
            DMA((3, 2)), DMA((3, 4)), DMA((3, 4)), DMA((3, 4)), DMA((3, 4)), DMA((3, 4)),
            DMA((8,)), DMA((8,)),
        ],
        compiler_params=pltpu.CompilerParams(
            collective_id=1, has_side_effects=True, vmem_limit_bytes=60 * 2**20
        ),
    )(grads, small)


def layer_norm(values, gain, shift):
    centred = values - jnp.mean(values, axis=-1, keepdims=True)
    spread = jnp.mean(centred * centred, axis=-1, keepdims=True)
    return centred * lax.rsqrt(spread + EPS) * gain + shift


def gelu_exact(values):
    return jax.nn.gelu(values, approximate=False)


def dot(left, right, dims):
    return lax.dot_general(left, right, (dims, ((), ())), preferred_element_type=F32)


def row_mask(lengths):
    ends = jnp.cumsum(lengths)
    places = jnp.arange(SEQ, dtype=jnp.int32)
    segment = jnp.sum((places[:, None] >= ends[None, :]).astype(jnp.int32), axis=1)
    valid = places < ends[-1]
    same = segment[:, None] == segment[None, :]
    diagonal = places[:, None] == places[None, :]
    return jnp.where(valid[:, None], same, diagonal), valid


def layer(x, lengths, cot, weights, smalls):
    wa, w1, w2 = weights[0], weights[1], weights[2]
    bq, bv, c1, bo, c2, g1, b1, g2, b2 = smalls
    scale = DH ** (-0.5)
    allowed, valid = row_mask(lengths)
    wq, wk, wv, wo = (
        wa[:, :, 192 * i : 192 * (i + 1)].transpose(1, 0, 2).reshape(D, D) for i in range(4)
    )
    up = w1.transpose(1, 0, 2).reshape(D, 4 * D)
    down = w2.transpose(1, 0, 2).reshape(D, 4 * D)
    q = (dot(x, wq, ((1,), (0,))) + bq).astype(BF)
    k = dot(x, wk, ((1,), (0,))).astype(BF)
    v = (dot(x, wv, ((1,), (0,))) + bv).astype(BF)
    qh, kh, vh = (i.reshape(SEQ, H, DH) for i in (q, k, v))
    scores = jnp.einsum("qhd,khd->hqk", qh, kh, preferred_element_type=F32) * scale
    scores = jnp.where(allowed[None], scores, NEGATIVE)
    top = jnp.max(scores, axis=-1, keepdims=True)
    e = jnp.exp(scores - top)
    full = e / jnp.sum(e, axis=-1, keepdims=True)
    low = full.astype(BF)
    mixed = jnp.einsum("hqk,khd->qhd", low, vh, preferred_element_type=F32)
    mixed = mixed.reshape(SEQ, D).astype(BF)
    attn = dot(mixed, wo, ((1,), (1,))) + bo
    normed, first_back = jax.vjp(layer_norm, x.astype(F32) + attn, g1, b1)
    normed_low = normed.astype(BF)
    inner = dot(normed_low, up, ((1,), (0,))) + c1
    act, gelu_back = jax.vjp(gelu_exact, inner)
    act = act.astype(BF)
    out, second_back = jax.vjp(layer_norm, normed + dot(act, down, ((1,), (1,))) + c2, g2, b2)
    hidden = out.astype(BF)
    second, gg2, gb2 = second_back(cot.astype(F32) * valid[:, None].astype(F32))
    dg = second.astype(BF)
    gc2 = jnp.sum(dg.astype(F32), axis=0)
    gdown = dot(dg, act, ((0,), (0,)))
    ig = gelu_back(dot(dg, down, ((1,), (0,))))[0].astype(BF)
    gc1 = jnp.sum(ig.astype(F32), axis=0)
    gup = dot(normed_low, ig, ((0,), (0,)))
    ng = dot(ig, up, ((1,), (1,))) + second
    first, gg1, gb1 = first_back(ng)
    ag = first.astype(BF)
    gbo = jnp.sum(ag.astype(F32), axis=0)
    gwo = dot(ag, mixed, ((0,), (0,)))
    mg = dot(ag, wo, ((1,), (0,))).astype(BF)
    mh = mg.reshape(SEQ, H, DH)
    pg = jnp.einsum("qhd,khd->hqk", mh, vh, preferred_element_type=F32)
    vg = jnp.einsum("hqk,qhd->khd", low, mh, preferred_element_type=F32)
    sg = (full * (pg - jnp.sum(full * pg, axis=-1, keepdims=True))).astype(BF)
    qg = jnp.einsum("hqk,khd->qhd", sg, kh, preferred_element_type=F32) * scale
    kg = jnp.einsum("hqk,qhd->khd", sg, qh, preferred_element_type=F32) * scale
    qg, kg, vg = (i.reshape(SEQ, D).astype(BF) for i in (qg, kg, vg))
    gwq, gwk, gwv = (dot(x, i, ((0,), (0,))) for i in (qg, kg, vg))
    gbq, gbv = (jnp.sum(i.astype(F32), axis=0) for i in (qg, vg))
    gx = dot(qg, wq, ((1,), (1,))) + dot(kg, wk, ((1,), (1,))) + dot(vg, wv, ((1,), (1,))) + first
    blocks = lambda i: i.reshape(D, 4, -1).transpose(1, 0, 2)
    ga = jnp.concatenate([blocks(i) for i in (gwq, gwk, gwv, gwo)], axis=2)
    grads = jnp.stack([ga, blocks(gup), blocks(gdown)]).astype(BF)
    return hidden, gx.astype(BF), grads, (gbq, gbv, gc1, gbo, gc2, gg1, gb1, gg2, gb2)


def body(
    hidden_in, seq_lengths, out_grad, query_weight, key_weight, value_weight, output_weight, up_weight,
    down_weight, query_bias, value_bias, inner_bias, output_bias, down_bias, first_gain, first_shift,
    second_gain, second_shift,
):
    n = lax.axis_size("dp")
    r = n // 8
    t = lax.axis_index("tensor")
    own = jnp.stack(
        [
            jnp.concatenate([query_weight, key_weight, value_weight, output_weight.T], axis=1),
            up_weight,
            down_weight.T,
        ]
    ).astype(BF)
    heads = jnp.concatenate([query_bias, value_bias], axis=0)
    vectors = [inner_bias, output_bias, down_bias, first_gain, first_shift, second_gain, second_shift]
    vectors = jnp.stack([i.reshape(-1) for i in vectors])
    if r > 1:
        groups = [[g * r + i for i in range(r)] for g in range(8)]
        own = lax.all_gather(own, "dp", axis=1, tiled=True, axis_index_groups=groups)
        heads = lax.all_gather(heads.astype(BF), "dp", axis=1, tiled=True, axis_index_groups=groups)
        vectors = lax.all_gather(vectors.astype(BF), "dp", axis=1, tiled=True, axis_index_groups=groups)
    heads = heads.astype(BF).astype(F32).reshape(1, 48)
    vectors = vectors.astype(BF).astype(F32)
    small = jnp.concatenate([jnp.pad(vectors, ((0, 0), (0, 32))), jnp.pad(heads, ((0, 0), (0, 80)))])
    weights, s = gather(r, own, small)
    s = s.transpose(3, 1, 2, 0, 4, 5).reshape(8, 4, 8, 128)
    vec = s[:, :, 0:7, 0:96]
    c1 = vec[:, :, 0].transpose(1, 0, 2).reshape(-1)
    bo, c2, g1, b1, g2, b2 = (vec[:, 0, i].reshape(D) for i in range(1, 7))
    hb = s[:, :, 7, 0:48].reshape(8, 4, 2, 3, 8).transpose(2, 1, 3, 0, 4).reshape(2, D)
    cut = lambda a: lax.dynamic_slice_in_dim(a, t * SEQ, SEQ, 0)
    x, cot = cut(hidden_in), cut(out_grad)
    lengths = lax.dynamic_slice_in_dim(seq_lengths, t, 1, 0)[0]
    hidden, gx, grads, gs = layer(x, lengths, cot, weights, (hb[0], hb[1], c1, bo, c2, g1, b1, g2, b2))
    gbq, gbv, gc1, gbo, gc2, gg1, gb1, gg2, gb2 = gs
    six = jnp.stack([i.reshape(8, 96) for i in (gbo, gc2, gg1, gb1, gg2, gb2)], axis=1)
    six = jnp.broadcast_to(six[:, None], (8, 4, 6, 96))
    gv = jnp.concatenate([gc1.reshape(4, 8, 1, 96).transpose(1, 0, 2, 3), six], axis=2)
    gh = jnp.stack([gbq, gbv]).reshape(2, 4, 3, 8, 8).transpose(3, 1, 0, 2, 4).reshape(8, 4, 1, 48)
    gs = jnp.concatenate(
        [jnp.pad(gv, ((0, 0), (0, 0), (0, 0), (0, 32))), jnp.pad(gh, ((0, 0), (0, 0), (0, 0), (0, 80)))],
        axis=2,
    )
    gs = gs.reshape(4, 2, 2, 2, 8, 128).transpose(3, 1, 2, 0, 4, 5)
    gw, gs = reduce(r, grads, gs)
    gv = gs[0:7, 0:96]
    gh = gs[7, 0:48].reshape(6, 8)
    if r > 1:
        gw = lax.psum_scatter(gw, "dp", scatter_dimension=1, tiled=True, axis_index_groups=groups)
        gv = lax.psum_scatter(gv, "dp", scatter_dimension=1, tiled=True, axis_index_groups=groups)
        gh = lax.psum_scatter(gh, "dp", scatter_dimension=1, tiled=True, axis_index_groups=groups)
    a = gw[0]
    return (
        hidden,
        gx,
        a[:, 0:192],
        a[:, 192:384],
        a[:, 384:576],
        a[:, 576:768].T,
        gw[1],
        gw[2].T,
        gh[0:3],
        gh[3:6],
        gv[0:1],
        gv[1],
        gv[2],
        gv[3],
        gv[4],
        gv[5],
        gv[6],
    )


def solution(mesh):
    both, dp = P(("dp", "tensor"), None), P("dp")
    rows_first, columns_first = P("dp", "tensor"), P("tensor", "dp")
    weights = (rows_first,) * 3 + (columns_first, rows_first, columns_first)
    smalls = (columns_first,) * 3 + (dp,) * 6
    return jax.shard_map(
        body,
        mesh=mesh,
        in_specs=(P("dp", None),) * 3 + weights + smalls,
        out_specs=(both, both) + weights + smalls,
        check_vma=False,
    )
```

```python
import functools

import jax
import jax.numpy as jnp
from jax import lax
from jax.experimental import pallas as pl
from jax.experimental.pallas import tpu as pltpu
from jax.sharding import PartitionSpec as P

SEQ = 512
D = 768
EPS = 1e-12
NEGATIVE = -1000000000.0
MESH = pl.DeviceIdType.MESH
BF = jnp.bfloat16
F32 = jnp.float32
DMA = pltpu.SemaphoreType.DMA
NN, NT, TN = ((1,), (0,)), ((1,), (1,)), ((0,), (0,))
HEADS = ((0, 1, 2, 5, 0, 0, 0), (0, 1, 2, 5, 1, 1, 1), (3, 4, 3, 4, 0, 1, 1))
SLOTS = (0, 64, 384, 256, 320, 448)
CHUNK = 256
ITEMS = 1 + 2 * (D // CHUNK)


def dot(a, b, dims):
    return lax.dot_general(a, b, (dims, ((), ())), preferred_element_type=F32)


def iota(shape, axis):
    return lax.broadcasted_iota(jnp.int32, shape, axis)


class Place:
    def __init__(self, r):
        dp = lax.axis_index("dp")
        t = lax.axis_index("tensor")
        g = lax.div(dp, r)
        self.r, self.q, self.t = r, lax.rem(dp, r), t
        self.z, self.x = lax.div(g, 2), lax.rem(g, 2)
        self.y, self.c = lax.div(t, 2), lax.rem(t, 2)
        self.xn, self.yn, self.cn = 1 - self.x, 1 - self.y, 1 - self.c
        self.zs = [lax.rem(self.z + i, 4) for i in range(4)]
        self.to_x = self.dev(self.z, self.xn, self.y, self.c)
        self.to_y = self.dev(self.z, self.x, self.yn, self.c)
        self.to_core = self.dev(self.z, self.x, self.y, self.cn)
        self.to_z = [self.dev(self.zs[i], self.x, self.y, self.c) for i in range(4)]
        self.peers = self.to_z[1:] + [self.to_x, self.to_y, self.to_core]

    def dev(self, z, x, y, c):
        return {"dp": (2 * z + x) * self.r + self.q, "tensor": 2 * y + c}


def remote(src, dst, ss, rs, to):
    return pltpu.make_async_remote_copy(
        src_ref=src, dst_ref=dst, send_sem=ss, recv_sem=rs, device_id=to, device_id_type=MESH
    )


def arrived(ref, sem):
    pltpu.make_async_copy(ref, ref, sem).wait()


def rows(z, x, first=0, count=96):
    return pl.ds(pl.multiple_of((2 * z + x) * 96 + first, 16), count)


def spread(d):
    lane, col = iota((128, D), 0), iota((128, D), 1)
    vec = (col == lane + 96 * d) & (lane < 96)
    head = ((col & 63) == lane + 8 * d) & (lane < 8)
    return vec.astype(F32).astype(BF), head.astype(F32).astype(BF)


def kernel(
    r,
    lens_ref, x_hbm, cot_hbm, wq_ref, wk_ref, wv_ref, wo_ref, w1_ref, w2_ref,
    bq_ref, bv_ref, c1_ref, bo_ref, c2_ref, g1_ref, b1_ref, g2_ref, b2_ref,
    hid_hbm, gx_hbm, o_ref, so_ref,
    own, w, g12, rb12, small, sb, vec_s, bqv_s, a_s, p_s, z1_s, rs1_s, acc, act_s, gp_s, nl_s,
    x_s, cot_s, dg_s, ig_s, ag_s, da_s, gv_s, s1, s2, s3, s4,
    io_sem, ownl, sz, sx, sy, sfx, sfy, sp, rz, rx, ry, rfx, rfy, rp, ssm, rsm,
    gsp, gsdx, gsdy, gsex, gsey, gsz, grp, grdx, grdy, grex, grey, grz, gssm, grsm, ready,
):
    me = Place(r)
    z, x, y, c, xn, yn, cn, zs = me.z, me.x, me.y, me.c, me.xn, me.yn, me.cn, me.zs
    bar = pltpu.get_barrier_semaphore()
    for peer in me.peers:
        pl.semaphore_signal(bar, inc=1, device_id=peer, device_id_type=MESH)
    mine = pl.ds(pl.multiple_of(me.t * SEQ, SEQ), SEQ)
    load_x = pltpu.make_async_copy(x_hbm.at[mine], x_s, io_sem.at[0])
    load_c = pltpu.make_async_copy(cot_hbm.at[mine], cot_s, io_sem.at[1])
    load_x.start()
    load_c.start()

    eye = (iota((96, 96), 0) == iota((96, 96), 1)).astype(F32).astype(BF)
    q, k, v = wq_ref[...], wk_ref[...], wv_ref[...]
    own[0, :, 0:128] = q[:, 0:128].astype(BF)
    own[0, :, 128:256] = k[:, 0:128].astype(BF)
    own[0, :, 256:384] = v[:, 0:128].astype(BF)
    own[0, :, 384:512] = jnp.concatenate([q[:, 128:192], v[:, 128:192]], axis=1).astype(BF)
    wo = wo_ref[...].astype(BF)
    o2 = dot(eye, wo[128:192], NT)
    own[0, :, 512:640] = jnp.concatenate([k[:, 128:192], o2], axis=1).astype(BF)
    own[0, :, 640:768] = dot(eye, wo[0:128], NT).astype(BF)
    small[...] = jnp.zeros_like(small)
    for i, ref in enumerate((c1_ref, bo_ref, c2_ref, g1_ref, b1_ref, g2_ref, b2_ref)):
        small[i : i + 1, 0:96] = ref[...].astype(BF).astype(F32)
    small[7:10, 0:8] = bq_ref[...].astype(BF).astype(F32)
    small[10:13, 0:8] = bv_ref[...].astype(BF).astype(F32)
    sb[c, x, y, z] = small[...]
    pl.semaphore_wait(bar, len(me.peers))

    def where(i):
        if isinstance(i, int) and i == 0:
            return 0, slice(None)
        j = lax.div(i - 1, 2)
        return 1 + lax.rem(i - 1, 2), pl.ds(pl.multiple_of(CHUNK * j, 128), CHUNK)

    def unit(i, zz, xx, yy, cc, half=None):
        kind, cols = where(i)
        rr = rows(zz, xx) if half is None else rows(zz, xx, 48 * half, 48)
        return w.at[kind, 2 * yy + cc, rr, cols]

    def own_sends(i):
        kind, cols = where(i)
        src, dst = own.at[kind, :, cols], unit(i, z, x, y, c)
        out = [remote(src, dst, sx.at[i, z], rx.at[i, z], me.to_x)]
        out += [remote(src, dst, sy.at[i, z], ry.at[i, z], me.to_y)]
        out += [remote(src, dst, sz.at[i, zs[j]], rz.at[i, z], me.to_z[j]) for j in (1, 3, 2)]
        return out

    def own_local(i):
        kind, cols = where(i)
        return pltpu.make_async_copy(own.at[kind, :, cols], unit(i, z, x, y, c), ownl.at[i])

    def z_sends(i, j):
        u = unit(i, zs[j], x, y, c)
        return [
            remote(u, u, sx.at[i, zs[j]], rx.at[i, zs[j]], me.to_x),
            remote(u, u, sy.at[i, zs[j]], ry.at[i, zs[j]], me.to_y),
        ]

    def x_send(i, j):
        u = unit(i, zs[j], xn, y, c, 0)
        return remote(u, u, sfy.at[i, zs[j]], rfy.at[i, zs[j]], me.to_y)

    def y_send(i, j):
        u = unit(i, zs[j], x, yn, c, 1)
        return remote(u, u, sfx.at[i, zs[j]], rfx.at[i, zs[j]], me.to_x)

    def core_send(i, yy):
        kind, cols = where(i)
        u = w.at[kind, 2 * yy + c, :, cols]
        return remote(u, u, sp.at[i, yy], rp.at[i, yy], me.to_core)

    def start_own(i):
        for cp in own_sends(i):
            cp.start()
        own_local(i).start()

    def from_z(i):
        for j in (1, 3, 2):
            arrived(unit(i, zs[j], x, y, c), rz.at[i, zs[j]])
            for cp in z_sends(i, j):
                cp.start()

    def from_xy(i):
        for j in (0, 1, 3, 2):
            arrived(unit(i, zs[j], xn, y, c), rx.at[i, zs[j]])
            x_send(i, j).start()
            arrived(unit(i, zs[j], x, yn, c), ry.at[i, zs[j]])
            y_send(i, j).start()
        own_local(i).wait()
        core_send(i, y).start()

    def from_far(i):
        for j in (0, 1, 3, 2):
            arrived(unit(i, zs[j], xn, yn, c, 0), rfy.at[i, zs[j]])
            arrived(unit(i, zs[j], xn, yn, c, 1), rfx.at[i, zs[j]])
        core_send(i, yn).start()

    def complete(i):
        kind, cols = where(i)
        for yy in (y, yn):
            arrived(w.at[kind, 2 * yy + cn, :, cols], rp.at[i, yy])

    def gather_sent(i):
        for cp in own_sends(i):
            cp.wait_send()
        for j in (1, 2, 3):
            for cp in z_sends(i, j):
                cp.wait_send()
        for j in range(4):
            x_send(i, j).wait_send()
            y_send(i, j).wait_send()
        for yy in (y, yn):
            core_send(i, yy).wait_send()

    own_small = sb.at[c, x, y, z]
    small_z = [remote(own_small, own_small, ssm.at[j], rsm.at[z], me.to_z[j]) for j in (1, 2, 3)]
    small_x = remote(sb.at[c, x, y], sb.at[c, x, y], ssm.at[4], rsm.at[4], me.to_x)
    small_y = [
        remote(sb.at[c, b, y], sb.at[c, b, y], ssm.at[5 + b], rsm.at[5 + b], me.to_y) for b in range(2)
    ]
    small_c = remote(sb.at[c], sb.at[c], ssm.at[7], rsm.at[7], me.to_core)

    for cp in small_z:
        cp.start()
    start_own(0)
    own[1] = w1_ref[...].astype(BF)
    own[2] = dot(eye, w2_ref[...].astype(BF), NT).astype(BF)
    start_own(1)
    for j in (1, 2, 3):
        arrived(own_small, rsm.at[zs[j]])
    small_x.start()
    from_z(0)
    start_own(2)
    arrived(sb.at[c, x, y], rsm.at[4])
    for cp in small_y:
        cp.start()

    ends, total = [], jnp.int32(0)
    for i in range(4):
        total = total + lens_ref[me.t, i]
        ends.append(total)
    seg_q = sum((iota((SEQ, 1), 0) >= e).astype(jnp.int32) for e in ends)
    seg_k = sum((iota((1, SEQ), 1) >= e).astype(jnp.int32) for e in ends)
    valid = iota((SEQ, 1), 0) < ends[3]
    same = jnp.where(valid, seg_q, iota((SEQ, 1), 0) + 8) == jnp.where(
        iota((1, SEQ), 1) < ends[3], seg_k, iota((1, SEQ), 1) + 8
    )
    z1_s[:, 0:SEQ] = jnp.where(same, 0.0, NEGATIVE)
    load_c.wait()
    cot_s[...] = jnp.where(valid, cot_s[...].astype(F32), 0.0).astype(BF)
    load_x.wait()

    from_xy(0)
    for b in range(2):
        arrived(sb.at[c, b, y], rsm.at[5 + b])
    small_c.start()
    from_z(1)
    start_own(3)
    arrived(sb.at[c], rsm.at[7])

    vec_s[...] = jnp.zeros_like(vec_s)
    bqv_s[...] = jnp.zeros_like(bqv_s)

    def expand(d, _):
        vec, head = spread(d)
        zz, xx = lax.div(d, 2), lax.rem(d, 2)
        part = jnp.concatenate([sb[t % 2, xx, t // 2, zz] for t in range(4)], axis=0).astype(BF)
        vec_s[...] += dot(part, vec, NN)
        bqv_s[...] += dot(part, head, NN)
        return 0

    lax.fori_loop(0, 8, expand, 0)
    col = iota((1, D), 1)
    for t in range(4):
        row = jnp.zeros((1, D), F32)
        for s, first in enumerate(SLOTS):
            keep = (col >= first) & (col < first + 64)
            row = row + jnp.where(keep, bqv_s[16 * t + 7 + s : 16 * t + 8 + s], 0.0)
        bqv_s[16 * t : 16 * t + 1] = row
    bo, c2, g1, b1, g2, b2 = (vec_s[i : i + 1] for i in range(1, 7))

    from_far(0)
    from_xy(1)
    from_z(2)
    complete(0)

    low = iota((1, 128), 1) < 64
    acc[...] = x_s[...].astype(F32) + bo

    def tile(n):
        return slice(128 * n, 128 * n + 128)

    def half_of(values, upper):
        return jnp.where(low, 0.0, values) if upper else jnp.where(low, values, 0.0)

    def mixed_of(t):
        return jnp.concatenate(
            [half_of(a_s[t, :, tile(4)].astype(F32), 1).astype(BF), a_s[t, :, tile(5)]], axis=1
        )

    def attend(t, _):
        pre = dot(x_s[...], w[0, t], NN) + bqv_s[pl.ds(pl.multiple_of(16 * t, 16), 1)]
        a_s[t] = pre.astype(BF)
        mix = [None] * 3
        for h, (qt, kt, vt, ot, qu, vu, ou) in enumerate(HEADS):
            qh = (half_of(a_s[t, :, tile(qt)].astype(F32), qu) * 0.125).astype(BF)
            s = dot(qh, a_s[t, :, tile(kt)], NT) + z1_s[:, 0:SEQ]
            e = jnp.exp(s - jnp.max(s, axis=-1, keepdims=True))
            p = (e / jnp.sum(e, axis=-1, keepdims=True)).astype(BF)
            p_s[t, h] = p
            mix[h] = dot(p, a_s[t, :, tile(vt)], NN)
        a_s[t, :, tile(5)] = jnp.where(low, mix[0], mix[1]).astype(BF)
        a_s[t, :, tile(4)] = jnp.where(low, a_s[t, :, tile(4)].astype(F32), mix[2]).astype(BF)
        acc[...] += dot(mixed_of(t), w[0, t, :, 512:768], NT)
        from_far(t + 1)
        from_xy(t + 2)
        from_z(t + 3)

        @pl.when(t < 3)
        def _():
            start_own(t + 4)

        return 0

    def attend_last(t, _):
        return 0

    lax.fori_loop(0, 4, attend, 0)
    load = None

    def norm1(i, _):
        rr = pl.ds(pl.multiple_of(i * 128, 128), 128)
        u = acc[rr]
        u = u - jnp.mean(u, axis=-1, keepdims=True)
        rs = lax.rsqrt(jnp.mean(u * u, axis=-1, keepdims=True) + EPS)
        n = u * rs
        z1_s[rr] = n
        rs1_s[rr] = jnp.broadcast_to(rs, (128, 128))
        n = n * g1 + b1
        nl_s[rr] = n.astype(BF)
        acc[rr] = n + c2
        return 0

    lax.fori_loop(0, 4, norm1, 0)

    def up(j, _):
        @pl.when(j == 1)
        def _():
            from_far(5)
            from_xy(6)

        @pl.when(j == 2)
        def _():
            from_far(6)

        complete(1 + 2 * j)
        complete(2 + 2 * j)
        cols = pl.ds(pl.multiple_of(CHUNK * j, CHUNK), CHUNK)

        def one(t, _):
            bias = vec_s[pl.ds(pl.multiple_of(16 * t, 16), 1), cols]
            u = dot(nl_s[...], w[1, t, :, cols], NN) + bias
            phi = 0.5 + 0.5 * lax.erf(u * 0.7071067811865476)
            a = (u * phi).astype(BF)
            act_s[t, :, cols] = a
            gp_s[t, :, cols] = (phi + u * (0.3989422804014327 * jnp.exp(-0.5 * u * u))).astype(BF)
            acc[...] += dot(a, w[2, t, :, cols], NT)
            return 0

        lax.fori_loop(0, 4, one, 0)
        return 0

    lax.fori_loop(0, D // CHUNK, up, 0)

    gv_s[...] = jnp.zeros_like(gv_s)

    def put(row, value):
        for t in range(4):
            gv_s[t, row : row + 1] += value

    def norm2(i, _):
        rr = pl.ds(pl.multiple_of(i * 128, 128), 128)
        u = acc[rr]
        u = u - jnp.mean(u, axis=-1, keepdims=True)
        rs = lax.rsqrt(jnp.mean(u * u, axis=-1, keepdims=True) + EPS)
        n = u * rs
        ag_s[rr] = (n * g2 + b2).astype(BF)
        ct = cot_s[rr].astype(F32)
        cz = ct * n
        put(5, jnp.sum(cz, axis=0, keepdims=True))
        put(6, jnp.sum(ct, axis=0, keepdims=True))
        cg = ct * g2
        grad = rs * (
            cg
            - jnp.mean(cg, axis=-1, keepdims=True)
            - n * jnp.mean(cg * n, axis=-1, keepdims=True)
        )
        acc[rr] = grad
        grad = grad.astype(BF)
        dg_s[rr] = grad
        put(2, jnp.sum(grad.astype(F32), axis=0, keepdims=True))
        return 0

    lax.fori_loop(0, 4, norm2, 0)
    save_hid = pltpu.make_async_copy(ag_s, hid_hbm, io_sem.at[2])
    save_hid.start()

    def gb(kind):
        return w.at[2] if kind == 0 else g12.at[kind - 1]

    def rb(kind):
        return w.at[1] if kind == 0 else rb12.at[kind - 1]

    def ex(kind, zz):
        return rb(kind).at[2, pl.ds(pl.multiple_of(96 * zz, 16), 96)]

    def ey(kind, zz):
        return rb(kind).at[2, pl.ds(pl.multiple_of(384 + 96 * zz, 16), 96)]

    def zb(kind, zz):
        return rb(kind).at[3, pl.ds(pl.multiple_of(96 * zz, 16), 96)]

    def dx(kind, zz):
        return rb(kind).at[3, pl.ds(pl.multiple_of(384 + 48 * zz, 16), 48)]

    def dy(kind, zz):
        return rb(kind).at[3, pl.ds(pl.multiple_of(576 + 48 * zz, 16), 48)]

    def pair_send(kind, yy):
        return remote(
            gb(kind).at[2 * yy + cn], rb(kind).at[yy], gsp.at[kind, yy], grp.at[kind, yy], me.to_core
        )

    def pair_add(kind, yy):
        arrived(rb(kind).at[yy], grp.at[kind, yy])

        def add(i, _):
            rr = pl.ds(pl.multiple_of(i * 192, 192), 192)
            gb(kind)[2 * yy + c, rr] = gb(kind)[2 * yy + c, rr] + rb(kind)[yy, rr]
            return 0

        lax.fori_loop(0, 4, add, 0)

    def first_sends(kind, j):
        far = gb(kind).at[2 * yn + c]
        return [
            remote(far.at[rows(zs[j], xn, 0, 48)], dx(kind, zs[j]), gsdx.at[kind, j], grdx.at[kind, zs[j]], me.to_x),
            remote(far.at[rows(zs[j], xn, 48, 48)], dy(kind, zs[j]), gsdy.at[kind, j], grdy.at[kind, zs[j]], me.to_y),
        ]

    def second_sends(kind, j):
        near_y = gb(kind).at[2 * yn + c, rows(zs[j], x)]
        near_x = gb(kind).at[2 * y + c, rows(zs[j], xn)]
        return [
            remote(near_y, ey(kind, zs[j]), gsey.at[kind, j], grey.at[kind, zs[j]], me.to_y),
            remote(near_x, ex(kind, zs[j]), gsex.at[kind, j], grex.at[kind, zs[j]], me.to_x),
        ]

    def third_send(kind, j):
        u = gb(kind).at[2 * y + c, rows(zs[j], x)]
        return remote(u, zb(kind, z), gsz.at[kind, j], grz.at[kind, z], me.to_z[j])

    ORDER = (2, 1, 3, 0)

    def first(kind):
        for j in ORDER:
            for cp in first_sends(kind, j):
                cp.start()

    def second(kind):
        for j in ORDER:
            to_y, to_x = second_sends(kind, j)
            arrived(dx(kind, zs[j]), grdx.at[kind, zs[j]])
            u = gb(kind).at[2 * yn + c, rows(zs[j], x, 0, 48)]
            u[...] = u[...] + dx(kind, zs[j])[...]
            to_y.start()
            arrived(dy(kind, zs[j]), grdy.at[kind, zs[j]])
            u = gb(kind).at[2 * y + c, rows(zs[j], xn, 48, 48)]
            u[...] = u[...] + dy(kind, zs[j])[...]
            to_x.start()

    def third(kind):
        for j in ORDER:
            u = gb(kind).at[2 * y + c, rows(zs[j], x)]
            arrived(ex(kind, zs[j]), grex.at[kind, zs[j]])
            arrived(ey(kind, zs[j]), grey.at[kind, zs[j]])
            s = u[...].astype(F32) + ex(kind, zs[j])[...].astype(F32) + ey(kind, zs[j])[...].astype(F32)
            if j:
                u[...] = s.astype(BF)
                third_send(kind, j).start()
            else:
                o_ref[kind] = s

    def fourth(kind):
        for j in (1, 3, 2):
            arrived(zb(kind, zs[j]), grz.at[kind, zs[j]])
            o_ref[kind] = o_ref[kind] + zb(kind, zs[j])[...].astype(F32)

    def reduce_sent(kind):
        for yy in (y, yn):
            pair_send(kind, yy).wait_send()
        for j in range(4):
            for cp in first_sends(kind, j) + second_sends(kind, j):
                cp.wait_send()
            if j:
                third_send(kind, j).wait_send()

    def down_grad(j, _):
        yy = jnp.where(j == 0, yn, y)
        g12[1, 2 * yy + cn] = dot(dg_s[...], act_s[2 * yy + cn], TN).astype(BF)
        pair_send(2, yy).start()
        g12[1, 2 * yy + c] = dot(dg_s[...], act_s[2 * yy + c], TN).astype(BF)
        return 0

    lax.fori_loop(0, 2, down_grad, 0)
    for i in range(ITEMS):
        gather_sent(i)
    pair_add(2, yn)
    first(2)
    pair_add(2, y)

    def up_grad(i, _):
        yy = jnp.where(i < 2, yn, y)
        cc = jnp.where(lax.rem(i, 2) == 0, cn, c)
        t = 2 * yy + cc
        ig = (dot(dg_s[...], w[2, t], NN) * gp_s[t].astype(F32)).astype(BF)
        ig_s[...] = ig
        gv_s[t, 0:1] = jnp.sum(ig.astype(F32), axis=0, keepdims=True)
        g12[0, t] = dot(nl_s[...], ig_s[...], TN).astype(BF)

        @pl.when(lax.rem(i, 2) == 0)
        def _():
            pair_send(1, yy).start()

        acc[...] += dot(ig_s[...], w[1, t], NT)

        @pl.when(i == 1)
        def _():
            second(2)
            pair_add(1, yn)
            first(1)

        return 0

    lax.fori_loop(0, 4, up_grad, 0)
    for peer in me.peers:
        pl.semaphore_signal(ready, inc=1, device_id=peer, device_id_type=MESH)
    pair_add(1, y)

    save_hid.wait()

    def norm1_back(i, _):
        rr = pl.ds(pl.multiple_of(i * 128, 128), 128)
        n, gr = z1_s[rr], acc[rr]
        put(3, jnp.sum(gr * n, axis=0, keepdims=True))
        put(4, jnp.sum(gr, axis=0, keepdims=True))
        cg = gr * g1
        grad = rs1_s[rr, 0:1] * (
            cg
            - jnp.mean(cg, axis=-1, keepdims=True)
            - n * jnp.mean(cg * n, axis=-1, keepdims=True)
        )
        acc[rr] = grad
        grad = grad.astype(BF)
        ag_s[rr] = grad
        put(1, jnp.sum(grad.astype(F32), axis=0, keepdims=True))
        return 0

    lax.fori_loop(0, 4, norm1_back, 0)
    pl.semaphore_wait(ready, len(me.peers))

    def attend_back(i, _):
        yy = jnp.where(i < 2, yn, y)
        cc = jnp.where(lax.rem(i, 2) == 0, cn, c)
        t = 2 * yy + cc
        mg = dot(ag_s[...], w[0, t, :, 512:768], NN)
        dq, dk, dv = [None] * 3, [None] * 3, [None] * 3
        for h, (qt, kt, vt, ot, qu, vu, ou) in enumerate(HEADS):
            go = half_of(mg[:, 128:256] if ot == 5 else mg[:, 0:128], ou)
            inner = jnp.sum(go * a_s[t, :, tile(ot)].astype(F32), axis=-1, keepdims=True)
            go = go.astype(BF)
            p = p_s[t, h]
            dv[h] = dot(p, go, TN)
            ds = (p.astype(F32) * (dot(go, a_s[t, :, tile(vt)], NT) - inner)).astype(BF)
            dq[h] = dot(ds, a_s[t, :, tile(kt)], NN) * 0.125
            dk[h] = dot(ds, a_s[t, :, tile(qt)], TN) * 0.125
        da_s[:, tile(0)] = jnp.where(low, dq[0], dq[1]).astype(BF)
        da_s[:, tile(1)] = jnp.where(low, dk[0], dk[1]).astype(BF)
        da_s[:, tile(2)] = jnp.where(low, dv[0], dv[1]).astype(BF)
        da_s[:, tile(3)] = jnp.where(low, dq[2], dv[2]).astype(BF)
        da_s[:, tile(4)] = jnp.where(low, dk[2], 0.0).astype(BF)
        sums = jnp.sum(da_s[...].astype(F32), axis=0, keepdims=True)
        for s, at in enumerate(SLOTS):
            n = at // 128
            keep = half_of(sums[:, tile(n)], (at // 64) % 2)
            gv_s[t, 7 + s : 8 + s, tile(n)] = keep
        g0 = w.at[2, t]
        g0[:, 0:512] = dot(x_s[...], da_s[:, 0:512], TN).astype(BF)
        tail = dot(ag_s[...], mixed_of(t), TN)
        g0[:, 512:640] = (tail[:, 0:128] + dot(x_s[...], da_s[:, tile(4)], TN)).astype(BF)
        g0[:, 640:768] = tail[:, 128:256].astype(BF)

        @pl.when(lax.rem(i, 2) == 0)
        def _():
            pair_send(0, yy).start()

        acc[...] += dot(da_s[...], w[0, t, :, 0:640], NT)

        @pl.when(i == 1)
        def _():
            third(2)
            pair_add(0, yn)
            first(0)

        @pl.when(i == 2)
        def _():
            second(1)
            fourth(2)

        return 0

    lax.fori_loop(0, 4, attend_back, 0)
    dg_s[...] = acc[...].astype(BF)
    save_gx = pltpu.make_async_copy(dg_s, gx_hbm, io_sem.at[3])
    save_gx.start()
    pair_add(0, y)
    second(0)

    def collect(d, _):
        vec, head = spread(d)
        zz, xx = lax.div(d, 2), lax.rem(d, 2)
        val = gv_s[...].reshape(64, D)
        high = val.astype(BF)
        rest = (val - high.astype(F32)).astype(BF)
        is_vec = (iota((64, 1), 0) & 15) < 7
        got = jnp.where(is_vec, dot(high, vec, NT) + dot(rest, vec, NT), dot(high, head, NT) + dot(rest, head, NT))
        for t in range(4):
            sb[t % 2, xx, t // 2, zz] = got[16 * t : 16 * t + 16]
        return 0

    for cp in small_z + [small_x] + small_y + [small_c]:
        cp.wait_send()
    lax.fori_loop(0, 8, collect, 0)
    half_c = remote(sb.at[cn], s1, gssm.at[0], grsm.at[0], me.to_core)
    half_c.start()
    third(1)
    arrived(s1, grsm.at[0])
    sb[c] = sb[c] + s1[...]
    half_x = remote(sb.at[c, xn], s2, gssm.at[1], grsm.at[1], me.to_x)
    half_x.start()
    fourth(1)
    arrived(s2, grsm.at[1])
    sb[c, x] = sb[c, x] + s2[...]
    half_y = remote(sb.at[c, x, yn], s3, gssm.at[2], grsm.at[2], me.to_y)
    half_y.start()
    third(0)
    arrived(s3, grsm.at[2])
    sb[c, x, y] = sb[c, x, y] + s3[...]
    quarter_z = [
        remote(sb.at[c, x, y, zs[j]], s4.at[z], gssm.at[2 + j], grsm.at[3 + z], me.to_z[j]) for j in (1, 2, 3)
    ]
    for cp in quarter_z:
        cp.start()
    fourth(0)
    total = sb[c, x, y, z]
    for j in (1, 2, 3):
        arrived(s4.at[zs[j]], grsm.at[3 + zs[j]])
        total = total + s4[zs[j]]
    so_ref[...] = total
    for cp in [half_c, half_x, half_y] + quarter_z:
        cp.wait_send()
    for kind in range(3):
        reduce_sent(kind)
    save_gx.wait()


def run(r, *args):
    vm, hbm = pl.BlockSpec(memory_space=pltpu.VMEM), pl.BlockSpec(memory_space=pl.ANY)
    sm = pl.BlockSpec(memory_space=pltpu.SMEM)
    t = (SEQ, D)
    V = pltpu.VMEM
    gather = [DMA((ITEMS, 4))] * 5 + [DMA((ITEMS, 2))]
    back = [DMA((3, 2))] + [DMA((3, 4))] * 5
    return pl.pallas_call(
        functools.partial(kernel, r),
        out_shape=(
            jax.ShapeDtypeStruct(t, BF),
            jax.ShapeDtypeStruct(t, BF),
            jax.ShapeDtypeStruct((3, 96, D), F32),
            jax.ShapeDtypeStruct((16, 128), F32),
        ),
        in_specs=[sm, hbm, hbm] + [vm] * 15,
        out_specs=(hbm, hbm, vm, vm),
        scratch_shapes=[
            V((3, 96, D), BF), V((3, 4, D, D), BF), V((2, 4, D, D), BF), V((2, 4, D, D), BF),
            V((16, 128), F32), V((2, 2, 2, 4, 16, 128), F32), V((64, D), F32), V((64, D), F32),
            V((4,) + t, BF), V((4, 3, SEQ, SEQ), BF), V(t, F32), V((SEQ, 128), F32), V(t, F32),
            V((4,) + t, BF), V((4,) + t, BF), V(t, BF),
            V(t, BF), V(t, BF), V(t, BF), V(t, BF), V(t, BF), V((SEQ, 640), BF), V((4, 16, D), F32),
            V((2, 2, 4, 16, 128), F32), V((2, 4, 16, 128), F32), V((4, 16, 128), F32), V((4, 16, 128), F32),
            DMA((4,)), DMA((ITEMS,)), *gather, *gather, DMA((8,)), DMA((8,)),
            *back, *back, DMA((8,)), DMA((8,)), pltpu.SemaphoreType.REGULAR,
        ],
        compiler_params=pltpu.CompilerParams(
            collective_id=0, has_side_effects=True, vmem_limit_bytes=67043328
        ),
    )(*args)


def body(
    hidden_in, seq_lengths, out_grad, query_weight, key_weight, value_weight, output_weight, up_weight,
    down_weight, query_bias, value_bias, inner_bias, output_bias, down_bias, first_gain, first_shift,
    second_gain, second_shift,
):
    r = lax.axis_size("dp") // 8
    groups = [[g * r + i for i in range(r)] for g in range(8)]

    def whole(value, axis):
        if r == 1:
            return value
        value = value.astype(BF)
        return lax.all_gather(value, "dp", axis=axis, tiled=True, axis_index_groups=groups).astype(F32)

    def shard(value, axis):
        if r == 1:
            return value
        return lax.psum_scatter(value, "dp", scatter_dimension=axis, tiled=True, axis_index_groups=groups)

    vectors = (output_bias, down_bias, first_gain, first_shift, second_gain, second_shift)
    hidden, gx, gw, gs = run(
        r, seq_lengths, hidden_in, out_grad,
        whole(query_weight, 0), whole(key_weight, 0), whole(value_weight, 0), whole(output_weight, 1),
        whole(up_weight, 0), whole(down_weight, 1),
        whole(query_bias, 1), whole(value_bias, 1), whole(inner_bias, 1),
        *(whole(i.reshape(1, -1), 1) for i in vectors),
    )
    gw = shard(gw, 1)
    gv = shard(gs[0:7, 0:96], 1)
    gh = shard(gs[7:13, 0:8], 1)
    a = gw[0]
    return (
        hidden,
        gx,
        jnp.concatenate([a[:, 0:128], a[:, 384:448]], axis=1),
        jnp.concatenate([a[:, 128:256], a[:, 512:576]], axis=1),
        jnp.concatenate([a[:, 256:384], a[:, 448:512]], axis=1),
        jnp.concatenate([a[:, 640:768], a[:, 576:640]], axis=1).T,
        gw[1],
        gw[2].T,
        gh[0:3],
        gh[3:6],
        gv[0:1],
        gv[1],
        gv[2],
        gv[3],
        gv[4],
        gv[5],
        gv[6],
    )


def solution(mesh):
    both, dp = P(("dp", "tensor"), None), P("dp")
    rows_first, columns_first = P("dp", "tensor"), P("tensor", "dp")
    weights = (rows_first,) * 3 + (columns_first, rows_first, columns_first)
    smalls = (columns_first,) * 3 + (dp,) * 6
    return jax.shard_map(
        body,
        mesh=mesh,
        in_specs=(P("dp", None),) * 3 + weights + smalls,
        out_specs=(both, both) + weights + smalls,
        check_vma=False,
    )
```

```python
import functools

import jax
import jax.numpy as jnp
from jax import lax
from jax.experimental import pallas as pl
from jax.experimental.pallas import tpu as pltpu
from jax.sharding import PartitionSpec as P

SEQ = 512
D = 768
EPS = 1e-12
NEGATIVE = -1000000000.0
MESH = pl.DeviceIdType.MESH
BF = jnp.bfloat16
F32 = jnp.float32
DMA = pltpu.SemaphoreType.DMA
NN, NT, TN = ((1,), (0,)), ((1,), (1,)), ((0,), (0,))
HEADS = ((0, 1, 2, 5, 0, 0, 0), (0, 1, 2, 5, 1, 1, 1), (3, 4, 3, 4, 0, 1, 1))
SLOTS = (0, 64, 384, 256, 320, 448)
ITEMS = ((0, 0, 384), (0, 384, 768), (1, 0, 768), (2, 0, 512), (2, 512, 768))
ORDER = (2, 1, 3, 0)
AHEAD = {1: 2, 0: 1}
STEPS = {
    ("pack",): (("sa", 0), ("o", 0)),
    ("expand",): (("ry", 0, 0), ("rx", 0, 0), ("sa", 1), ("q", 0, 3), ("o", 1), ("q", 0, 1), ("sa", 2),
        ("q", 0, 2), ("ry", 0, 3), ("rx", 0, 3), ("ry", 1, 0), ("rx", 1, 0), ("rx", 0, 1), ("ry", 0, 1), ("sa", 3),
        ("q", 1, 3)),
    ("att", 0, 0): (("ry", 0, 2), ("q", 1, 1), ("rx", 0, 2), ("o", 2), ("q", 1, 2), ("ry", 1, 3), ("rx", 1, 3),
        ("ry", 1, 1), ("fa", 0), ("rx", 1, 1), ("ry", 1, 2), ("ry", 2, 0), ("rx", 1, 2), ("rx", 2, 0), ("q", 2, 3),
        ("q", 2, 1), ("q", 2, 2), ("ry", 2, 3), ("fa", 1), ("o", 3), ("rx", 2, 3), ("ry", 2, 1)),
    ("att", 1, 0): (("ry", 2, 2),),
    ("att", 1, 1): (("rx", 2, 1),),
    ("att", 1, 2): (("q", 3, 3), ("rx", 2, 2)),
    ("att", 1, 3): (("ry", 3, 0),),
    ("att", 2, 1): (("rx", 3, 0), ("q", 3, 1)),
    ("att", 3, 0): (("o", 4), ("q", 3, 2)),
    ("att", 3, 3): (("ry", 3, 3),),
    ("up0", 0): (("q", 4, 3), ("rx", 3, 3), ("fa", 2), ("q", 4, 1), ("ry", 3, 1), ("q", 4, 2), ("ry", 3, 2),
        ("ry", 4, 0)),
    ("up0", 1): (("rx", 3, 1), ("rx", 3, 2), ("rx", 4, 0)),
    ("up0", 2): (("ry", 4, 3), ("ry", 4, 1), ("ry", 4, 2)),
    ("up0", 3): (("rx", 4, 3), ("rx", 4, 1)),
    ("down0", 0): (("rx", 4, 2), ("fa", 3)),
    ("down0", 1): (("fa", 4),),
    ("dw2", 0, 1): (("ps", 2, 2),),
    ("dw2", 1, 1): (("ps", 2, 1),),
    ("dw2", 2, 1): (("pa", 2, 2), ("ps", 2, 3)),
    ("dw2", 3, 0): (("pa", 2, 1),),
    ("dw2", 3, 1): (("ps", 2, 0),),
    ("dw1", 0, 0): (("pa", 2, 3),),
    ("dw1", 0, 1): (("pa", 2, 0),),
    ("dw1", 1, 0): (("ps", 1, 0),),
    ("dw1", 1, 1): (("by", 2, 2), ("bx", 2, 2)),
    ("dw1", 2, 1): (("by", 2, 1), ("bx", 2, 1), ("pa", 1, 0)),
    ("dw1", 3, 0): (("ps", 1, 1),),
    ("dw1", 3, 1): (("by", 2, 3), ("bx", 2, 3)),
    ("dw0", 0, 0): (("pa", 1, 1),),
    ("dw0", 0, 1): (("by", 2, 0), ("bx", 2, 0)),
    ("dw0", 0, 2): (("cz", 2, 2),),
    ("dw0", 0, 3): (("cz", 2, 1),),
    ("dw0", 0, 4): (("ps", 0, 0),),
    ("dw0", 1, 1): (("by", 1, 2),),
    ("dw0", 1, 3): (("bx", 1, 2),),
    ("dw0", 1, 4): (("by", 1, 1), ("pa", 0, 0)),
    ("dw0", 2, 1): (("cz", 2, 3), ("bx", 1, 1)),
    ("dw0", 2, 2): (("cz", 2, 0), ("fz", 2, 2)),
    ("dw0", 2, 4): (("fz", 2, 3), ("ps", 0, 1)),
    ("dw0", 3, 0): (("by", 1, 3),),
    ("dw0", 3, 1): (("cz", 1, 2), ("bx", 1, 3)),
    ("dw0", 3, 2): (("fz", 2, 1),),
    ("dw0", 3, 4): (("by", 1, 0), ("pa", 0, 1)),
    ("small",): (("bx", 1, 0),),
    ("tail",): (("by", 0, 2), ("sb", 0), ("cz", 1, 1), ("sb", 1), ("cz", 1, 3), ("cz", 1, 0), ("fz", 1, 2),
        ("bx", 0, 2), ("sb", 2), ("by", 0, 1), ("fz", 1, 3), ("cz", 0, 2), ("sb", 3), ("bx", 0, 1), ("fz", 1, 1),
        ("by", 0, 3), ("cz", 0, 1), ("bx", 0, 3), ("sb", 4), ("by", 0, 0), ("cz", 0, 3), ("bx", 0, 0),
        ("cz", 0, 0), ("fz", 0, 3), ("fz", 0, 2), ("fz", 0, 1)),
}


def dot(a, b, dims):
    return lax.dot_general(a, b, (dims, ((), ())), preferred_element_type=F32)


def iota(shape, axis):
    return lax.broadcasted_iota(jnp.int32, shape, axis)


class Place:
    def __init__(self, r):
        dp = lax.axis_index("dp")
        t = lax.axis_index("tensor")
        g = lax.div(dp, r)
        self.r, self.q, self.t = r, lax.rem(dp, r), t
        self.z, self.x = lax.div(g, 2), lax.rem(g, 2)
        self.y, self.c = lax.div(t, 2), lax.rem(t, 2)
        self.xn, self.yn, self.cn = 1 - self.x, 1 - self.y, 1 - self.c
        self.zs = [lax.rem(self.z + i, 4) for i in range(4)]
        self.to_x = self.dev(self.z, self.xn, self.y, self.c)
        self.to_y = self.dev(self.z, self.x, self.yn, self.c)
        self.to_core = self.dev(self.z, self.x, self.y, self.cn)
        self.to_z = [self.dev(self.zs[i], self.x, self.y, self.c) for i in range(4)]
        self.peers = self.to_z[1:] + [self.to_x, self.to_y, self.to_core]

    def dev(self, z, x, y, c):
        return {"dp": (2 * z + x) * self.r + self.q, "tensor": 2 * y + c}


def remote(src, dst, ss, rs, to):
    return pltpu.make_async_remote_copy(
        src_ref=src, dst_ref=dst, send_sem=ss, recv_sem=rs, device_id=to, device_id_type=MESH
    )


def arrived(ref, sem):
    pltpu.make_async_copy(ref, ref, sem).wait()


def spread(d):
    lane, col = iota((128, D), 0), iota((128, D), 1)
    vec = (col == lane + 96 * d) & (lane < 96)
    head = ((col & 63) == lane + 8 * d) & (lane < 8)
    return vec.astype(F32).astype(BF), head.astype(F32).astype(BF)


def kernel(
    r,
    lens_ref, x_hbm, cot_hbm, wq_ref, wk_ref, wv_ref, wo_ref, w1_ref, w2_ref,
    bq_ref, bv_ref, c1_ref, bo_ref, c2_ref, g1_ref, b1_ref, g2_ref, b2_ref,
    hid_hbm, gx_hbm, o_ref, so_ref,
    own, w, g12, rb12, small, sb, vec_s, bqv_s, a_s, p_s, z1_s, rs1_s, acc, act_s, gp_s, nl_s,
    x_s, cot_s, dg_s, dgt_s, ig_s, ag_s, da_s, gv_s, s1, s2, s3, s4,
    io_sem, own_sem, s_z, s_x, s_y, s_far_x, s_far_y, s_core, r_z, r_x, r_y, r_far_x, r_far_y, r_core,
    ss_small, rs_small,
    t_p, t_y1, t_x1, t_x2, t_y2, t_z, u_p, u_y1, u_x1, u_x2, u_y2, u_z, ss_grad, rs_grad, ready,
):
    me = Place(r)
    z, x, y, c, xn, yn, cn, zs = me.z, me.x, me.y, me.c, me.xn, me.yn, me.cn, me.zs
    bar = pltpu.get_barrier_semaphore()
    for peer in me.peers:
        pl.semaphore_signal(bar, inc=1, device_id=peer, device_id_type=MESH)
    mine = pl.ds(pl.multiple_of(me.t * SEQ, SEQ), SEQ)
    load_x = pltpu.make_async_copy(x_hbm.at[mine], x_s, io_sem.at[0])
    load_c = pltpu.make_async_copy(cot_hbm.at[mine], cot_s, io_sem.at[1])
    load_x.start()
    load_c.start()

    near, far = slice(0, 48), slice(48, 96)

    def piece(i, zz, xx, yy, rr=slice(None)):
        kind, a, b = ITEMS[i]
        return w.at[kind, yy, c, 2 * zz + xx, rr, a:b]

    def x_pair(i, zz, yy):
        kind, a, b = ITEMS[i]
        return w.at[kind, yy, c, pl.ds(2 * zz, 2), near, a:b]

    def y_pair(i, zz, xx):
        kind, a, b = ITEMS[i]
        return w.at[kind, :, c, 2 * zz + xx, far, a:b]

    def own_local(i):
        kind, a, b = ITEMS[i]
        return pltpu.make_async_copy(own.at[kind, :, a:b], piece(i, z, x, y), own_sem.at[i])

    def o_sends(i):
        kind, a, b = ITEMS[i]
        src = own.at[kind, :, a:b]
        out = [
            remote(own.at[kind, near, a:b], piece(i, z, x, y, near), s_x.at[i, z], r_x.at[i, z], me.to_x),
            remote(own.at[kind, far, a:b], piece(i, z, x, y, far), s_y.at[i, z], r_y.at[i, z], me.to_y),
        ]
        for j in (1, 3, 2):
            out.append(remote(src, piece(i, z, x, y), s_z.at[i, zs[j]], r_z.at[i, z], me.to_z[j]))
        return out

    def o_wait(i):
        own_local(i).start()
        own_local(i).wait()

    def q_wait(i, j):
        arrived(piece(i, zs[j], x, y), r_z.at[i, zs[j]])

    def q_sends(i, j):
        a, b = piece(i, zs[j], x, y, near), piece(i, zs[j], x, y, far)
        return [
            remote(a, a, s_x.at[i, zs[j]], r_x.at[i, zs[j]], me.to_x),
            remote(b, b, s_y.at[i, zs[j]], r_y.at[i, zs[j]], me.to_y),
        ]

    def ry_wait(i, j):
        arrived(piece(i, zs[j], xn, y, near), r_x.at[i, zs[j]])

    def ry_sends(i, j):
        u = x_pair(i, zs[j], y)
        return [remote(u, u, s_far_y.at[i, zs[j]], r_far_y.at[i, zs[j]], me.to_y)]

    def rx_wait(i, j):
        arrived(piece(i, zs[j], x, yn, far), r_y.at[i, zs[j]])

    def rx_sends(i, j):
        u = y_pair(i, zs[j], x)
        return [remote(u, u, s_far_x.at[i, zs[j]], r_far_x.at[i, zs[j]], me.to_x)]

    def fa_wait(i):
        for j in range(4):
            arrived(x_pair(i, zs[j], yn), r_far_y.at[i, zs[j]])
            arrived(y_pair(i, zs[j], xn), r_far_x.at[i, zs[j]])

    def fa_sends(i):
        kind, a, b = ITEMS[i]
        u = w.at[kind, :, c, :, :, a:b]
        return [remote(u, u, s_core.at[i], r_core.at[i], me.to_core)]

    def complete(i):
        kind, a, b = ITEMS[i]
        arrived(w.at[kind, :, cn, :, :, a:b], r_core.at[i])

    def sa_wait(n):
        if n == 1:
            for j in (1, 2, 3):
                arrived(sb.at[c, x, y, z], rs_small.at[zs[j]])
        if n == 2:
            arrived(sb.at[c, x, y], rs_small.at[4])
        if n == 3:
            arrived(sb.at[c, :, y], rs_small.at[5])

    def sa_sends(n):
        u = (sb.at[c, x, y, z], sb.at[c, x, y], sb.at[c, :, y], sb.at[c])[n]
        if n == 0:
            return [remote(u, u, ss_small.at[j], rs_small.at[z], me.to_z[j]) for j in (1, 3, 2)]
        return [remote(u, u, ss_small.at[3 + n], rs_small.at[3 + n], (me.to_x, me.to_y, me.to_core)[n - 1])]

    def grad(kind):
        return w.at[2] if kind == 0 else g12.at[kind - 1]

    def land(kind):
        return w.at[1] if kind == 0 else rb12.at[kind - 1]

    def pairs(zz):
        return pl.ds(2 * zz, 2)

    def y1(kind, zz):
        return land(kind).at[1, 0, pairs(zz), near]

    def x1(kind, zz):
        return land(kind).at[1, 0, pairs(zz), far]

    def x2(kind, zz):
        return land(kind).at[1, 1, zz, near]

    def y2(kind, zz):
        return land(kind).at[1, 1, zz, far]

    def zb(kind, zz):
        return land(kind).at[1, 1, 4 + zz]

    def ps_sends(kind, n):
        if kind == 2:
            zz = zs[n]
            return [
                remote(grad(2).at[:, cn, pairs(zz)], land(2).at[0, :, pairs(zz)], t_p.at[2, n], u_p.at[2, zz], me.to_core)
            ]
        yy = (yn, y)[n]
        return [remote(grad(kind).at[yy, cn], land(kind).at[0, yy], t_p.at[kind, n], u_p.at[kind, yy], me.to_core)]

    def y1_send(kind, j):
        src = grad(kind).at[yn, c, pairs(zs[j]), near]
        return remote(src, y1(kind, zs[j]), t_y1.at[kind, j], u_y1.at[kind, zs[j]], me.to_y)

    def x1_send(kind, j):
        src = grad(kind).at[:, c, 2 * zs[j] + xn, far]
        return remote(src, x1(kind, zs[j]), t_x1.at[kind, j], u_x1.at[kind, zs[j]], me.to_x)

    def pa_wait(kind, n):
        g = grad(kind)
        if kind == 2:
            zz = zs[n]
            arrived(land(2).at[0, :, pairs(zz)], u_p.at[2, zz])
            g[:, c, pairs(zz)] = g[:, c, pairs(zz)] + land(2)[0, :, pairs(zz)]
            return
        yy = (yn, y)[n]
        arrived(land(kind).at[0, yy], u_p.at[kind, yy])

        def add(i, _):
            d = pl.ds(2 * i, 2)
            g[yy, c, d] = g[yy, c, d] + land(kind)[0, yy, d]
            return 0

        lax.fori_loop(0, 4, add, 0)

    def pa_sends(kind, n):
        if kind == 2:
            return [y1_send(2, n), x1_send(2, n)]
        return [(y1_send, x1_send)[n](kind, j) for j in ORDER[: AHEAD[kind]]]

    def later(kind, j, send):
        n = ORDER.index(j) + AHEAD.get(kind, 4)
        return [send(kind, ORDER[n])] if n < 4 else []

    def by_wait(kind, j):
        arrived(y1(kind, zs[j]), u_y1.at[kind, zs[j]])
        u = grad(kind).at[y, c, pairs(zs[j]), near]
        u[...] = u[...] + y1(kind, zs[j])[...]

    def by_sends(kind, j):
        src = grad(kind).at[y, c, 2 * zs[j] + xn, near]
        return [
            remote(src, x2(kind, zs[j]), t_x2.at[kind, j], u_x2.at[kind, zs[j]], me.to_x)
        ] + later(kind, j, y1_send)

    def bx_wait(kind, j):
        arrived(x1(kind, zs[j]), u_x1.at[kind, zs[j]])
        u = grad(kind).at[:, c, 2 * zs[j] + x, far]
        u[...] = u[...] + x1(kind, zs[j])[...]

    def bx_sends(kind, j):
        src = grad(kind).at[yn, c, 2 * zs[j] + x, far]
        return [
            remote(src, y2(kind, zs[j]), t_y2.at[kind, j], u_y2.at[kind, zs[j]], me.to_y)
        ] + later(kind, j, x1_send)

    def cz_wait(kind, j):
        arrived(x2(kind, zs[j]), u_x2.at[kind, zs[j]])
        arrived(y2(kind, zs[j]), u_y2.at[kind, zs[j]])
        u = grad(kind).at[y, c, 2 * zs[j] + x]
        add = land(kind).at[1, 1, zs[j]]
        if j:
            u[...] = u[...] + add[...]
        else:
            o_ref[kind] = u[...].astype(F32) + add[...].astype(F32)

    def cz_sends(kind, j):
        if not j:
            return []
        src = grad(kind).at[y, c, 2 * zs[j] + x]
        return [remote(src, zb(kind, z), t_z.at[kind, j], u_z.at[kind, z], me.to_z[j])]

    def fz_wait(kind, j):
        arrived(zb(kind, zs[j]), u_z.at[kind, zs[j]])
        o_ref[kind] = o_ref[kind] + zb(kind, zs[j])[...].astype(F32)

    def sb_wait(n):
        if n == 1:
            arrived(s1, rs_grad.at[4])
            sb[c] = sb[c] + s1[...]
        if n == 2:
            arrived(s2, rs_grad.at[5])
            sb[c, x] = sb[c, x] + s2[...]
        if n == 3:
            arrived(s3, rs_grad.at[6])
            sb[c, x, y] = sb[c, x, y] + s3[...]
        if n == 4:
            total = sb[c, x, y, z]
            for j in (1, 2, 3):
                arrived(s4.at[zs[j]], rs_grad.at[zs[j]])
                total = total + s4[zs[j]]
            so_ref[...] = total

    def sb_sends(n):
        if n == 3:
            return [
                remote(sb.at[c, x, y, zs[j]], s4.at[z], ss_grad.at[j], rs_grad.at[z], me.to_z[j]) for j in (1, 3, 2)
            ]
        if n == 4:
            return []
        src, dst = ((sb.at[cn], s1), (sb.at[c, xn], s2), (sb.at[c, x, yn], s3))[n]
        return [remote(src, dst, ss_grad.at[4 + n], rs_grad.at[4 + n], (me.to_core, me.to_x, me.to_y)[n])]

    waits = {
        "o": o_wait, "q": q_wait, "ry": ry_wait, "rx": rx_wait, "fa": fa_wait, "sa": sa_wait,
        "pa": pa_wait, "by": by_wait, "bx": bx_wait, "cz": cz_wait, "fz": fz_wait, "sb": sb_wait,
    }
    sends = {
        "o": o_sends, "q": q_sends, "ry": ry_sends, "rx": rx_sends, "fa": fa_sends, "sa": sa_sends,
        "ps": ps_sends, "pa": pa_sends, "by": by_sends, "bx": bx_sends, "cz": cz_sends, "sb": sb_sends,
    }
    gathers = {"o", "q", "ry", "rx", "fa", "sa"}

    def transfers(steps):
        for name, *args in steps:
            if name == "o":
                for cp in o_sends(*args):
                    cp.start()
            if name in waits:
                waits[name](*args)
            if name in sends and name != "o":
                for cp in sends[name](*args):
                    cp.start()

    def at(name, index=None, part=None):
        if index is None:
            transfers(STEPS.get((name,), ()))
            return
        for n in range(4):
            key = (name, n) if part is None else (name, n, part)
            if key in STEPS:
                pl.when(index == n)(functools.partial(transfers, STEPS[key]))

    def sent(of_gather):
        for steps in STEPS.values():
            for name, *args in steps:
                if name in sends and (name in gathers) == of_gather:
                    for cp in sends[name](*args):
                        cp.wait_send()

    eye = (iota((96, 96), 0) == iota((96, 96), 1)).astype(F32).astype(BF)
    q, k, v = wq_ref[...], wk_ref[...], wv_ref[...]
    own[0, :, 0:128] = q[:, 0:128].astype(BF)
    own[0, :, 128:256] = k[:, 0:128].astype(BF)
    own[0, :, 256:384] = v[:, 0:128].astype(BF)
    own[0, :, 384:512] = jnp.concatenate([q[:, 128:192], v[:, 128:192]], axis=1).astype(BF)
    wo = wo_ref[...].astype(BF)
    o2 = dot(eye, wo[128:192], NT)
    own[0, :, 512:640] = jnp.concatenate([k[:, 128:192], o2], axis=1).astype(BF)
    own[0, :, 640:768] = dot(eye, wo[0:128], NT).astype(BF)
    small[...] = jnp.zeros_like(small)
    for i, ref in enumerate((c1_ref, bo_ref, c2_ref, g1_ref, b1_ref, g2_ref, b2_ref)):
        small[i : i + 1, 0:96] = ref[...].astype(BF).astype(F32)
    small[7:10, 0:8] = bq_ref[...].astype(BF).astype(F32)
    small[10:13, 0:8] = bv_ref[...].astype(BF).astype(F32)
    sb[c, x, y, z] = small[...]
    pl.semaphore_wait(bar, len(me.peers))
    at("pack")
    own[1] = w1_ref[...].astype(BF)
    own[2] = w2_ref[...].astype(BF)
    at("mask")

    ends, total = [], jnp.int32(0)
    for i in range(4):
        total = total + lens_ref[me.t, i]
        ends.append(total)
    row, lane = iota((SEQ, 1), 0), iota((1, SEQ), 1)
    seg_q = sum((row >= e).astype(jnp.int32) for e in ends)
    seg_k = sum((lane >= e).astype(jnp.int32) for e in ends)
    valid = row < ends[3]
    same = jnp.where(valid, seg_q, row + 8) == jnp.where(lane < ends[3], seg_k, lane + 8)
    z1_s[:, 0:SEQ] = jnp.where(same, 0.0, NEGATIVE)
    load_c.wait()
    cot_s[...] = jnp.where(valid, cot_s[...].astype(F32), 0.0).astype(BF)
    load_x.wait()
    at("expand")
    arrived(sb.at[c], rs_small.at[6])

    vec_s[...] = jnp.zeros_like(vec_s)
    bqv_s[...] = jnp.zeros_like(bqv_s)

    def expand(d, _):
        vec, head = spread(d)
        zz, xx = lax.div(d, 2), lax.rem(d, 2)
        part = jnp.concatenate([sb[t % 2, xx, t // 2, zz] for t in range(4)], axis=0).astype(BF)
        vec_s[...] += dot(part, vec, NN)
        bqv_s[...] += dot(part, head, NN)
        return 0

    lax.fori_loop(0, 8, expand, 0)
    col = iota((1, D), 1)
    for t in range(4):
        bias = jnp.zeros((1, D), F32)
        for s, start in enumerate(SLOTS):
            keep = (col >= start) & (col < start + 64)
            bias = bias + jnp.where(keep, bqv_s[16 * t + 7 + s : 16 * t + 8 + s], 0.0)
        bqv_s[16 * t : 16 * t + 1] = bias
    bo, c2, g1, b1, g2, b2 = (vec_s[i : i + 1] for i in range(1, 7))

    low = iota((1, 128), 1) < 64
    acc[...] = x_s[...].astype(F32) + bo

    def tile(n):
        return slice(128 * n, 128 * n + 128)

    def half_of(values, upper):
        return jnp.where(low, 0.0, values) if upper else jnp.where(low, values, 0.0)

    def mixed_of(t):
        return jnp.concatenate(
            [half_of(a_s[t, :, tile(4)].astype(F32), 1).astype(BF), a_s[t, :, tile(5)]], axis=1
        )

    def block(kind, yy, cc, cols=slice(None)):
        value = w[kind, yy, cc, :, :, cols]
        return value.reshape(D, value.shape[-1])

    def attend(t, _):
        yy, cc = lax.div(t, 2), lax.rem(t, 2)
        at("att", t, 0)

        @pl.when(t == 0)
        def _():
            for i, item in enumerate(ITEMS):
                if item[0] == 0:
                    complete(i)

        pre = dot(x_s[...], block(0, yy, cc), NN) + bqv_s[pl.ds(pl.multiple_of(16 * t, 16), 1)]
        a_s[t] = pre.astype(BF)
        mix = [None] * 3
        for h, (qt, kt, vt, ot, qu, vu, ou) in enumerate(HEADS):
            at("att", t, h + 1)
            qh = (half_of(a_s[t, :, tile(qt)].astype(F32), qu) * 0.125).astype(BF)
            s = dot(qh, a_s[t, :, tile(kt)], NT) + z1_s[:, 0:SEQ]
            e = jnp.exp(s - jnp.max(s, axis=-1, keepdims=True))
            p = (e / jnp.sum(e, axis=-1, keepdims=True)).astype(BF)
            p_s[t, h] = p
            mix[h] = dot(p, a_s[t, :, tile(vt)], NN)
        a_s[t, :, tile(5)] = jnp.where(low, mix[0], mix[1]).astype(BF)
        a_s[t, :, tile(4)] = jnp.where(low, a_s[t, :, tile(4)].astype(F32), mix[2]).astype(BF)
        acc[...] += dot(mixed_of(t), block(0, yy, cc, slice(512, 768)), NT)
        return 0

    lax.fori_loop(0, 4, attend, 0)

    at("ln1")

    def norm1(i, _):
        rr = pl.ds(pl.multiple_of(i * 128, 128), 128)
        u = acc[rr]
        u = u - jnp.mean(u, axis=-1, keepdims=True)
        rs = lax.rsqrt(jnp.mean(u * u, axis=-1, keepdims=True) + EPS)
        n = u * rs
        z1_s[rr] = n
        rs1_s[rr] = jnp.broadcast_to(rs, (128, 128))
        n = n * g1 + b1
        nl_s[rr] = n.astype(BF)
        acc[rr] = n + c2
        return 0

    lax.fori_loop(0, 4, norm1, 0)

    def up(i, t, _):
        kind, a, b = ITEMS[i]
        at(f"up{a}", t)
        pl.when(t == 0)(functools.partial(complete, i))
        bias = vec_s[pl.ds(pl.multiple_of(16 * t, 16), 1), a:b]
        u = dot(nl_s[...], block(1, lax.div(t, 2), lax.rem(t, 2), slice(a, b)), NN) + bias
        phi = 0.5 + 0.5 * lax.erf(u * 0.7071067811865476)
        act_s[t, :, a:b] = (u * phi).astype(BF)
        gp_s[t, :, a:b] = (phi + u * (0.3989422804014327 * jnp.exp(-0.5 * u * u))).astype(BF)
        return 0

    def down(i, t, _):
        kind, a, b = ITEMS[i]
        at(f"down{a}", t)
        pl.when(t == 0)(functools.partial(complete, i))
        acc[...] += dot(act_s[t, :, a:b], block(2, lax.div(t, 2), lax.rem(t, 2), slice(a, b)), NT)
        return 0

    for i, item in enumerate(ITEMS):
        if item[0]:
            lax.fori_loop(0, 4, functools.partial((up, down)[item[0] - 1], i), 0)

    at("ln2")
    gv_s[...] = jnp.zeros_like(gv_s)

    def put(row, value):
        gv_s[0, row : row + 1] += value

    def norm2(i, _):
        rr = pl.ds(pl.multiple_of(i * 128, 128), 128)
        u = acc[rr]
        u = u - jnp.mean(u, axis=-1, keepdims=True)
        rs = lax.rsqrt(jnp.mean(u * u, axis=-1, keepdims=True) + EPS)
        n = u * rs
        ag_s[rr] = (n * g2 + b2).astype(BF)
        ct = cot_s[rr].astype(F32)
        cz = ct * n
        put(5, jnp.sum(cz, axis=0, keepdims=True))
        put(6, jnp.sum(ct, axis=0, keepdims=True))
        cg = ct * g2
        grad = rs * (
            cg
            - jnp.mean(cg, axis=-1, keepdims=True)
            - n * jnp.mean(cg * n, axis=-1, keepdims=True)
        )
        acc[rr] = grad
        grad = grad.astype(BF)
        dg_s[rr] = grad
        put(2, jnp.sum(grad.astype(F32), axis=0, keepdims=True))
        return 0

    lax.fori_loop(0, 4, norm2, 0)
    save_hid = pltpu.make_async_copy(ag_s, hid_hbm, io_sem.at[2])
    save_hid.start()

    dgt_s[...] = dg_s[...].T

    def down_grad(n, cc):
        zz = zs[ORDER[n]]
        rr = pl.ds(pl.multiple_of(192 * zz, 64), 192)
        for yy in range(2):
            value = dot(dgt_s[rr], act_s[2 * yy + cc], NN).astype(BF)
            g12[1, yy, cc, pairs(zz)] = value.reshape(2, 96, D)

    for n in range(4):
        transfers(STEPS.get(("dw2", n, 0), ()))
        down_grad(n, cn)
        transfers(STEPS.get(("dw2", n, 1), ()))
        down_grad(n, c)

    def turn(n):
        return jnp.where(n < 2, yn, y), jnp.where(lax.rem(n, 2) == 0, cn, c)

    def up_grad(n, _):
        yy, cc = turn(n)
        t = 2 * yy + cc
        at("dw1", n, 0)
        ig = (dot(dg_s[...], block(2, yy, cc), NN) * gp_s[t].astype(F32)).astype(BF)
        ig_s[...] = ig
        gv_s[t, 0:1] = jnp.sum(ig.astype(F32), axis=0, keepdims=True)
        g12[0, yy, cc] = dot(nl_s[...], ig_s[...], TN).astype(BF).reshape(8, 96, D)
        at("dw1", n, 1)
        acc[...] += dot(ig_s[...], block(1, yy, cc), NT)
        return 0

    lax.fori_loop(0, 4, up_grad, 0)
    sent(True)
    for peer in me.peers:
        pl.semaphore_signal(ready, inc=1, device_id=peer, device_id_type=MESH)

    at("ln1b")
    save_hid.wait()

    def norm1_back(i, _):
        rr = pl.ds(pl.multiple_of(i * 128, 128), 128)
        n, gr = z1_s[rr], acc[rr]
        put(3, jnp.sum(gr * n, axis=0, keepdims=True))
        put(4, jnp.sum(gr, axis=0, keepdims=True))
        cg = gr * g1
        grad = rs1_s[rr, 0:1] * (
            cg
            - jnp.mean(cg, axis=-1, keepdims=True)
            - n * jnp.mean(cg * n, axis=-1, keepdims=True)
        )
        acc[rr] = grad
        grad = grad.astype(BF)
        ag_s[rr] = grad
        put(1, jnp.sum(grad.astype(F32), axis=0, keepdims=True))
        return 0

    lax.fori_loop(0, 4, norm1_back, 0)

    def attend_back(n, _):
        yy, cc = turn(n)
        t = 2 * yy + cc
        at("dw0", n, 0)
        pl.when(n == 0)(functools.partial(pl.semaphore_wait, ready, len(me.peers)))
        mg = dot(ag_s[...], block(0, yy, cc, slice(512, 768)), NN)
        dq, dk, dv = [None] * 3, [None] * 3, [None] * 3
        for h, (qt, kt, vt, ot, qu, vu, ou) in enumerate(HEADS):
            if h:
                at("dw0", n, h)
            go = half_of(mg[:, 128:256] if ot == 5 else mg[:, 0:128], ou)
            inner = jnp.sum(go * a_s[t, :, tile(ot)].astype(F32), axis=-1, keepdims=True)
            go = go.astype(BF)
            p = p_s[t, h]
            dv[h] = dot(p, go, TN)
            ds = (p.astype(F32) * (dot(go, a_s[t, :, tile(vt)], NT) - inner)).astype(BF)
            dq[h] = dot(ds, a_s[t, :, tile(kt)], NN) * 0.125
            dk[h] = dot(ds, a_s[t, :, tile(qt)], TN) * 0.125
        da_s[:, tile(0)] = jnp.where(low, dq[0], dq[1]).astype(BF)
        da_s[:, tile(1)] = jnp.where(low, dk[0], dk[1]).astype(BF)
        da_s[:, tile(2)] = jnp.where(low, dv[0], dv[1]).astype(BF)
        da_s[:, tile(3)] = jnp.where(low, dq[2], dv[2]).astype(BF)
        da_s[:, tile(4)] = jnp.where(low, dk[2], 0.0).astype(BF)
        at("dw0", n, 3)
        sums = jnp.sum(da_s[...].astype(F32), axis=0, keepdims=True)
        for s, start in enumerate(SLOTS):
            m = start // 128
            gv_s[t, 7 + s : 8 + s, tile(m)] = half_of(sums[:, tile(m)], (start // 64) % 2)
        g0 = w.at[2, yy, cc]
        g0[:, :, 0:512] = dot(x_s[...], da_s[:, 0:512], TN).astype(BF).reshape(8, 96, 512)
        tail = dot(ag_s[...], mixed_of(t), TN)
        mixed = tail[:, 0:128] + dot(x_s[...], da_s[:, tile(4)], TN)
        g0[:, :, 512:640] = mixed.astype(BF).reshape(8, 96, 128)
        g0[:, :, 640:768] = tail[:, 128:256].astype(BF).reshape(8, 96, 128)
        at("dw0", n, 4)
        acc[...] += dot(da_s[...], block(0, yy, cc, slice(0, 640)), NT)
        return 0

    lax.fori_loop(0, 4, attend_back, 0)
    at("gx")
    dg_s[...] = acc[...].astype(BF)
    save_gx = pltpu.make_async_copy(dg_s, gx_hbm, io_sem.at[3])
    save_gx.start()
    at("small")

    for t in range(1, 4):
        gv_s[t, 1:7] = gv_s[0, 1:7]

    def collect(d, _):
        vec, head = spread(d)
        zz, xx = lax.div(d, 2), lax.rem(d, 2)
        val = gv_s[...].reshape(64, D)
        high = val.astype(BF)
        rest = (val - high.astype(F32)).astype(BF)
        is_vec = (iota((64, 1), 0) & 15) < 7
        got = jnp.where(is_vec, dot(high, vec, NT) + dot(rest, vec, NT), dot(high, head, NT) + dot(rest, head, NT))
        for t in range(4):
            sb[t % 2, xx, t // 2, zz] = got[16 * t : 16 * t + 16]
        return 0

    lax.fori_loop(0, 8, collect, 0)
    at("tail")
    sent(False)
    save_gx.wait()


def run(r, *args):
    vm, hbm = pl.BlockSpec(memory_space=pltpu.VMEM), pl.BlockSpec(memory_space=pl.ANY)
    sm = pl.BlockSpec(memory_space=pltpu.SMEM)
    t = (SEQ, D)
    V = pltpu.VMEM
    items = len(ITEMS)
    gather = [DMA((items, 4))] * 5 + [DMA((items,))]
    back = [DMA((3, 4))] * 6
    blocks = (2, 2, 8, 96, D)
    return pl.pallas_call(
        functools.partial(kernel, r),
        out_shape=(
            jax.ShapeDtypeStruct(t, BF),
            jax.ShapeDtypeStruct(t, BF),
            jax.ShapeDtypeStruct((3, 96, D), F32),
            jax.ShapeDtypeStruct((16, 128), F32),
        ),
        in_specs=[sm, hbm, hbm] + [vm] * 15,
        out_specs=(hbm, hbm, vm, vm),
        scratch_shapes=[
            V((3, 96, D), BF), V((3,) + blocks, BF), V((2,) + blocks, BF), V((2,) + blocks, BF),
            V((16, 128), F32), V((2, 2, 2, 4, 16, 128), F32), V((64, D), F32), V((64, D), F32),
            V((4,) + t, BF), V((4, 3, SEQ, SEQ), BF), V(t, F32), V((SEQ, 128), F32), V(t, F32),
            V((4,) + t, BF), V((4,) + t, BF), V(t, BF),
            V(t, BF), V(t, BF), V(t, BF), V((D, SEQ), BF), V(t, BF), V(t, BF), V((SEQ, 640), BF), V((4, 16, D), F32),
            V((2, 2, 4, 16, 128), F32), V((2, 4, 16, 128), F32), V((4, 16, 128), F32), V((4, 16, 128), F32),
            DMA((4,)), DMA((items,)), *gather, *gather, DMA((8,)), DMA((8,)),
            *back, *back, DMA((8,)), DMA((8,)), pltpu.SemaphoreType.REGULAR,
        ],
        compiler_params=pltpu.CompilerParams(
            collective_id=0, has_side_effects=True, vmem_limit_bytes=67043328
        ),
    )(*args)


def finish_kernel(g_ref, s_ref, *outs):
    wq, wk, wv, wo, w1, w2, bq, bv, c1, bo, c2, g1, b1, g2, b2 = outs
    a = g_ref[0]
    for n, ref in enumerate((wq, wk, wv)):
        ref[:, 0:128] = a[:, 128 * n : 128 * n + 128]
    wq[:, 128:192] = a[:, 384:448]
    wk[:, 128:192] = a[:, 512:576]
    wv[:, 128:192] = a[:, 448:512]
    eye = (iota((96, 96), 0) == iota((96, 96), 1)).astype(F32)
    turned = lax.dot_general(
        a[:, 512:768], eye, (TN, ((), ())), preferred_element_type=F32, precision=lax.Precision.HIGHEST
    )
    wo[0:128] = turned[128:256]
    wo[128:192] = turned[64:128]
    w1[...] = g_ref[1]
    w2[...] = g_ref[2]
    bq[...] = s_ref[7:10, 0:8]
    bv[...] = s_ref[10:13, 0:8]
    for n, ref in enumerate((c1, bo, c2, g1, b1, g2, b2)):
        ref[...] = s_ref[n : n + 1, 0:96]


def finish(grads, small):
    shapes = [(96, 192)] * 3 + [(192, 96), (96, D), (96, D), (3, 8), (3, 8)] + [(1, 96)] * 7
    out = pl.pallas_call(
        finish_kernel,
        out_shape=[jax.ShapeDtypeStruct(s, F32) for s in shapes],
        in_specs=[pl.BlockSpec(memory_space=pltpu.VMEM)] * 2,
        out_specs=[pl.BlockSpec(memory_space=pltpu.VMEM)] * 15,
    )(grads, small)
    out = list(out)
    return out[:5] + [out[5].T] + out[6:9] + [i.reshape(96) for i in out[9:]]


def body(
    hidden_in, seq_lengths, out_grad, query_weight, key_weight, value_weight, output_weight, up_weight,
    down_weight, query_bias, value_bias, inner_bias, output_bias, down_bias, first_gain, first_shift,
    second_gain, second_shift,
):
    r = lax.axis_size("dp") // 8
    groups = [[g * r + i for i in range(r)] for g in range(8)]

    def whole(value, axis):
        if r == 1:
            return value
        value = value.astype(BF)
        return lax.all_gather(value, "dp", axis=axis, tiled=True, axis_index_groups=groups).astype(F32)

    def shard(value, axis):
        if r == 1:
            return value
        return lax.psum_scatter(value, "dp", scatter_dimension=axis, tiled=True, axis_index_groups=groups)

    vectors = (output_bias, down_bias, first_gain, first_shift, second_gain, second_shift)
    hidden, gx, gw, gs = run(
        r, seq_lengths, hidden_in, out_grad,
        whole(query_weight, 0), whole(key_weight, 0), whole(value_weight, 0), whole(output_weight, 1),
        whole(up_weight, 0), whole(down_weight.T, 0),
        whole(query_bias, 1), whole(value_bias, 1), whole(inner_bias, 1),
        *(whole(i.reshape(1, -1), 1) for i in vectors),
    )
    if r == 1:
        return (hidden, gx, *finish(gw, gs))
    gw = shard(gw, 1)
    gv = shard(gs[0:7, 0:96], 1)
    gh = shard(gs[7:13, 0:8], 1)
    a = gw[0]
    return (
        hidden,
        gx,
        jnp.concatenate([a[:, 0:128], a[:, 384:448]], axis=1),
        jnp.concatenate([a[:, 128:256], a[:, 512:576]], axis=1),
        jnp.concatenate([a[:, 256:384], a[:, 448:512]], axis=1),
        jnp.concatenate([a[:, 640:768], a[:, 576:640]], axis=1).T,
        gw[1],
        gw[2].T,
        gh[0:3],
        gh[3:6],
        gv[0:1],
        *(gv[i] for i in range(1, 7)),
    )


def solution(mesh):
    both, dp = P(("dp", "tensor"), None), P("dp")
    rows_first, columns_first = P("dp", "tensor"), P("tensor", "dp")
    weights = (rows_first,) * 3 + (columns_first, rows_first, columns_first)
    smalls = (columns_first,) * 3 + (dp,) * 6
    return jax.shard_map(
        body,
        mesh=mesh,
        in_specs=(P("dp", None),) * 3 + weights + smalls,
        out_specs=(both, both) + weights + smalls,
        check_vma=False,
    )
```

```python
import functools

import jax
import jax.numpy as jnp
from jax import lax
from jax.experimental import pallas as pl
from jax.experimental.pallas import tpu as pltpu
from jax.sharding import PartitionSpec as P

SEQ = 512
D = 768
EPS = 1e-12
NEGATIVE = -1000000000.0
MESH = pl.DeviceIdType.MESH
BF = jnp.bfloat16
F32 = jnp.float32
DMA = pltpu.SemaphoreType.DMA
NN, NT, TN = ((1,), (0,)), ((1,), (1,)), ((0,), (0,))
HEADS = ((0, 1, 2, 5, 0, 0, 0), (0, 1, 2, 5, 1, 1, 1), (3, 4, 3, 4, 0, 1, 1))
SLOTS = (0, 64, 384, 256, 320, 448)
ITEMS = ((0, 0, 768), (1, 0, 768), (2, 0, 512), (2, 512, 768))
ORDER = (2, 1, 3, 0)
AHEAD = {1: 3, 0: 1}
STEPS = {
    ("pack",): (("o", 0), ("sa", 0)),
    ("mask",): (("oz", 0), ("o", 1), ("o", 2)),
    ("expand",): (("o", 3), ("ry", 0, 0), ("rx", 1, 0), ("ry", 1, 0), ("rx", 2, 0), ("sa", 1), ("rx", 0, 0),
        ("ry", 2, 0), ("q", 0, 3), ("q", 0, 1), ("q", 0, 2), ("sa", 2), ("oz", 1), ("rx", 0, 1), ("rx", 3, 0),
        ("rx", 0, 3), ("ry", 0, 3), ("sa", 3), ("ry", 0, 2), ("ry", 3, 0), ("ry", 0, 1), ("q", 1, 3), ("rx", 0, 2),
        ("oz", 2)),
    ("att", 0, 0): (("q", 1, 1), ("q", 1, 2), ("ry", 1, 3), ("oz", 3), ("rx", 1, 3), ("fa", 0), ("ry", 1, 1),
        ("q", 2, 3), ("rx", 1, 2), ("rx", 1, 1), ("ry", 1, 2)),
    ("att", 1, 0): (("q", 2, 1),),
    ("att", 1, 2): (("q", 2, 2),),
    ("att", 2, 0): (("rx", 2, 3),),
    ("att", 2, 2): (("ry", 2, 3),),
    ("att", 2, 3): (("q", 3, 2), ("q", 3, 3), ("fa", 1), ("q", 3, 1)),
    ("att", 3, 0): (("ry", 2, 1),),
    ("att", 3, 1): (("rx", 2, 2),),
    ("att", 3, 2): (("rx", 2, 1), ("ry", 2, 2)),
    ("up0", 0): (("ry", 3, 2), ("ry", 3, 1), ("rx", 3, 1)),
    ("up0", 1): (("ry", 3, 3), ("rx", 3, 2), ("rx", 3, 3)),
    ("up0", 2): (("fa", 2),),
    ("down0", 0): (("fa", 3),),
    ("dw2", 0, 1): (("ps", 2, 2),),
    ("dw2", 2, 0): (("pa", 2, 2), ("ps", 2, 1)),
    ("dw2", 2, 1): (("ps", 2, 3),),
    ("dw1", 0, 0): (("pa", 2, 3),),
    ("dw1", 0, 1): (("ps", 1, 0), ("pa", 2, 1)),
    ("dw1", 1, 1): (("by", 2, 2), ("bx", 2, 2), ("ps", 2, 0)),
    ("dw1", 2, 1): (("pa", 2, 0),),
    ("dw1", 3, 0): (("ps", 1, 1),),
    ("dw1", 3, 1): (("by", 2, 1), ("bx", 2, 1), ("pa", 1, 0)),
    ("ln1b",): (("by", 2, 3), ("pa", 1, 1)),
    ("dw0", 1, 2): (("bx", 2, 3), ("ps", 0, 0), ("cz", 2, 2), ("by", 1, 2)),
    ("dw0", 1, 4): (("bx", 1, 2), ("cz", 2, 1)),
    ("dw0", 2, 1): (("by", 2, 0),),
    ("dw0", 2, 4): (("ps", 0, 1), ("pa", 0, 0)),
    ("dw0", 3, 0): (("by", 1, 1), ("cz", 2, 3), ("bx", 1, 1), ("by", 1, 3)),
    ("dw0", 3, 1): (("by", 1, 0),),
    ("dw0", 3, 2): (("bx", 2, 0),),
    ("dw0", 3, 3): (("cz", 1, 2),),
    ("dw0", 3, 4): (("bx", 1, 3), ("pa", 0, 1)),
    ("gx",): (("by", 0, 2),),
    ("tail",): (("sb", 0), ("sb", 1), ("cz", 1, 1), ("bx", 1, 0), ("cz", 2, 0), ("bx", 0, 2), ("cz", 1, 3),
        ("by", 0, 1), ("cz", 0, 2), ("bx", 0, 1), ("sb", 2), ("by", 0, 3), ("cz", 0, 1), ("bx", 0, 3), ("sb", 3),
        ("cz", 1, 0), ("fz", 1), ("by", 0, 0), ("cz", 0, 3), ("fz", 2), ("bx", 0, 0), ("sb", 4), ("cz", 0, 0),
        ("fz", 0)),
}


def dot(a, b, dims):
    return lax.dot_general(a, b, (dims, ((), ())), preferred_element_type=F32)


def iota(shape, axis):
    return lax.broadcasted_iota(jnp.int32, shape, axis)


class Place:
    def __init__(self, r):
        dp = lax.axis_index("dp")
        t = lax.axis_index("tensor")
        g = lax.div(dp, r)
        self.r, self.q, self.t = r, lax.rem(dp, r), t
        self.z, self.x = lax.div(g, 2), lax.rem(g, 2)
        self.y, self.c = lax.div(t, 2), lax.rem(t, 2)
        self.xn, self.yn, self.cn = 1 - self.x, 1 - self.y, 1 - self.c
        self.zs = [lax.rem(self.z + i, 4) for i in range(4)]
        self.to_x = self.dev(self.z, self.xn, self.y, self.c)
        self.to_y = self.dev(self.z, self.x, self.yn, self.c)
        self.to_core = self.dev(self.z, self.x, self.y, self.cn)
        self.to_z = [self.dev(self.zs[i], self.x, self.y, self.c) for i in range(4)]
        self.peers = self.to_z[1:] + [self.to_x, self.to_y, self.to_core]

    def dev(self, z, x, y, c):
        return {"dp": (2 * z + x) * self.r + self.q, "tensor": 2 * y + c}


def remote(src, dst, ss, rs, to):
    return pltpu.make_async_remote_copy(
        src_ref=src, dst_ref=dst, send_sem=ss, recv_sem=rs, device_id=to, device_id_type=MESH
    )


def arrived(ref, sem):
    pltpu.make_async_copy(ref, ref, sem).wait()


def spread(d):
    lane, col = iota((128, D), 0), iota((128, D), 1)
    vec = (col == lane + 96 * d) & (lane < 96)
    head = ((col & 63) == lane + 8 * d) & (lane < 8)
    return vec.astype(F32).astype(BF), head.astype(F32).astype(BF)


def kernel(
    r,
    lens_ref, x_hbm, cot_hbm, wq_ref, wk_ref, wv_ref, wo_ref, w1_ref, w2_ref,
    bq_ref, bv_ref, c1_ref, bo_ref, c2_ref, g1_ref, b1_ref, g2_ref, b2_ref,
    hid_hbm, gx_hbm, o_ref, so_ref,
    own, w, g12, rb12, small, sb, vec_s, bqv_s, a_s, p_s, z1_s, rs1_s, acc, act_s, gp_s, nl_s,
    x_s, cot_s, dg_s, dgt_s, ig_s, ag_s, da_s, gv_s, s1, s2, s3, s4,
    io_sem, own_sem, s_first, s_far, s_core, r_z, r_x, r_y, r_far, r_core, ss_small, rs_small,
    t_p, t_1, t_2, u_p, u_y1, u_x1, u_2, u_z, ss_grad, rs_grad, ready,
):
    me = Place(r)
    z, x, y, c, xn, yn, cn, zs = me.z, me.x, me.y, me.c, me.xn, me.yn, me.cn, me.zs
    bar = pltpu.get_barrier_semaphore()
    for peer in me.peers:
        pl.semaphore_signal(bar, inc=1, device_id=peer, device_id_type=MESH)
    mine = pl.ds(pl.multiple_of(me.t * SEQ, SEQ), SEQ)
    load_x = pltpu.make_async_copy(x_hbm.at[mine], x_s, io_sem.at[0])
    load_c = pltpu.make_async_copy(cot_hbm.at[mine], cot_s, io_sem.at[1])
    load_x.start()
    load_c.start()

    near, far = slice(0, 48), slice(48, 96)

    def piece(i, zz, xx, yy, rr=slice(None)):
        kind, a, b = ITEMS[i]
        return w.at[kind, yy, c, 2 * zz + xx, rr, a:b]

    def x_pair(i, zz, yy):
        kind, a, b = ITEMS[i]
        return w.at[kind, yy, c, pl.ds(2 * zz, 2), near, a:b]

    def y_pair(i, zz, xx):
        kind, a, b = ITEMS[i]
        return w.at[kind, :, c, 2 * zz + xx, far, a:b]

    def o_sends(i):
        kind, a, b = ITEMS[i]
        return [
            remote(own.at[kind, near, a:b], piece(i, z, x, y, near), s_first.at[i], r_x.at[i, z], me.to_x),
            remote(own.at[kind, far, a:b], piece(i, z, x, y, far), s_first.at[i], r_y.at[i, z], me.to_y),
        ]

    def o_wait(i):
        kind, a, b = ITEMS[i]
        cp = pltpu.make_async_copy(own.at[kind, :, a:b], piece(i, z, x, y), own_sem.at[0])
        cp.start()
        cp.wait()

    def oz_sends(i):
        kind, a, b = ITEMS[i]
        src, dst = own.at[kind, :, a:b], piece(i, z, x, y)
        return [remote(src, dst, s_first.at[i], r_z.at[i, z], me.to_z[j]) for j in (1, 3, 2)]

    def q_wait(i, j):
        arrived(piece(i, zs[j], x, y), r_z.at[i, zs[j]])

    def q_sends(i, j):
        a, b = piece(i, zs[j], x, y, near), piece(i, zs[j], x, y, far)
        return [
            remote(a, a, s_first.at[i], r_x.at[i, zs[j]], me.to_x),
            remote(b, b, s_first.at[i], r_y.at[i, zs[j]], me.to_y),
        ]

    def ry_wait(i, j):
        arrived(piece(i, zs[j], xn, y, near), r_x.at[i, zs[j]])

    def ry_sends(i, j):
        u = x_pair(i, zs[j], y)
        return [remote(u, u, s_far.at[i], r_far.at[i], me.to_y)]

    def rx_wait(i, j):
        arrived(piece(i, zs[j], x, yn, far), r_y.at[i, zs[j]])

    def rx_sends(i, j):
        u = y_pair(i, zs[j], x)
        return [remote(u, u, s_far.at[i], r_far.at[i], me.to_x)]

    def fa_wait(i):
        kind, a, b = ITEMS[i]
        arrived(w.at[kind, yn, c, :, :, a:b], r_far.at[i])

    def fa_sends(i):
        kind, a, b = ITEMS[i]
        u = w.at[kind, :, c, :, :, a:b]
        return [remote(u, u, s_core.at[i], r_core.at[i], me.to_core)]

    def complete(i):
        kind, a, b = ITEMS[i]
        arrived(w.at[kind, :, cn, :, :, a:b], r_core.at[i])

    def sa_wait(n):
        if n == 1:
            for j in (1, 2, 3):
                arrived(sb.at[c, x, y, z], rs_small.at[zs[j]])
        if n == 2:
            arrived(sb.at[c, x, y], rs_small.at[4])
        if n == 3:
            arrived(sb.at[c, :, y], rs_small.at[5])

    def sa_sends(n):
        u = (sb.at[c, x, y, z], sb.at[c, x, y], sb.at[c, :, y], sb.at[c])[n]
        if n == 0:
            return [remote(u, u, ss_small.at[j], rs_small.at[z], me.to_z[j]) for j in (1, 3, 2)]
        return [remote(u, u, ss_small.at[3 + n], rs_small.at[3 + n], (me.to_x, me.to_y, me.to_core)[n - 1])]

    def grad(kind):
        return w.at[2] if kind == 0 else g12.at[kind - 1]

    def land(kind):
        return w.at[1] if kind == 0 else rb12.at[kind - 1]

    def pairs(zz):
        return pl.ds(2 * zz, 2)

    def y1(kind, zz):
        return land(kind).at[1, 0, pairs(zz), near]

    def x1(kind, zz):
        return land(kind).at[1, 0, pairs(zz), far]

    def x2(kind, zz):
        return land(kind).at[1, 1, zz, near]

    def y2(kind, zz):
        return land(kind).at[1, 1, zz, far]

    def zb(kind, j):
        return land(kind).at[1, 1, 3 + j]

    def ps_sends(kind, n):
        if kind == 2:
            zz = zs[n]
            return [
                remote(grad(2).at[:, cn, pairs(zz)], land(2).at[0, :, pairs(zz)], t_p.at[2], u_p.at[2, zz], me.to_core)
            ]
        yy = (yn, y)[n]
        return [remote(grad(kind).at[yy, cn], land(kind).at[0, yy], t_p.at[kind], u_p.at[kind, yy], me.to_core)]

    def y1_send(kind, j):
        src = grad(kind).at[yn, c, pairs(zs[j]), near]
        return remote(src, y1(kind, zs[j]), t_1.at[kind], u_y1.at[kind, zs[j]], me.to_y)

    def x1_send(kind, j):
        src = grad(kind).at[:, c, 2 * zs[j] + xn, far]
        return remote(src, x1(kind, zs[j]), t_1.at[kind], u_x1.at[kind, zs[j]], me.to_x)

    def pa_wait(kind, n):
        g = grad(kind)
        if kind == 2:
            zz = zs[n]
            arrived(land(2).at[0, :, pairs(zz)], u_p.at[2, zz])
            g[:, c, pairs(zz)] = g[:, c, pairs(zz)] + land(2)[0, :, pairs(zz)]
            return
        yy = (yn, y)[n]
        arrived(land(kind).at[0, yy], u_p.at[kind, yy])

        def add(i, _):
            d = pl.ds(2 * i, 2)
            g[yy, c, d] = g[yy, c, d] + land(kind)[0, yy, d]
            return 0

        lax.fori_loop(0, 4, add, 0)

    def pa_sends(kind, n):
        if kind == 2:
            return [y1_send(2, n), x1_send(2, n)]
        return [(y1_send, x1_send)[n](kind, j) for j in ORDER[: AHEAD[kind]]]

    def later(kind, j, send):
        n = ORDER.index(j) + AHEAD.get(kind, 4)
        return [send(kind, ORDER[n])] if n < 4 else []

    def by_wait(kind, j):
        arrived(y1(kind, zs[j]), u_y1.at[kind, zs[j]])
        u = grad(kind).at[y, c, pairs(zs[j]), near]
        u[...] = u[...] + y1(kind, zs[j])[...]

    def by_sends(kind, j):
        src = grad(kind).at[y, c, 2 * zs[j] + xn, near]
        return [
            remote(src, x2(kind, zs[j]), t_2.at[kind], u_2.at[kind, zs[j]], me.to_x)
        ] + later(kind, j, y1_send)

    def bx_wait(kind, j):
        arrived(x1(kind, zs[j]), u_x1.at[kind, zs[j]])
        u = grad(kind).at[:, c, 2 * zs[j] + x, far]
        u[...] = u[...] + x1(kind, zs[j])[...]

    def bx_sends(kind, j):
        src = grad(kind).at[yn, c, 2 * zs[j] + x, far]
        return [
            remote(src, y2(kind, zs[j]), t_2.at[kind], u_2.at[kind, zs[j]], me.to_y)
        ] + later(kind, j, x1_send)

    def cz_wait(kind, j):
        arrived(land(kind).at[1, 1, zs[j]], u_2.at[kind, zs[j]])
        u = grad(kind).at[y, c, 2 * zs[j] + x]
        add = land(kind).at[1, 1, zs[j]]
        if j:
            u[...] = u[...] + add[...]
        else:
            o_ref[kind] = u[...].astype(F32) + add[...].astype(F32)

    def cz_sends(kind, j):
        if not j:
            return []
        src = grad(kind).at[y, c, 2 * zs[j] + x]
        return [remote(src, zb(kind, 4 - j), t_2.at[kind], u_z.at[kind], me.to_z[j])]

    def fz_wait(kind):
        arrived(land(kind).at[1, 1, 4:7], u_z.at[kind])
        o_ref[kind] = o_ref[kind] + sum(zb(kind, j)[...].astype(F32) for j in (1, 2, 3))

    def sb_wait(n):
        if n == 1:
            arrived(s1, rs_grad.at[4])
            sb[c] = sb[c] + s1[...]
        if n == 2:
            arrived(s2, rs_grad.at[5])
            sb[c, x] = sb[c, x] + s2[...]
        if n == 3:
            arrived(s3, rs_grad.at[6])
            sb[c, x, y] = sb[c, x, y] + s3[...]
        if n == 4:
            total = sb[c, x, y, z]
            for j in (1, 2, 3):
                arrived(s4.at[zs[j]], rs_grad.at[zs[j]])
                total = total + s4[zs[j]]
            so_ref[...] = total

    def sb_sends(n):
        if n == 3:
            return [
                remote(sb.at[c, x, y, zs[j]], s4.at[z], ss_grad.at[j], rs_grad.at[z], me.to_z[j]) for j in (1, 3, 2)
            ]
        if n == 4:
            return []
        src, dst = ((sb.at[cn], s1), (sb.at[c, xn], s2), (sb.at[c, x, yn], s3))[n]
        return [remote(src, dst, ss_grad.at[4 + n], rs_grad.at[4 + n], (me.to_core, me.to_x, me.to_y)[n])]

    waits = {
        "o": o_wait, "q": q_wait, "ry": ry_wait, "rx": rx_wait, "fa": fa_wait, "sa": sa_wait,
        "pa": pa_wait, "by": by_wait, "bx": bx_wait, "cz": cz_wait, "fz": fz_wait, "sb": sb_wait,
    }
    sends = {
        "o": o_sends, "oz": oz_sends, "q": q_sends, "ry": ry_sends, "rx": rx_sends, "fa": fa_sends, "sa": sa_sends,
        "ps": ps_sends, "pa": pa_sends, "by": by_sends, "bx": bx_sends, "cz": cz_sends, "sb": sb_sends,
    }

    def transfers(steps):
        for name, *args in steps:
            if name == "o":
                for cp in o_sends(*args):
                    cp.start()
            if name in waits:
                waits[name](*args)
            if name in sends and name != "o":
                for cp in sends[name](*args):
                    cp.start()

    def at(name, index=None, part=None):
        if index is None:
            transfers(STEPS.get((name,), ()))
            return
        for n in range(4):
            key = (name, n) if part is None else (name, n, part)
            if key in STEPS:
                pl.when(index == n)(functools.partial(transfers, STEPS[key]))

    def gather_sent():
        for i, (kind, a, b) in enumerate(ITEMS):
            arrived(w.at[kind, y, c, 0:7, :, a:b], s_first.at[i])
            arrived(w.at[kind, y, c, :, :, a:b], s_far.at[i])
            arrived(w.at[kind, :, c, :, :, a:b], s_core.at[i])
        for n in range(4):
            for cp in sa_sends(n):
                cp.wait_send()

    def grads_sent():
        for kind in range(3):
            arrived(grad(kind).at[:, cn], t_p.at[kind])
            arrived(grad(kind).at[y, c], t_1.at[kind])
            arrived(grad(kind).at[y, c, 0:7], t_2.at[kind])
        for n in range(4):
            for cp in sb_sends(n):
                cp.wait_send()

    eye = (iota((96, 96), 0) == iota((96, 96), 1)).astype(F32).astype(BF)
    q, k, v = wq_ref[...], wk_ref[...], wv_ref[...]
    own[0, :, 0:128] = q[:, 0:128].astype(BF)
    own[0, :, 128:256] = k[:, 0:128].astype(BF)
    own[0, :, 256:384] = v[:, 0:128].astype(BF)
    own[0, :, 384:512] = jnp.concatenate([q[:, 128:192], v[:, 128:192]], axis=1).astype(BF)
    wo = wo_ref[...].astype(BF)
    o2 = dot(eye, wo[128:192], NT)
    own[0, :, 512:640] = jnp.concatenate([k[:, 128:192], o2], axis=1).astype(BF)
    own[0, :, 640:768] = dot(eye, wo[0:128], NT).astype(BF)
    small[...] = jnp.zeros_like(small)
    for i, ref in enumerate((c1_ref, bo_ref, c2_ref, g1_ref, b1_ref, g2_ref, b2_ref)):
        small[i : i + 1, 0:96] = ref[...].astype(BF).astype(F32)
    small[7:10, 0:8] = bq_ref[...].astype(BF).astype(F32)
    small[10:13, 0:8] = bv_ref[...].astype(BF).astype(F32)
    sb[c, x, y, z] = small[...]
    pl.semaphore_wait(bar, len(me.peers))
    at("pack")
    own[1] = w1_ref[...].astype(BF)
    own[2] = w2_ref[...].astype(BF)
    at("mask")

    ends, total = [], jnp.int32(0)
    for i in range(4):
        total = total + lens_ref[me.t, i]
        ends.append(total)
    row, lane = iota((SEQ, 1), 0), iota((1, SEQ), 1)
    seg_q = sum((row >= e).astype(jnp.int32) for e in ends)
    seg_k = sum((lane >= e).astype(jnp.int32) for e in ends)
    valid = row < ends[3]
    same = jnp.where(valid, seg_q, row + 8) == jnp.where(lane < ends[3], seg_k, lane + 8)
    z1_s[:, 0:SEQ] = jnp.where(same, 0.0, NEGATIVE)
    load_c.wait()
    cot_s[...] = jnp.where(valid, cot_s[...].astype(F32), 0.0).astype(BF)
    load_x.wait()
    at("expand")
    arrived(sb.at[c], rs_small.at[6])

    vec_s[...] = jnp.zeros_like(vec_s)
    bqv_s[...] = jnp.zeros_like(bqv_s)

    def expand(d, _):
        vec, head = spread(d)
        zz, xx = lax.div(d, 2), lax.rem(d, 2)
        part = jnp.concatenate([sb[t % 2, xx, t // 2, zz] for t in range(4)], axis=0).astype(BF)
        vec_s[...] += dot(part, vec, NN)
        bqv_s[...] += dot(part, head, NN)
        return 0

    lax.fori_loop(0, 8, expand, 0)
    col = iota((1, D), 1)
    for t in range(4):
        bias = jnp.zeros((1, D), F32)
        for s, start in enumerate(SLOTS):
            keep = (col >= start) & (col < start + 64)
            bias = bias + jnp.where(keep, bqv_s[16 * t + 7 + s : 16 * t + 8 + s], 0.0)
        bqv_s[16 * t : 16 * t + 1] = bias
    bo, c2, g1, b1, g2, b2 = (vec_s[i : i + 1] for i in range(1, 7))

    low = iota((1, 128), 1) < 64
    acc[...] = x_s[...].astype(F32) + bo

    def tile(n):
        return slice(128 * n, 128 * n + 128)

    def half_of(values, upper):
        return jnp.where(low, 0.0, values) if upper else jnp.where(low, values, 0.0)

    def mixed_of(t):
        return jnp.concatenate(
            [half_of(a_s[t, :, tile(4)].astype(F32), 1).astype(BF), a_s[t, :, tile(5)]], axis=1
        )

    def block(kind, yy, cc, cols=slice(None)):
        value = w[kind, yy, cc, :, :, cols]
        return value.reshape(D, value.shape[-1])

    def attend(t, _):
        yy, cc = lax.div(t, 2), lax.rem(t, 2)
        at("att", t, 0)

        @pl.when(t == 0)
        def _():
            for i, item in enumerate(ITEMS):
                if item[0] == 0:
                    complete(i)

        pre = dot(x_s[...], block(0, yy, cc), NN) + bqv_s[pl.ds(pl.multiple_of(16 * t, 16), 1)]
        a_s[t] = pre.astype(BF)
        mix = [None] * 3
        for h, (qt, kt, vt, ot, qu, vu, ou) in enumerate(HEADS):
            at("att", t, h + 1)
            qh = (half_of(a_s[t, :, tile(qt)].astype(F32), qu) * 0.125).astype(BF)
            s = dot(qh, a_s[t, :, tile(kt)], NT) + z1_s[:, 0:SEQ]
            e = jnp.exp(s - jnp.max(s, axis=-1, keepdims=True))
            p = (e / jnp.sum(e, axis=-1, keepdims=True)).astype(BF)
            p_s[t, h] = p
            mix[h] = dot(p, a_s[t, :, tile(vt)], NN)
        a_s[t, :, tile(5)] = jnp.where(low, mix[0], mix[1]).astype(BF)
        a_s[t, :, tile(4)] = jnp.where(low, a_s[t, :, tile(4)].astype(F32), mix[2]).astype(BF)
        acc[...] += dot(mixed_of(t), block(0, yy, cc, slice(512, 768)), NT)
        return 0

    lax.fori_loop(0, 4, attend, 0)

    at("ln1")

    def norm1(i, _):
        rr = pl.ds(pl.multiple_of(i * 128, 128), 128)
        u = acc[rr]
        u = u - jnp.mean(u, axis=-1, keepdims=True)
        rs = lax.rsqrt(jnp.mean(u * u, axis=-1, keepdims=True) + EPS)
        n = u * rs
        z1_s[rr] = n
        rs1_s[rr] = jnp.broadcast_to(rs, (128, 128))
        n = n * g1 + b1
        nl_s[rr] = n.astype(BF)
        acc[rr] = n + c2
        return 0

    lax.fori_loop(0, 4, norm1, 0)

    def up(i, t, _):
        kind, a, b = ITEMS[i]
        at(f"up{a}", t)
        pl.when(t == 0)(functools.partial(complete, i))
        bias = vec_s[pl.ds(pl.multiple_of(16 * t, 16), 1), a:b]
        u = dot(nl_s[...], block(1, lax.div(t, 2), lax.rem(t, 2), slice(a, b)), NN) + bias
        phi = 0.5 + 0.5 * lax.erf(u * 0.7071067811865476)
        act_s[t, :, a:b] = (u * phi).astype(BF)
        gp_s[t, :, a:b] = (phi + u * (0.3989422804014327 * jnp.exp(-0.5 * u * u))).astype(BF)
        return 0

    def down(i, t, _):
        kind, a, b = ITEMS[i]
        at(f"down{a}", t)
        pl.when(t == 0)(functools.partial(complete, i))
        acc[...] += dot(act_s[t, :, a:b], block(2, lax.div(t, 2), lax.rem(t, 2), slice(a, b)), NT)
        return 0

    for i, item in enumerate(ITEMS):
        if item[0]:
            lax.fori_loop(0, 4, functools.partial((up, down)[item[0] - 1], i), 0)

    at("ln2")
    gv_s[...] = jnp.zeros_like(gv_s)

    def put(row, value):
        gv_s[0, row : row + 1] += value

    def norm2(i, sums):
        rr = pl.ds(pl.multiple_of(i * 128, 128), 128)
        u = acc[rr]
        u = u - jnp.mean(u, axis=-1, keepdims=True)
        rs = lax.rsqrt(jnp.mean(u * u, axis=-1, keepdims=True) + EPS)
        n = u * rs
        ag_s[rr] = (n * g2 + b2).astype(BF)
        ct = cot_s[rr].astype(F32)
        cg = ct * g2
        cgn = cg * n
        grad = rs * (cg - jnp.mean(cg, axis=-1, keepdims=True) - n * jnp.mean(cgn, axis=-1, keepdims=True))
        acc[rr] = grad
        grad = grad.astype(BF)
        dg_s[rr] = grad
        dgt_s[:, rr] = grad.T
        add = (ct * n, ct, grad.astype(F32))
        return tuple(a + jnp.sum(b, axis=0, keepdims=True) for a, b in zip(sums, add))

    sums = lax.fori_loop(0, 4, norm2, (jnp.zeros((1, D), F32),) * 3)
    for row, value in zip((5, 6, 2), sums):
        put(row, value)
    save_hid = pltpu.make_async_copy(ag_s, hid_hbm, io_sem.at[2])
    save_hid.start()


    def down_grad(n, cc):
        zz = zs[ORDER[n]]
        rr = pl.ds(pl.multiple_of(192 * zz, 64), 192)
        for yy in range(2):
            value = dot(dgt_s[rr], act_s[2 * yy + cc], NN).astype(BF)
            g12[1, yy, cc, pairs(zz)] = value.reshape(2, 96, D)

    for n in range(4):
        transfers(STEPS.get(("dw2", n, 0), ()))
        down_grad(n, cn)
        transfers(STEPS.get(("dw2", n, 1), ()))
        down_grad(n, c)

    def turn(n):
        return jnp.where(n < 2, yn, y), jnp.where(lax.rem(n, 2) == 0, cn, c)

    def up_grad(n, _):
        yy, cc = turn(n)
        t = 2 * yy + cc
        at("dw1", n, 0)
        ig = (dot(dg_s[...], block(2, yy, cc), NN) * gp_s[t].astype(F32)).astype(BF)
        ig_s[...] = ig
        gv_s[t, 0:1] = jnp.sum(ig.astype(F32), axis=0, keepdims=True)
        g12[0, yy, cc] = dot(nl_s[...], ig_s[...], TN).astype(BF).reshape(8, 96, D)
        at("dw1", n, 1)
        acc[...] += dot(ig_s[...], block(1, yy, cc), NT)
        return 0

    lax.fori_loop(0, 4, up_grad, 0)
    gather_sent()
    for peer in me.peers:
        pl.semaphore_signal(ready, inc=1, device_id=peer, device_id_type=MESH)

    at("ln1b")
    save_hid.wait()

    def norm1_back(i, _):
        rr = pl.ds(pl.multiple_of(i * 128, 128), 128)
        n, gr = z1_s[rr], acc[rr]
        put(3, jnp.sum(gr * n, axis=0, keepdims=True))
        put(4, jnp.sum(gr, axis=0, keepdims=True))
        cg = gr * g1
        grad = rs1_s[rr, 0:1] * (
            cg
            - jnp.mean(cg, axis=-1, keepdims=True)
            - n * jnp.mean(cg * n, axis=-1, keepdims=True)
        )
        acc[rr] = grad
        grad = grad.astype(BF)
        ag_s[rr] = grad
        put(1, jnp.sum(grad.astype(F32), axis=0, keepdims=True))
        return 0

    lax.fori_loop(0, 4, norm1_back, 0)

    def attend_back(n, _):
        yy, cc = turn(n)
        t = 2 * yy + cc
        at("dw0", n, 0)
        pl.when(n == 0)(functools.partial(pl.semaphore_wait, ready, len(me.peers)))
        mg = dot(ag_s[...], block(0, yy, cc, slice(512, 768)), NN)
        dq, dk, dv = [None] * 3, [None] * 3, [None] * 3
        for h, (qt, kt, vt, ot, qu, vu, ou) in enumerate(HEADS):
            if h:
                at("dw0", n, h)
            go = half_of(mg[:, 128:256] if ot == 5 else mg[:, 0:128], ou)
            inner = jnp.sum(go * a_s[t, :, tile(ot)].astype(F32), axis=-1, keepdims=True)
            go = go.astype(BF)
            p = p_s[t, h]
            dv[h] = dot(p, go, TN)
            ds = (p.astype(F32) * (dot(go, a_s[t, :, tile(vt)], NT) - inner)).astype(BF)
            dq[h] = dot(ds, a_s[t, :, tile(kt)], NN) * 0.125
            dk[h] = dot(ds, a_s[t, :, tile(qt)], TN) * 0.125
        da_s[:, tile(0)] = jnp.where(low, dq[0], dq[1]).astype(BF)
        da_s[:, tile(1)] = jnp.where(low, dk[0], dk[1]).astype(BF)
        da_s[:, tile(2)] = jnp.where(low, dv[0], dv[1]).astype(BF)
        da_s[:, tile(3)] = jnp.where(low, dq[2], dv[2]).astype(BF)
        da_s[:, tile(4)] = jnp.where(low, dk[2], 0.0).astype(BF)
        at("dw0", n, 3)
        sums = jnp.sum(da_s[...].astype(F32), axis=0, keepdims=True)
        for s, start in enumerate(SLOTS):
            m = start // 128
            gv_s[t, 7 + s : 8 + s, tile(m)] = half_of(sums[:, tile(m)], (start // 64) % 2)
        g0 = w.at[2, yy, cc]
        g0[:, :, 0:512] = dot(x_s[...], da_s[:, 0:512], TN).astype(BF).reshape(8, 96, 512)
        tail = dot(ag_s[...], mixed_of(t), TN)
        mixed = tail[:, 0:128] + dot(x_s[...], da_s[:, tile(4)], TN)
        g0[:, :, 512:640] = mixed.astype(BF).reshape(8, 96, 128)
        g0[:, :, 640:768] = tail[:, 128:256].astype(BF).reshape(8, 96, 128)
        at("dw0", n, 4)
        acc[...] += dot(da_s[...], block(0, yy, cc, slice(0, 640)), NT)
        return 0

    lax.fori_loop(0, 4, attend_back, 0)
    at("gx")
    dg_s[...] = acc[...].astype(BF)
    save_gx = pltpu.make_async_copy(dg_s, gx_hbm, io_sem.at[3])
    save_gx.start()
    at("small")

    for t in range(1, 4):
        gv_s[t, 1:7] = gv_s[0, 1:7]

    def collect(d, _):
        vec, head = spread(d)
        zz, xx = lax.div(d, 2), lax.rem(d, 2)
        val = gv_s[...].reshape(64, D)
        high = val.astype(BF)
        rest = (val - high.astype(F32)).astype(BF)
        is_vec = (iota((64, 1), 0) & 15) < 7
        got = jnp.where(is_vec, dot(high, vec, NT) + dot(rest, vec, NT), dot(high, head, NT) + dot(rest, head, NT))
        for t in range(4):
            sb[t % 2, xx, t // 2, zz] = got[16 * t : 16 * t + 16]
        return 0

    lax.fori_loop(0, 8, collect, 0)
    at("tail")
    grads_sent()
    save_gx.wait()


def run(r, *args):
    vm, hbm = pl.BlockSpec(memory_space=pltpu.VMEM), pl.BlockSpec(memory_space=pl.ANY)
    sm = pl.BlockSpec(memory_space=pltpu.SMEM)
    t = (SEQ, D)
    V = pltpu.VMEM
    items = len(ITEMS)
    gather = [DMA((items,))] * 3 + [DMA((items, 4))] * 3 + [DMA((items,))] * 2
    back = [DMA((3,))] * 3 + [DMA((3, 4))] * 4 + [DMA((3,))]
    blocks = (2, 2, 8, 96, D)
    return pl.pallas_call(
        functools.partial(kernel, r),
        out_shape=(
            jax.ShapeDtypeStruct(t, BF),
            jax.ShapeDtypeStruct(t, BF),
            jax.ShapeDtypeStruct((3, 96, D), F32),
            jax.ShapeDtypeStruct((16, 128), F32),
        ),
        in_specs=[sm, hbm, hbm] + [vm] * 15,
        out_specs=(hbm, hbm, vm, vm),
        scratch_shapes=[
            V((3, 96, D), BF), V((3,) + blocks, BF), V((2,) + blocks, BF), V((2,) + blocks, BF),
            V((16, 128), F32), V((2, 2, 2, 4, 16, 128), F32), V((64, D), F32), V((64, D), F32),
            V((4,) + t, BF), V((4, 3, SEQ, SEQ), BF), V(t, F32), V((SEQ, 128), F32), V(t, F32),
            V((4,) + t, BF), V((4,) + t, BF), V(t, BF),
            V(t, BF), V(t, BF), V(t, BF), V((D, SEQ), BF), V(t, BF), V(t, BF), V((SEQ, 640), BF), V((4, 16, D), F32),
            V((2, 2, 4, 16, 128), F32), V((2, 4, 16, 128), F32), V((4, 16, 128), F32), V((4, 16, 128), F32),
            DMA((4,)), DMA((1,)), *gather, DMA((7,)), DMA((7,)),
            *back, DMA((7,)), DMA((7,)), pltpu.SemaphoreType.REGULAR,
        ],
        compiler_params=pltpu.CompilerParams(
            collective_id=0, has_side_effects=True, vmem_limit_bytes=67043328
        ),
    )(*args)


def finish_kernel(h_in, x_in, g_ref, s_ref, *outs):
    h_out, x_out, wq, wk, wv, wo, w1, w2, bq, bv, c1, bo, c2, g1, b1, g2, b2 = outs[:17]
    h_s, x_s, sem = outs[17:]
    there = [pltpu.make_async_copy(a, b, sem.at[i]) for i, (a, b) in enumerate(((h_in, h_s), (x_in, x_s)))]
    back = [pltpu.make_async_copy(a, b, sem.at[2 + i]) for i, (a, b) in enumerate(((h_s, h_out), (x_s, x_out)))]
    for cp in there:
        cp.start()
    a = g_ref[0]
    for n, ref in enumerate((wq, wk, wv)):
        ref[:, 0:128] = a[:, 128 * n : 128 * n + 128]
    wq[:, 128:192] = a[:, 384:448]
    wk[:, 128:192] = a[:, 512:576]
    wv[:, 128:192] = a[:, 448:512]
    eye = (iota((96, 96), 0) == iota((96, 96), 1)).astype(F32)
    turned = lax.dot_general(
        a[:, 512:768], eye, (TN, ((), ())), preferred_element_type=F32, precision=lax.Precision.HIGHEST
    )
    wo[0:128] = turned[128:256]
    wo[128:192] = turned[64:128]
    w1[...] = g_ref[1]
    w2[...] = g_ref[2]
    bq[...] = s_ref[7:10, 0:8]
    bv[...] = s_ref[10:13, 0:8]
    for n, ref in enumerate((c1, bo, c2, g1, b1, g2, b2)):
        ref[...] = s_ref[n : n + 1, 0:96]
    for first, second in zip(there, back):
        first.wait()
        second.start()
    for cp in back:
        cp.wait()


def finish(hidden, gx, grads, small):
    shapes = [(96, 192)] * 3 + [(192, 96), (96, D), (96, D), (3, 8), (3, 8)] + [(1, 96)] * 7
    tokens = jax.ShapeDtypeStruct((SEQ, D), BF)
    vm, hbm = pl.BlockSpec(memory_space=pltpu.VMEM), pl.BlockSpec(memory_space=pl.ANY)
    out = pl.pallas_call(
        finish_kernel,
        out_shape=[tokens, tokens] + [jax.ShapeDtypeStruct(s, F32) for s in shapes],
        in_specs=[hbm, hbm, vm, vm],
        out_specs=[hbm, hbm] + [vm] * 15,
        scratch_shapes=[pltpu.VMEM((SEQ, D), BF)] * 2 + [DMA((4,))],
    )(hidden, gx, grads, small)
    out = list(out)
    return out[:7] + [out[7].T] + out[8:11] + [i.reshape(96) for i in out[11:]]


def body(
    hidden_in, seq_lengths, out_grad, query_weight, key_weight, value_weight, output_weight, up_weight,
    down_weight, query_bias, value_bias, inner_bias, output_bias, down_bias, first_gain, first_shift,
    second_gain, second_shift,
):
    r = lax.axis_size("dp") // 8
    groups = [[g * r + i for i in range(r)] for g in range(8)]

    def whole(value, axis):
        if r == 1:
            return value
        value = value.astype(BF)
        return lax.all_gather(value, "dp", axis=axis, tiled=True, axis_index_groups=groups).astype(F32)

    def shard(value, axis):
        if r == 1:
            return value
        return lax.psum_scatter(value, "dp", scatter_dimension=axis, tiled=True, axis_index_groups=groups)

    vectors = (output_bias, down_bias, first_gain, first_shift, second_gain, second_shift)
    hidden, gx, gw, gs = run(
        r, seq_lengths, hidden_in, out_grad,
        whole(query_weight, 0), whole(key_weight, 0), whole(value_weight, 0), whole(output_weight, 1),
        whole(up_weight, 0), whole(down_weight.T, 0),
        whole(query_bias, 1), whole(value_bias, 1), whole(inner_bias, 1),
        *(whole(i.reshape(1, -1), 1) for i in vectors),
    )
    if r == 1:
        return tuple(finish(hidden, gx, gw, gs))
    gw = shard(gw, 1)
    gv = shard(gs[0:7, 0:96], 1)
    gh = shard(gs[7:13, 0:8], 1)
    a = gw[0]
    return (
        hidden,
        gx,
        jnp.concatenate([a[:, 0:128], a[:, 384:448]], axis=1),
        jnp.concatenate([a[:, 128:256], a[:, 512:576]], axis=1),
        jnp.concatenate([a[:, 256:384], a[:, 448:512]], axis=1),
        jnp.concatenate([a[:, 640:768], a[:, 576:640]], axis=1).T,
        gw[1],
        gw[2].T,
        gh[0:3],
        gh[3:6],
        gv[0:1],
        *(gv[i] for i in range(1, 7)),
    )


def solution(mesh):
    both, dp = P(("dp", "tensor"), None), P("dp")
    rows_first, columns_first = P("dp", "tensor"), P("tensor", "dp")
    weights = (rows_first,) * 3 + (columns_first, rows_first, columns_first)
    smalls = (columns_first,) * 3 + (dp,) * 6
    return jax.shard_map(
        body,
        mesh=mesh,
        in_specs=(P("dp", None),) * 3 + weights + smalls,
        out_specs=(both, both) + weights + smalls,
        check_vma=False,
    )
```

```python
import functools

import jax
import jax.numpy as jnp
from jax import lax
from jax.experimental import pallas as pl
from jax.experimental.pallas import tpu as pltpu
from jax.sharding import PartitionSpec as P

SEQ = 512
D = 768
EPS = 1e-12
NEGATIVE = -1000000000.0
MESH = pl.DeviceIdType.MESH
BF = jnp.bfloat16
F32 = jnp.float32
DMA = pltpu.SemaphoreType.DMA
NN, NT, TN = ((1,), (0,)), ((1,), (1,)), ((0,), (0,))
HEADS = ((0, 1, 2, 5, 0, 0, 0), (0, 1, 2, 5, 1, 1, 1), (3, 4, 3, 4, 0, 1, 1))
SLOTS = (0, 64, 384, 256, 320, 448)
ITEMS = ((0, 0, 768), (1, 0, 768), (2, 0, 512), (2, 512, 768))
ORDER = (2, 1, 3, 0)
AHEAD = {1: 3, 0: 1}
STEPS = {
    ("pack",): (("o", 0), ("sa", 0)),
    ("mask",): (("oz", 0), ("o", 1), ("o", 2)),
    ("expand",): (("o", 3), ("ry", 0, 0), ("rx", 1, 0), ("ry", 1, 0), ("rx", 2, 0), ("sa", 1), ("rx", 0, 0),
        ("ry", 2, 0), ("q", 0, 3), ("q", 0, 1), ("q", 0, 2), ("sa", 2), ("oz", 1), ("rx", 0, 1), ("rx", 3, 0),
        ("rx", 0, 3), ("ry", 0, 3), ("sa", 3), ("ry", 0, 2), ("ry", 3, 0), ("ry", 0, 1), ("q", 1, 3), ("rx", 0, 2),
        ("oz", 2)),
    ("att", 0, 0): (("q", 1, 1), ("q", 1, 2), ("ry", 1, 3), ("oz", 3), ("rx", 1, 3), ("fa", 0), ("ry", 1, 1),
        ("q", 2, 3), ("rx", 1, 2), ("rx", 1, 1), ("ry", 1, 2)),
    ("att", 1, 0): (("q", 2, 1),),
    ("att", 1, 2): (("q", 2, 2),),
    ("att", 2, 0): (("rx", 2, 3),),
    ("att", 2, 2): (("ry", 2, 3),),
    ("att", 2, 3): (("q", 3, 2), ("q", 3, 3), ("fa", 1), ("q", 3, 1)),
    ("att", 3, 0): (("ry", 2, 1),),
    ("att", 3, 1): (("rx", 2, 2),),
    ("att", 3, 2): (("rx", 2, 1), ("ry", 2, 2)),
    ("up0", 0): (("ry", 3, 2), ("ry", 3, 1), ("rx", 3, 1)),
    ("up0", 1): (("ry", 3, 3), ("rx", 3, 2), ("rx", 3, 3)),
    ("up0", 2): (("fa", 2),),
    ("down0", 0): (("fa", 3),),
    ("dw2", 0, 1): (("ps", 2, 2),),
    ("dw2", 2, 0): (("pa", 2, 2), ("ps", 2, 1)),
    ("dw2", 2, 1): (("ps", 2, 3),),
    ("dw1", 0, 0): (("pa", 2, 3),),
    ("dw1", 0, 1): (("ps", 1, 0), ("pa", 2, 1)),
    ("dw1", 1, 1): (("by", 2, 2), ("bx", 2, 2), ("ps", 2, 0)),
    ("dw1", 2, 1): (("pa", 2, 0),),
    ("dw1", 3, 0): (("ps", 1, 1),),
    ("dw1", 3, 1): (("by", 2, 1), ("bx", 2, 1), ("pa", 1, 0)),
    ("ln1b",): (("by", 2, 3), ("pa", 1, 1)),
    ("dw0", 1, 2): (("bx", 2, 3), ("ps", 0, 0), ("cz", 2, 2), ("by", 1, 2)),
    ("dw0", 1, 4): (("bx", 1, 2), ("cz", 2, 1)),
    ("dw0", 2, 1): (("by", 2, 0),),
    ("dw0", 2, 4): (("ps", 0, 1), ("pa", 0, 0)),
    ("dw0", 3, 0): (("by", 1, 1), ("cz", 2, 3), ("bx", 1, 1), ("by", 1, 3)),
    ("dw0", 3, 1): (("by", 1, 0),),
    ("dw0", 3, 2): (("bx", 2, 0),),
    ("dw0", 3, 3): (("cz", 1, 2),),
    ("dw0", 3, 4): (("bx", 1, 3), ("pa", 0, 1)),
    ("gx",): (("by", 0, 2),),
    ("tail",): (("sb", 0), ("sb", 1), ("cz", 1, 1), ("bx", 1, 0), ("cz", 2, 0), ("bx", 0, 2), ("cz", 1, 3),
        ("by", 0, 1), ("cz", 0, 2), ("bx", 0, 1), ("sb", 2), ("by", 0, 3), ("cz", 0, 1), ("bx", 0, 3), ("sb", 3),
        ("cz", 1, 0), ("fz", 1), ("by", 0, 0), ("cz", 0, 3), ("fz", 2), ("bx", 0, 0), ("sb", 4), ("cz", 0, 0),
        ("fz", 0)),
}


def dot(a, b, dims):
    return lax.dot_general(a, b, (dims, ((), ())), preferred_element_type=F32)


def iota(shape, axis):
    return lax.broadcasted_iota(jnp.int32, shape, axis)


class Place:
    def __init__(self, r):
        dp = lax.axis_index("dp")
        t = lax.axis_index("tensor")
        g = lax.div(dp, r)
        self.r, self.q, self.t = r, lax.rem(dp, r), t
        self.z, self.x = lax.div(g, 2), lax.rem(g, 2)
        self.y, self.c = lax.div(t, 2), lax.rem(t, 2)
        self.xn, self.yn, self.cn = 1 - self.x, 1 - self.y, 1 - self.c
        self.zs = [lax.rem(self.z + i, 4) for i in range(4)]
        self.to_x = self.dev(self.z, self.xn, self.y, self.c)
        self.to_y = self.dev(self.z, self.x, self.yn, self.c)
        self.to_core = self.dev(self.z, self.x, self.y, self.cn)
        self.to_z = [self.dev(self.zs[i], self.x, self.y, self.c) for i in range(4)]
        self.peers = self.to_z[1:] + [self.to_x, self.to_y, self.to_core]

    def dev(self, z, x, y, c):
        return {"dp": (2 * z + x) * self.r + self.q, "tensor": 2 * y + c}


def remote(src, dst, ss, rs, to):
    return pltpu.make_async_remote_copy(
        src_ref=src, dst_ref=dst, send_sem=ss, recv_sem=rs, device_id=to, device_id_type=MESH
    )


def arrived(ref, sem):
    pltpu.make_async_copy(ref, ref, sem).wait()


def spread(d):
    lane, col = iota((128, D), 0), iota((128, D), 1)
    vec = (col == lane + 96 * d) & (lane < 96)
    head = ((col & 63) == lane + 8 * d) & (lane < 8)
    return vec.astype(F32).astype(BF), head.astype(F32).astype(BF)


def kernel(
    r,
    lens_ref, x_hbm, cot_hbm, *refs,
):
    shards_hbm, (hid_hbm, gx_hbm, o_hbm, so_hbm), refs = refs[:15], refs[15:19], refs[19:]
    shards, (load_sem, o_ref, so_ref, *refs) = refs[:15], refs[15:]
    work(
        r, lens_ref, x_hbm, cot_hbm, shards_hbm, shards, load_sem, hid_hbm, gx_hbm, o_hbm, so_hbm, o_ref, so_ref, *refs
    )


def work(
    r, lens_ref, x_hbm, cot_hbm, shards_hbm, shards, load_sem, hid_hbm, gx_hbm, o_hbm, so_hbm, o_ref, so_ref,
    own, w, g12, rb12, small, sb, vec_s, bqv_s, a_s, p_s, z1_s, rs1_s, acc, act_s, gp_s, nl_s,
    x_s, cot_s, dg_s, dgt_s, ig_s, ag_s, da_s, gv_s, s1, s2, s3, s4,
    io_sem, own_sem, s_first, s_far, s_core, r_z, r_x, r_y, r_far, r_core, ss_small, rs_small,
    t_p, t_1, t_2, u_p, u_y1, u_x1, u_2, u_z, ss_grad, rs_grad, ready,
):
    me = Place(r)
    z, x, y, c, xn, yn, cn, zs = me.z, me.x, me.y, me.c, me.xn, me.yn, me.cn, me.zs
    bar = pltpu.get_barrier_semaphore()
    for peer in me.peers:
        pl.semaphore_signal(bar, inc=1, device_id=peer, device_id_type=MESH)
    mine = pl.ds(pl.multiple_of(me.t * SEQ, SEQ), SEQ)
    load_x = pltpu.make_async_copy(x_hbm.at[mine], x_s, io_sem.at[0])
    load_c = pltpu.make_async_copy(cot_hbm.at[mine], cot_s, io_sem.at[1])
    loads = [pltpu.make_async_copy(a, b, load_sem.at[i]) for i, (a, b) in enumerate(zip(shards_hbm, shards))]
    for cp in loads:
        cp.start()
    load_x.start()
    load_c.start()
    wq_ref, wk_ref, wv_ref, wo_ref, w1_ref, w2_ref, bq_ref, bv_ref, *vector_refs = shards

    near, far = slice(0, 48), slice(48, 96)

    def piece(i, zz, xx, yy, rr=slice(None)):
        kind, a, b = ITEMS[i]
        return w.at[kind, yy, c, 2 * zz + xx, rr, a:b]

    def x_pair(i, zz, yy):
        kind, a, b = ITEMS[i]
        return w.at[kind, yy, c, pl.ds(2 * zz, 2), near, a:b]

    def y_pair(i, zz, xx):
        kind, a, b = ITEMS[i]
        return w.at[kind, :, c, 2 * zz + xx, far, a:b]

    def o_sends(i):
        kind, a, b = ITEMS[i]
        return [
            remote(own.at[kind, near, a:b], piece(i, z, x, y, near), s_first.at[i], r_x.at[i, z], me.to_x),
            remote(own.at[kind, far, a:b], piece(i, z, x, y, far), s_first.at[i], r_y.at[i, z], me.to_y),
        ]

    def o_wait(i):
        kind, a, b = ITEMS[i]
        cp = pltpu.make_async_copy(own.at[kind, :, a:b], piece(i, z, x, y), own_sem.at[0])
        cp.start()
        cp.wait()

    def oz_sends(i):
        kind, a, b = ITEMS[i]
        src, dst = own.at[kind, :, a:b], piece(i, z, x, y)
        return [remote(src, dst, s_first.at[i], r_z.at[i, z], me.to_z[j]) for j in (1, 3, 2)]

    def q_wait(i, j):
        arrived(piece(i, zs[j], x, y), r_z.at[i, zs[j]])

    def q_sends(i, j):
        a, b = piece(i, zs[j], x, y, near), piece(i, zs[j], x, y, far)
        return [
            remote(a, a, s_first.at[i], r_x.at[i, zs[j]], me.to_x),
            remote(b, b, s_first.at[i], r_y.at[i, zs[j]], me.to_y),
        ]

    def ry_wait(i, j):
        arrived(piece(i, zs[j], xn, y, near), r_x.at[i, zs[j]])

    def ry_sends(i, j):
        u = x_pair(i, zs[j], y)
        return [remote(u, u, s_far.at[i], r_far.at[i], me.to_y)]

    def rx_wait(i, j):
        arrived(piece(i, zs[j], x, yn, far), r_y.at[i, zs[j]])

    def rx_sends(i, j):
        u = y_pair(i, zs[j], x)
        return [remote(u, u, s_far.at[i], r_far.at[i], me.to_x)]

    def fa_wait(i):
        kind, a, b = ITEMS[i]
        arrived(w.at[kind, yn, c, :, :, a:b], r_far.at[i])

    def fa_sends(i):
        kind, a, b = ITEMS[i]
        u = w.at[kind, :, c, :, :, a:b]
        return [remote(u, u, s_core.at[i], r_core.at[i], me.to_core)]

    def complete(i):
        kind, a, b = ITEMS[i]
        arrived(w.at[kind, :, cn, :, :, a:b], r_core.at[i])

    def sa_wait(n):
        if n == 1:
            for j in (1, 2, 3):
                arrived(sb.at[c, x, y, z], rs_small.at[zs[j]])
        if n == 2:
            arrived(sb.at[c, x, y], rs_small.at[4])
        if n == 3:
            arrived(sb.at[c, :, y], rs_small.at[5])

    def sa_sends(n):
        u = (sb.at[c, x, y, z], sb.at[c, x, y], sb.at[c, :, y], sb.at[c])[n]
        if n == 0:
            return [remote(u, u, ss_small.at[j], rs_small.at[z], me.to_z[j]) for j in (1, 3, 2)]
        return [remote(u, u, ss_small.at[3 + n], rs_small.at[3 + n], (me.to_x, me.to_y, me.to_core)[n - 1])]

    def grad(kind):
        return w.at[2] if kind == 0 else g12.at[kind - 1]

    def land(kind):
        return w.at[1] if kind == 0 else rb12.at[kind - 1]

    def pairs(zz):
        return pl.ds(2 * zz, 2)

    def y1(kind, zz):
        return land(kind).at[1, 0, pairs(zz), near]

    def x1(kind, zz):
        return land(kind).at[1, 0, pairs(zz), far]

    def x2(kind, zz):
        return land(kind).at[1, 1, zz, near]

    def y2(kind, zz):
        return land(kind).at[1, 1, zz, far]

    def zb(kind, j):
        return land(kind).at[1, 1, 3 + j]

    def ps_sends(kind, n):
        if kind == 2:
            zz = zs[n]
            return [
                remote(grad(2).at[:, cn, pairs(zz)], land(2).at[0, :, pairs(zz)], t_p.at[2], u_p.at[2, zz], me.to_core)
            ]
        yy = (yn, y)[n]
        return [remote(grad(kind).at[yy, cn], land(kind).at[0, yy], t_p.at[kind], u_p.at[kind, yy], me.to_core)]

    def y1_send(kind, j):
        src = grad(kind).at[yn, c, pairs(zs[j]), near]
        return remote(src, y1(kind, zs[j]), t_1.at[kind], u_y1.at[kind, zs[j]], me.to_y)

    def x1_send(kind, j):
        src = grad(kind).at[:, c, 2 * zs[j] + xn, far]
        return remote(src, x1(kind, zs[j]), t_1.at[kind], u_x1.at[kind, zs[j]], me.to_x)

    def pa_wait(kind, n):
        g = grad(kind)
        if kind == 2:
            zz = zs[n]
            arrived(land(2).at[0, :, pairs(zz)], u_p.at[2, zz])
            g[:, c, pairs(zz)] = g[:, c, pairs(zz)] + land(2)[0, :, pairs(zz)]
            return
        yy = (yn, y)[n]
        arrived(land(kind).at[0, yy], u_p.at[kind, yy])

        def add(i, _):
            d = pl.ds(2 * i, 2)
            g[yy, c, d] = g[yy, c, d] + land(kind)[0, yy, d]
            return 0

        lax.fori_loop(0, 4, add, 0)

    def pa_sends(kind, n):
        if kind == 2:
            return [y1_send(2, n), x1_send(2, n)]
        return [(y1_send, x1_send)[n](kind, j) for j in ORDER[: AHEAD[kind]]]

    def later(kind, j, send):
        n = ORDER.index(j) + AHEAD.get(kind, 4)
        return [send(kind, ORDER[n])] if n < 4 else []

    def by_wait(kind, j):
        arrived(y1(kind, zs[j]), u_y1.at[kind, zs[j]])
        u = grad(kind).at[y, c, pairs(zs[j]), near]
        u[...] = u[...] + y1(kind, zs[j])[...]

    def by_sends(kind, j):
        src = grad(kind).at[y, c, 2 * zs[j] + xn, near]
        return [
            remote(src, x2(kind, zs[j]), t_2.at[kind], u_2.at[kind, zs[j]], me.to_x)
        ] + later(kind, j, y1_send)

    def bx_wait(kind, j):
        arrived(x1(kind, zs[j]), u_x1.at[kind, zs[j]])
        u = grad(kind).at[:, c, 2 * zs[j] + x, far]
        u[...] = u[...] + x1(kind, zs[j])[...]

    def bx_sends(kind, j):
        src = grad(kind).at[yn, c, 2 * zs[j] + x, far]
        return [
            remote(src, y2(kind, zs[j]), t_2.at[kind], u_2.at[kind, zs[j]], me.to_y)
        ] + later(kind, j, x1_send)

    def cz_wait(kind, j):
        arrived(land(kind).at[1, 1, zs[j]], u_2.at[kind, zs[j]])
        u = grad(kind).at[y, c, 2 * zs[j] + x]
        add = land(kind).at[1, 1, zs[j]]
        if j:
            u[...] = u[...] + add[...]
        else:
            o_ref[kind] = u[...].astype(F32) + add[...].astype(F32)

    def cz_sends(kind, j):
        if not j:
            return []
        src = grad(kind).at[y, c, 2 * zs[j] + x]
        return [remote(src, zb(kind, 4 - j), t_2.at[kind], u_z.at[kind], me.to_z[j])]

    def fz_wait(kind):
        arrived(land(kind).at[1, 1, 4:7], u_z.at[kind])
        o_ref[kind] = o_ref[kind] + sum(zb(kind, j)[...].astype(F32) for j in (1, 2, 3))
        save_grads[kind].start()

    save_grads = [pltpu.make_async_copy(o_ref.at[n], o_hbm.at[n], io_sem.at[4 + n]) for n in range(3)]
    save_small = pltpu.make_async_copy(so_ref, so_hbm, io_sem.at[7])

    def sb_wait(n):
        if n == 1:
            arrived(s1, rs_grad.at[4])
            sb[c] = sb[c] + s1[...]
        if n == 2:
            arrived(s2, rs_grad.at[5])
            sb[c, x] = sb[c, x] + s2[...]
        if n == 3:
            arrived(s3, rs_grad.at[6])
            sb[c, x, y] = sb[c, x, y] + s3[...]
        if n == 4:
            total = sb[c, x, y, z]
            for j in (1, 2, 3):
                arrived(s4.at[zs[j]], rs_grad.at[zs[j]])
                total = total + s4[zs[j]]
            so_ref[...] = total
            save_small.start()

    def sb_sends(n):
        if n == 3:
            return [
                remote(sb.at[c, x, y, zs[j]], s4.at[z], ss_grad.at[j], rs_grad.at[z], me.to_z[j]) for j in (1, 3, 2)
            ]
        if n == 4:
            return []
        src, dst = ((sb.at[cn], s1), (sb.at[c, xn], s2), (sb.at[c, x, yn], s3))[n]
        return [remote(src, dst, ss_grad.at[4 + n], rs_grad.at[4 + n], (me.to_core, me.to_x, me.to_y)[n])]

    waits = {
        "o": o_wait, "q": q_wait, "ry": ry_wait, "rx": rx_wait, "fa": fa_wait, "sa": sa_wait,
        "pa": pa_wait, "by": by_wait, "bx": bx_wait, "cz": cz_wait, "fz": fz_wait, "sb": sb_wait,
    }
    sends = {
        "o": o_sends, "oz": oz_sends, "q": q_sends, "ry": ry_sends, "rx": rx_sends, "fa": fa_sends, "sa": sa_sends,
        "ps": ps_sends, "pa": pa_sends, "by": by_sends, "bx": bx_sends, "cz": cz_sends, "sb": sb_sends,
    }

    def transfers(steps):
        for name, *args in steps:
            if name == "o":
                for cp in o_sends(*args):
                    cp.start()
            if name in waits:
                waits[name](*args)
            if name in sends and name != "o":
                for cp in sends[name](*args):
                    cp.start()

    def at(name, index=None, part=None):
        if index is None:
            transfers(STEPS.get((name,), ()))
            return
        for n in range(4):
            key = (name, n) if part is None else (name, n, part)
            if key in STEPS:
                pl.when(index == n)(functools.partial(transfers, STEPS[key]))

    def gather_sent():
        for i, (kind, a, b) in enumerate(ITEMS):
            arrived(w.at[kind, y, c, 0:7, :, a:b], s_first.at[i])
            arrived(w.at[kind, y, c, :, :, a:b], s_far.at[i])
            arrived(w.at[kind, :, c, :, :, a:b], s_core.at[i])
        for n in range(4):
            for cp in sa_sends(n):
                cp.wait_send()

    def grads_sent():
        for kind in range(3):
            arrived(grad(kind).at[:, cn], t_p.at[kind])
            arrived(grad(kind).at[y, c], t_1.at[kind])
            arrived(grad(kind).at[y, c, 0:7], t_2.at[kind])
        for n in range(4):
            for cp in sb_sends(n):
                cp.wait_send()

    eye = (iota((96, 96), 0) == iota((96, 96), 1)).astype(F32).astype(BF)
    for cp in loads:
        cp.wait()
    q, k, v = wq_ref[...], wk_ref[...], wv_ref[...]
    own[0, :, 0:128] = q[:, 0:128].astype(BF)
    own[0, :, 128:256] = k[:, 0:128].astype(BF)
    own[0, :, 256:384] = v[:, 0:128].astype(BF)
    own[0, :, 384:512] = jnp.concatenate([q[:, 128:192], v[:, 128:192]], axis=1).astype(BF)
    wo = wo_ref[...].astype(BF)
    o2 = dot(eye, wo[128:192], NT)
    own[0, :, 512:640] = jnp.concatenate([k[:, 128:192], o2], axis=1).astype(BF)
    own[0, :, 640:768] = dot(eye, wo[0:128], NT).astype(BF)
    small[...] = jnp.zeros_like(small)
    for i, ref in enumerate(vector_refs):
        small[i : i + 1, 0:96] = ref[...].astype(BF).astype(F32)
    small[7:10, 0:8] = bq_ref[...].astype(BF).astype(F32)
    small[10:13, 0:8] = bv_ref[...].astype(BF).astype(F32)
    sb[c, x, y, z] = small[...]
    pl.semaphore_wait(bar, len(me.peers))
    at("pack")
    own[1] = w1_ref[...].astype(BF)
    own[2] = w2_ref[...].astype(BF)
    at("mask")

    ends, total = [], jnp.int32(0)
    for i in range(4):
        total = total + lens_ref[me.t, i]
        ends.append(total)
    row, lane = iota((SEQ, 1), 0), iota((1, SEQ), 1)
    seg_q = sum((row >= e).astype(jnp.int32) for e in ends)
    seg_k = sum((lane >= e).astype(jnp.int32) for e in ends)
    valid = row < ends[3]
    same = jnp.where(valid, seg_q, row + 8) == jnp.where(lane < ends[3], seg_k, lane + 8)
    z1_s[:, 0:SEQ] = jnp.where(same, 0.0, NEGATIVE)
    load_c.wait()
    cot_s[...] = jnp.where(valid, cot_s[...].astype(F32), 0.0).astype(BF)
    load_x.wait()
    at("expand")
    arrived(sb.at[c], rs_small.at[6])

    vec_s[...] = jnp.zeros_like(vec_s)
    bqv_s[...] = jnp.zeros_like(bqv_s)

    def expand(d, _):
        vec, head = spread(d)
        zz, xx = lax.div(d, 2), lax.rem(d, 2)
        part = jnp.concatenate([sb[t % 2, xx, t // 2, zz] for t in range(4)], axis=0).astype(BF)
        vec_s[...] += dot(part, vec, NN)
        bqv_s[...] += dot(part, head, NN)
        return 0

    lax.fori_loop(0, 8, expand, 0)
    col = iota((1, D), 1)
    for t in range(4):
        bias = jnp.zeros((1, D), F32)
        for s, start in enumerate(SLOTS):
            keep = (col >= start) & (col < start + 64)
            bias = bias + jnp.where(keep, bqv_s[16 * t + 7 + s : 16 * t + 8 + s], 0.0)
        bqv_s[16 * t : 16 * t + 1] = bias
    bo, c2, g1, b1, g2, b2 = (vec_s[i : i + 1] for i in range(1, 7))

    low = iota((1, 128), 1) < 64
    acc[...] = x_s[...].astype(F32) + bo

    def tile(n):
        return slice(128 * n, 128 * n + 128)

    def half_of(values, upper):
        return jnp.where(low, 0.0, values) if upper else jnp.where(low, values, 0.0)

    def mixed_of(t):
        return jnp.concatenate(
            [half_of(a_s[t, :, tile(4)].astype(F32), 1).astype(BF), a_s[t, :, tile(5)]], axis=1
        )

    def block(kind, yy, cc, cols=slice(None)):
        value = w[kind, yy, cc, :, :, cols]
        return value.reshape(D, value.shape[-1])

    def attend(t, _):
        yy, cc = lax.div(t, 2), lax.rem(t, 2)
        at("att", t, 0)

        @pl.when(t == 0)
        def _():
            for i, item in enumerate(ITEMS):
                if item[0] == 0:
                    complete(i)

        pre = dot(x_s[...], block(0, yy, cc), NN) + bqv_s[pl.ds(pl.multiple_of(16 * t, 16), 1)]
        a_s[t] = pre.astype(BF)
        mix = [None] * 3
        for h, (qt, kt, vt, ot, qu, vu, ou) in enumerate(HEADS):
            at("att", t, h + 1)
            qh = (half_of(a_s[t, :, tile(qt)].astype(F32), qu) * 0.125).astype(BF)
            s = dot(qh, a_s[t, :, tile(kt)], NT) + z1_s[:, 0:SEQ]
            e = jnp.exp(s - jnp.max(s, axis=-1, keepdims=True))
            p = (e / jnp.sum(e, axis=-1, keepdims=True)).astype(BF)
            p_s[t, h] = p
            mix[h] = dot(p, a_s[t, :, tile(vt)], NN)
        a_s[t, :, tile(5)] = jnp.where(low, mix[0], mix[1]).astype(BF)
        a_s[t, :, tile(4)] = jnp.where(low, a_s[t, :, tile(4)].astype(F32), mix[2]).astype(BF)
        acc[...] += dot(mixed_of(t), block(0, yy, cc, slice(512, 768)), NT)
        return 0

    lax.fori_loop(0, 4, attend, 0)

    at("ln1")

    def norm1(i, _):
        rr = pl.ds(pl.multiple_of(i * 256, 256), 256)
        u = acc[rr]
        u = u - jnp.mean(u, axis=-1, keepdims=True)
        rs = lax.rsqrt(jnp.mean(u * u, axis=-1, keepdims=True) + EPS)
        n = u * rs
        z1_s[rr] = n
        rs1_s[rr] = jnp.broadcast_to(rs, (256, 128))
        n = n * g1 + b1
        nl_s[rr] = n.astype(BF)
        acc[rr] = n + c2
        return 0

    lax.fori_loop(0, 2, norm1, 0)

    def up(i, t, _):
        kind, a, b = ITEMS[i]
        at(f"up{a}", t)
        pl.when(t == 0)(functools.partial(complete, i))
        bias = vec_s[pl.ds(pl.multiple_of(16 * t, 16), 1), a:b]
        u = dot(nl_s[...], block(1, lax.div(t, 2), lax.rem(t, 2), slice(a, b)), NN) + bias
        phi = 0.5 + 0.5 * lax.erf(u * 0.7071067811865476)
        act_s[t, :, a:b] = (u * phi).astype(BF)
        gp_s[t, :, a:b] = (phi + u * (0.3989422804014327 * jnp.exp(-0.5 * u * u))).astype(BF)
        return 0

    def down(i, n, _):
        kind, a, b = ITEMS[i]
        at(f"down{a}", n)
        pl.when(n == 0)(functools.partial(complete, i))
        act = jnp.concatenate([act_s[2 * n, :, a:b], act_s[2 * n + 1, :, a:b]], axis=1)
        weight = jnp.concatenate([block(2, n, 0, slice(a, b)), block(2, n, 1, slice(a, b))], axis=1)
        acc[...] += dot(act, weight, NT)
        return 0

    for i, item in enumerate(ITEMS):
        if item[0]:
            lax.fori_loop(0, 6 - 2 * item[0], functools.partial((up, down)[item[0] - 1], i), 0)

    at("ln2")
    gv_s[...] = jnp.zeros_like(gv_s)

    def put(row, value):
        gv_s[0, row : row + 1] += value

    def norm2(i, sums):
        rr = pl.ds(pl.multiple_of(i * 256, 256), 256)
        u = acc[rr]
        u = u - jnp.mean(u, axis=-1, keepdims=True)
        rs = lax.rsqrt(jnp.mean(u * u, axis=-1, keepdims=True) + EPS)
        n = u * rs
        ag_s[rr] = (n * g2 + b2).astype(BF)
        ct = cot_s[rr].astype(F32)
        cg = ct * g2
        cgn = cg * n
        grad = rs * (cg - jnp.mean(cg, axis=-1, keepdims=True) - n * jnp.mean(cgn, axis=-1, keepdims=True))
        acc[rr] = grad
        grad = grad.astype(BF)
        dg_s[rr] = grad
        dgt_s[:, rr] = grad.T
        add = (ct * n, ct, grad.astype(F32))
        return tuple(a + jnp.sum(b, axis=0, keepdims=True) for a, b in zip(sums, add))

    sums = lax.fori_loop(0, 2, norm2, (jnp.zeros((1, D), F32),) * 3)
    for row, value in zip((5, 6, 2), sums):
        put(row, value)
    save_hid = pltpu.make_async_copy(ag_s, hid_hbm, io_sem.at[2])
    save_hid.start()


    def down_grad(n, cc):
        zz = zs[ORDER[n]]
        rr = pl.ds(pl.multiple_of(192 * zz, 64), 192)
        for yy in range(2):
            value = dot(dgt_s[rr], act_s[2 * yy + cc], NN).astype(BF)
            g12[1, yy, cc, pairs(zz)] = value.reshape(2, 96, D)

    for n in range(4):
        transfers(STEPS.get(("dw2", n, 0), ()))
        down_grad(n, cn)
        transfers(STEPS.get(("dw2", n, 1), ()))
        down_grad(n, c)

    def turn(n):
        return jnp.where(n < 2, yn, y), jnp.where(lax.rem(n, 2) == 0, cn, c)

    def up_grad(n, _):
        yy, cc = turn(n)
        t = 2 * yy + cc
        at("dw1", n, 0)
        ig = (dot(dg_s[...], block(2, yy, cc), NN) * gp_s[t].astype(F32)).astype(BF)
        ig_s[...] = ig
        gv_s[t, 0:1] = jnp.sum(ig.astype(F32), axis=0, keepdims=True)
        g12[0, yy, cc] = dot(nl_s[...], ig_s[...], TN).astype(BF).reshape(8, 96, D)
        at("dw1", n, 1)
        acc[...] += dot(ig_s[...], block(1, yy, cc), NT)
        return 0

    lax.fori_loop(0, 4, up_grad, 0)
    gather_sent()
    for peer in me.peers:
        pl.semaphore_signal(ready, inc=1, device_id=peer, device_id_type=MESH)

    at("ln1b")
    save_hid.wait()

    def norm1_back(i, _):
        rr = pl.ds(pl.multiple_of(i * 256, 256), 256)
        n, gr = z1_s[rr], acc[rr]
        put(3, jnp.sum(gr * n, axis=0, keepdims=True))
        put(4, jnp.sum(gr, axis=0, keepdims=True))
        cg = gr * g1
        grad = rs1_s[rr, 0:1] * (
            cg
            - jnp.mean(cg, axis=-1, keepdims=True)
            - n * jnp.mean(cg * n, axis=-1, keepdims=True)
        )
        acc[rr] = grad
        grad = grad.astype(BF)
        ag_s[rr] = grad
        put(1, jnp.sum(grad.astype(F32), axis=0, keepdims=True))
        return 0

    lax.fori_loop(0, 2, norm1_back, 0)

    def attend_back(n, _):
        yy, cc = turn(n)
        t = 2 * yy + cc
        at("dw0", n, 0)
        pl.when(n == 0)(functools.partial(pl.semaphore_wait, ready, len(me.peers)))
        mg = dot(ag_s[...], block(0, yy, cc, slice(512, 768)), NN)
        dq, dk, dv = [None] * 3, [None] * 3, [None] * 3
        for h, (qt, kt, vt, ot, qu, vu, ou) in enumerate(HEADS):
            if h:
                at("dw0", n, h)
            go = half_of(mg[:, 128:256] if ot == 5 else mg[:, 0:128], ou)
            inner = jnp.sum(go * a_s[t, :, tile(ot)].astype(F32), axis=-1, keepdims=True)
            go = go.astype(BF)
            p = p_s[t, h]
            dv[h] = dot(p, go, TN)
            ds = (p.astype(F32) * (dot(go, a_s[t, :, tile(vt)], NT) - inner)).astype(BF)
            dq[h] = dot(ds, a_s[t, :, tile(kt)], NN) * 0.125
            dk[h] = dot(ds, a_s[t, :, tile(qt)], TN) * 0.125
        da_s[:, tile(0)] = jnp.where(low, dq[0], dq[1]).astype(BF)
        da_s[:, tile(1)] = jnp.where(low, dk[0], dk[1]).astype(BF)
        da_s[:, tile(2)] = jnp.where(low, dv[0], dv[1]).astype(BF)
        da_s[:, tile(3)] = jnp.where(low, dq[2], dv[2]).astype(BF)
        da_s[:, tile(4)] = jnp.where(low, dk[2], 0.0).astype(BF)
        at("dw0", n, 3)
        sums = jnp.sum(da_s[...].astype(F32), axis=0, keepdims=True)
        for s, start in enumerate(SLOTS):
            m = start // 128
            gv_s[t, 7 + s : 8 + s, tile(m)] = half_of(sums[:, tile(m)], (start // 64) % 2)
        g0 = w.at[2, yy, cc]
        g0[:, :, 0:512] = dot(x_s[...], da_s[:, 0:512], TN).astype(BF).reshape(8, 96, 512)
        tail = dot(ag_s[...], mixed_of(t), TN)
        mixed = tail[:, 0:128] + dot(x_s[...], da_s[:, tile(4)], TN)
        g0[:, :, 512:640] = mixed.astype(BF).reshape(8, 96, 128)
        g0[:, :, 640:768] = tail[:, 128:256].astype(BF).reshape(8, 96, 128)
        at("dw0", n, 4)
        acc[...] += dot(da_s[...], block(0, yy, cc, slice(0, 640)), NT)
        return 0

    lax.fori_loop(0, 4, attend_back, 0)
    at("gx")
    dg_s[...] = acc[...].astype(BF)
    save_gx = pltpu.make_async_copy(dg_s, gx_hbm, io_sem.at[3])
    save_gx.start()
    at("small")

    for t in range(1, 4):
        gv_s[t, 1:7] = gv_s[0, 1:7]

    def collect(d, _):
        vec, head = spread(d)
        zz, xx = lax.div(d, 2), lax.rem(d, 2)
        val = gv_s[...].reshape(64, D)
        high = val.astype(BF)
        rest = (val - high.astype(F32)).astype(BF)
        is_vec = (iota((64, 1), 0) & 15) < 7
        got = jnp.where(is_vec, dot(high, vec, NT) + dot(rest, vec, NT), dot(high, head, NT) + dot(rest, head, NT))
        for t in range(4):
            sb[t % 2, xx, t // 2, zz] = got[16 * t : 16 * t + 16]
        return 0

    lax.fori_loop(0, 8, collect, 0)
    at("tail")
    grads_sent()
    for cp in [save_gx, save_small] + save_grads:
        cp.wait()


def run(r, *args):
    hbm, sm = pl.BlockSpec(memory_space=pl.ANY), pl.BlockSpec(memory_space=pltpu.SMEM)
    t = (SEQ, D)
    V = pltpu.VMEM
    items = len(ITEMS)
    gather = [DMA((items,))] * 3 + [DMA((items, 4))] * 3 + [DMA((items,))] * 2
    back = [DMA((3,))] * 3 + [DMA((3, 4))] * 4 + [DMA((3,))]
    blocks = (2, 2, 8, 96, D)
    return pl.pallas_call(
        functools.partial(kernel, r),
        out_shape=(
            jax.ShapeDtypeStruct(t, BF),
            jax.ShapeDtypeStruct(t, BF),
            jax.ShapeDtypeStruct((3, 96, D), F32),
            jax.ShapeDtypeStruct((16, 128), F32),
        ),
        in_specs=[sm] + [hbm] * 17,
        out_specs=(hbm,) * 4,
        scratch_shapes=[V(i.shape, i.dtype) for i in args[3:]]
        + [DMA((15,)), V((3, 96, D), F32), V((16, 128), F32)]
        + [
            V((3, 96, D), BF), V((3,) + blocks, BF), V((2,) + blocks, BF), V((2,) + blocks, BF),
            V((16, 128), F32), V((2, 2, 2, 4, 16, 128), F32), V((64, D), F32), V((64, D), F32),
            V((4,) + t, BF), V((4, 3, SEQ, SEQ), BF), V(t, F32), V((SEQ, 128), F32), V(t, F32),
            V((4,) + t, BF), V((4,) + t, BF), V(t, BF),
            V(t, BF), V(t, BF), V(t, BF), V((D, SEQ), BF), V(t, BF), V(t, BF), V((SEQ, 640), BF), V((4, 16, D), F32),
            V((2, 2, 4, 16, 128), F32), V((2, 4, 16, 128), F32), V((4, 16, 128), F32), V((4, 16, 128), F32),
            DMA((8,)), DMA((1,)), *gather, DMA((7,)), DMA((7,)),
            *back, DMA((7,)), DMA((7,)), pltpu.SemaphoreType.REGULAR,
        ],
        compiler_params=pltpu.CompilerParams(
            collective_id=0, has_side_effects=True, vmem_limit_bytes=67043328
        ),
    )(*args)


FINAL = ((96, 192),) * 3 + ((192, 96), (96, D), (96, D), (3, 8), (3, 8)) + ((1, 96),) * 7


def finish_kernel(hid_hbm, gx_hbm, g_hbm, s_hbm, *refs):
    outs, scratch, sem = refs[:17], refs[17:-1], refs[-1]
    hid, gx, g, s = scratch[:4]
    wq, wk, wv, wo, w1, w2, bq, bv, *vectors = scratch[4:]

    def copy(n, src, dst):
        cp = pltpu.make_async_copy(src, dst, sem.at[n])
        cp.start()
        return cp

    get_g, get_s = copy(0, g_hbm, g), copy(1, s_hbm, s)
    get_hid, get_gx = copy(2, hid_hbm, hid), copy(3, gx_hbm, gx)
    get_g.wait()
    out = [copy(8, g.at[1], outs[6]), copy(9, g.at[2], outs[7])]
    a = g[0]
    for n, ref in enumerate((wq, wk, wv)):
        ref[:, 0:128] = a[:, 128 * n : 128 * n + 128]
    wq[:, 128:192] = a[:, 384:448]
    wk[:, 128:192] = a[:, 512:576]
    wv[:, 128:192] = a[:, 448:512]
    out += [copy(10 + n, ref, outs[2 + n]) for n, ref in enumerate((wq, wk, wv))]
    get_hid.wait()
    out.append(copy(4, hid, outs[0]))
    get_gx.wait()
    out.append(copy(5, gx, outs[1]))
    eye = (iota((96, 96), 0) == iota((96, 96), 1)).astype(F32)
    turned = lax.dot_general(
        a[:, 512:768], eye, (TN, ((), ())), preferred_element_type=F32, precision=lax.Precision.HIGHEST
    )
    wo[0:128] = turned[128:256]
    wo[128:192] = turned[64:128]
    out.append(copy(6, wo, outs[5]))
    get_s.wait()
    bq[...] = s[7:10, 0:8]
    bv[...] = s[10:13, 0:8]
    for n, ref in enumerate(vectors):
        ref[...] = s[n : n + 1, 0:96]
    out += [copy(13 + n, ref, outs[8 + n]) for n, ref in enumerate((bq, bv, *vectors))]
    for cp in out:
        cp.wait()


def finish(hidden, gx, grads, small):
    tokens = jax.ShapeDtypeStruct((SEQ, D), BF)
    hbm = pl.BlockSpec(memory_space=pl.ANY)
    out = pl.pallas_call(
        finish_kernel,
        out_shape=[tokens, tokens] + [jax.ShapeDtypeStruct(s, F32) for s in FINAL],
        in_specs=[hbm] * 4,
        out_specs=[hbm] * 17,
        scratch_shapes=[pltpu.VMEM((SEQ, D), BF)] * 2
        + [pltpu.VMEM((3, 96, D), F32), pltpu.VMEM((16, 128), F32)]
        + [pltpu.VMEM(s, F32) for s in FINAL]
        + [DMA((22,))],
    )(hidden, gx, grads, small)
    out = list(out)
    return out[:7] + [out[7].T] + out[8:11] + [i.reshape(96) for i in out[11:]]


def body(
    hidden_in, seq_lengths, out_grad, query_weight, key_weight, value_weight, output_weight, up_weight,
    down_weight, query_bias, value_bias, inner_bias, output_bias, down_bias, first_gain, first_shift,
    second_gain, second_shift,
):
    r = lax.axis_size("dp") // 8
    groups = [[g * r + i for i in range(r)] for g in range(8)]

    def whole(value, axis):
        if r == 1:
            return value
        value = value.astype(BF)
        return lax.all_gather(value, "dp", axis=axis, tiled=True, axis_index_groups=groups).astype(F32)

    def shard(value, axis):
        if r == 1:
            return value
        return lax.psum_scatter(value, "dp", scatter_dimension=axis, tiled=True, axis_index_groups=groups)

    vectors = (output_bias, down_bias, first_gain, first_shift, second_gain, second_shift)
    hidden, gx, gw, gs = run(
        r, seq_lengths, hidden_in, out_grad,
        whole(query_weight, 0), whole(key_weight, 0), whole(value_weight, 0), whole(output_weight, 1),
        whole(up_weight, 0), whole(down_weight.T, 0),
        whole(query_bias, 1), whole(value_bias, 1), whole(inner_bias, 1),
        *(whole(i.reshape(1, -1), 1) for i in vectors),
    )
    if r == 1:
        return tuple(finish(hidden, gx, gw, gs))
    gw = shard(gw, 1)
    gv = shard(gs[0:7, 0:96], 1)
    gh = shard(gs[7:13, 0:8], 1)
    a = gw[0]
    return (
        hidden,
        gx,
        jnp.concatenate([a[:, 0:128], a[:, 384:448]], axis=1),
        jnp.concatenate([a[:, 128:256], a[:, 512:576]], axis=1),
        jnp.concatenate([a[:, 256:384], a[:, 448:512]], axis=1),
        jnp.concatenate([a[:, 640:768], a[:, 576:640]], axis=1).T,
        gw[1],
        gw[2].T,
        gh[0:3],
        gh[3:6],
        gv[0:1],
        *(gv[i] for i in range(1, 7)),
    )


def solution(mesh):
    both, dp = P(("dp", "tensor"), None), P("dp")
    rows_first, columns_first = P("dp", "tensor"), P("tensor", "dp")
    weights = (rows_first,) * 3 + (columns_first, rows_first, columns_first)
    smalls = (columns_first,) * 3 + (dp,) * 6
    return jax.shard_map(
        body,
        mesh=mesh,
        in_specs=(P("dp", None),) * 3 + weights + smalls,
        out_specs=(both, both) + weights + smalls,
        check_vma=False,
    )
```

```python
import functools

import jax
import jax.numpy as jnp
from jax import lax
from jax.experimental import pallas as pl
from jax.experimental.pallas import tpu as pltpu
from jax.sharding import PartitionSpec as P

SEQ = 512
D = 768
EPS = 1e-12
NEGATIVE = -1000000000.0
MESH = pl.DeviceIdType.MESH
BF = jnp.bfloat16
F32 = jnp.float32
DMA = pltpu.SemaphoreType.DMA
NN, NT, TN = ((1,), (0,)), ((1,), (1,)), ((0,), (0,))
HEADS = ((0, 1, 2, 5, 0, 0, 0), (0, 1, 2, 5, 1, 1, 1), (3, 4, 3, 4, 0, 1, 1))
SLOTS = (0, 64, 384, 256, 320, 448)
ITEMS = ((0, 0, 768), (1, 0, 768), (2, 0, 512), (2, 512, 768))
PIECES = (3, 2, 1, 0)
ORDER = (2, 3, 1, 0)
AHEAD = 1
PAIRED = (1, 2)
STEPS = {
    ("pack",): (("o", 0), ("sa", 0)),
    ("mask",): (("oz", 0), ("o", 1), ("o", 2)),
    ("expand",): (("o", 3), ("ry", 0, 0), ("rx", 1, 0), ("ry", 1, 0), ("rx", 2, 0), ("sa", 1), ("rx", 0, 0),
        ("ry", 2, 0), ("q", 0, 3), ("q", 0, 1), ("q", 0, 2), ("sa", 2), ("oz", 1), ("rx", 0, 1), ("rx", 3, 0),
        ("rx", 0, 3), ("ry", 0, 3), ("sa", 3), ("ry", 0, 2), ("ry", 3, 0), ("ry", 0, 1), ("q", 1, 3), ("rx", 0, 2),
        ("oz", 2)),
    ("att", 0, 0): (("q", 1, 1), ("q", 1, 2), ("ry", 1, 3), ("oz", 3), ("rx", 1, 3), ("fa", 0), ("ry", 1, 1),
        ("q", 2, 3), ("rx", 1, 2), ("rx", 1, 1), ("ry", 1, 2)),
    ("att", 1, 0): (("q", 2, 1),),
    ("att", 1, 2): (("q", 2, 2),),
    ("att", 2, 0): (("rx", 2, 3),),
    ("att", 2, 2): (("ry", 2, 3),),
    ("att", 2, 3): (("q", 3, 2), ("q", 3, 3), ("fa", 1), ("q", 3, 1)),
    ("att", 3, 0): (("ry", 2, 1),),
    ("att", 3, 1): (("rx", 2, 2),),
    ("att", 3, 2): (("rx", 2, 1), ("ry", 2, 2)),
    ("up0", 0): (("ry", 3, 2), ("ry", 3, 1), ("rx", 3, 1)),
    ("up0", 1): (("ry", 3, 3), ("rx", 3, 2), ("rx", 3, 3)),
    ("up0", 2): (("fa", 2),),
    ("down0", 0): (("fa", 3),),
    ("dw2", 0, 1): (("ps", 2, 3),),
    ("dw2", 2, 1): (("pa", 2, 3), ("ps", 2, 1)),
    ("dw2", 3, 0): (("bx", 2, 3),),
    ("dw2", 3, 1): (("by", 2, 3), ("ps", 2, 2), ("ps", 2, 0)),
    ("dw1", 0, 0): (("pa", 2, 1),),
    ("dw1", 0, 1): (("ps", 1, 0), ("pa", 2, 2)),
    ("dw1", 1, 0): (("pa", 2, 0),),
    ("dw1", 2, 0): (("cz", 2, 3), ("pa", 1, 0)),
    ("dw1", 2, 1): (("by", 2, 1),),
    ("dw1", 3, 0): (("ps", 1, 1), ("ee", 2), ("bx", 2, 1)),
    ("dw0", 0, 0): (("pa", 1, 1),),
    ("dw0", 0, 1): (("bx", 1, 3), ("by", 1, 1)),
    ("dw0", 0, 2): (("by", 1, 3),),
    ("dw0", 1, 0): (("by", 2, 2), ("by", 2, 0), ("bx", 2, 2)),
    ("dw0", 1, 2): (("cz", 2, 1), ("bx", 2, 0), ("ps", 0, 0)),
    ("dw0", 1, 4): (("ee", 1), ("bx", 1, 1)),
    ("dw0", 2, 0): (("cz", 1, 3),),
    ("dw0", 2, 2): (("pa", 0, 0),),
    ("dw0", 2, 4): (("cz", 2, 2),),
    ("dw0", 3, 1): (("bx", 1, 2), ("by", 1, 2), ("ps", 0, 1)),
    ("dw0", 3, 2): (("cz", 2, 0), ("by", 1, 0)),
    ("dw0", 3, 4): (("pa", 0, 1),),
    ("tail",): (("sb", 0), ("cz", 1, 2), ("by", 0, 2), ("sb", 1), ("cz", 1, 1), ("fz", 2), ("bx", 0, 2),
        ("bx", 1, 0), ("by", 0, 3), ("sb", 2), ("cz", 0, 2), ("bx", 0, 3), ("by", 0, 1), ("sb", 3), ("cz", 0, 3),
        ("bx", 0, 1), ("cz", 1, 0), ("cz", 0, 1), ("fz", 1), ("sb", 4), ("by", 0, 0), ("bx", 0, 0), ("cz", 0, 0),
        ("fz", 0)),
}


def dot(a, b, dims):
    return lax.dot_general(a, b, (dims, ((), ())), preferred_element_type=F32)


def iota(shape, axis):
    return lax.broadcasted_iota(jnp.int32, shape, axis)


class Place:
    def __init__(self, r):
        dp = lax.axis_index("dp")
        t = lax.axis_index("tensor")
        g = lax.div(dp, r)
        self.r, self.q, self.t = r, lax.rem(dp, r), t
        self.z, self.x = lax.div(g, 2), lax.rem(g, 2)
        self.y, self.c = lax.div(t, 2), lax.rem(t, 2)
        self.xn, self.yn, self.cn = 1 - self.x, 1 - self.y, 1 - self.c
        self.zs = [lax.rem(self.z + i, 4) for i in range(4)]
        self.to_x = self.dev(self.z, self.xn, self.y, self.c)
        self.to_y = self.dev(self.z, self.x, self.yn, self.c)
        self.to_core = self.dev(self.z, self.x, self.y, self.cn)
        self.to_z = [self.dev(self.zs[i], self.x, self.y, self.c) for i in range(4)]
        self.zx = [self.z, self.z + 1 - 2 * lax.rem(self.z, 2), self.zs[2], 3 - self.z]
        self.to_zx = [self.dev(i, self.x, self.y, self.c) for i in self.zx]
        self.peers = self.to_z[1:] + [self.to_x, self.to_y, self.to_core]

    def dev(self, z, x, y, c):
        return {"dp": (2 * z + x) * self.r + self.q, "tensor": 2 * y + c}


def remote(src, dst, ss, rs, to):
    return pltpu.make_async_remote_copy(
        src_ref=src, dst_ref=dst, send_sem=ss, recv_sem=rs, device_id=to, device_id_type=MESH
    )


def arrived(ref, sem):
    pltpu.make_async_copy(ref, ref, sem).wait()


def spread(d):
    lane, col = iota((128, D), 0), iota((128, D), 1)
    vec = (col == lane + 96 * d) & (lane < 96)
    head = ((col & 63) == lane + 8 * d) & (lane < 8)
    return vec.astype(F32).astype(BF), head.astype(F32).astype(BF)


def kernel(
    r,
    lens_ref, x_hbm, cot_hbm, *refs,
):
    shards_hbm, (hid_hbm, gx_hbm, o_hbm, so_hbm), refs = refs[:15], refs[15:19], refs[19:]
    shards, (load_sem, o_ref, so_ref, *refs) = refs[:15], refs[15:]
    work(
        r, lens_ref, x_hbm, cot_hbm, shards_hbm, shards, load_sem, hid_hbm, gx_hbm, o_hbm, so_hbm, o_ref, so_ref, *refs
    )


def work(
    r, lens_ref, x_hbm, cot_hbm, shards_hbm, shards, load_sem, hid_hbm, gx_hbm, o_hbm, so_hbm, o_ref, so_ref,
    own, w, g12, rb12, small, sb, vec_s, bqv_s, a_s, p_s, z1_s, rs1_s, acc, act_s, gp_s, nl_s,
    x_s, cot_s, dg_s, dgt_s, ig_s, ag_s, da_s, gv_s, s1, s2, s3, s4,
    io_sem, own_sem, s_first, s_far, s_core, r_z, r_x, r_y, r_far, r_core, ss_small, rs_small,
    t_p, t_1, t_2, u_p, u_y1, u_x1, u_2, u_z, u_e, ss_grad, rs_grad, ready,
):
    me = Place(r)
    z, x, y, c, xn, yn, cn, zs, zx = me.z, me.x, me.y, me.c, me.xn, me.yn, me.cn, me.zs, me.zx
    bar = pltpu.get_barrier_semaphore()
    for peer in me.peers:
        pl.semaphore_signal(bar, inc=1, device_id=peer, device_id_type=MESH)
    mine = pl.ds(pl.multiple_of(me.t * SEQ, SEQ), SEQ)
    load_x = pltpu.make_async_copy(x_hbm.at[mine], x_s, io_sem.at[0])
    load_c = pltpu.make_async_copy(cot_hbm.at[mine], cot_s, io_sem.at[1])
    loads = [pltpu.make_async_copy(a, b, load_sem.at[i]) for i, (a, b) in enumerate(zip(shards_hbm, shards))]
    for cp in loads:
        cp.start()
    load_x.start()
    load_c.start()
    wq_ref, wk_ref, wv_ref, wo_ref, w1_ref, w2_ref, bq_ref, bv_ref, *vector_refs = shards

    near, far = slice(0, 48), slice(48, 96)

    def piece(i, zz, xx, yy, rr=slice(None)):
        kind, a, b = ITEMS[i]
        return w.at[kind, yy, c, 2 * zz + xx, rr, a:b]

    def x_pair(i, zz, yy):
        kind, a, b = ITEMS[i]
        return w.at[kind, yy, c, pl.ds(2 * zz, 2), near, a:b]

    def y_pair(i, zz, xx):
        kind, a, b = ITEMS[i]
        return w.at[kind, :, c, 2 * zz + xx, far, a:b]

    def o_sends(i):
        kind, a, b = ITEMS[i]
        return [
            remote(own.at[kind, near, a:b], piece(i, z, x, y, near), s_first.at[i], r_x.at[i, z], me.to_x),
            remote(own.at[kind, far, a:b], piece(i, z, x, y, far), s_first.at[i], r_y.at[i, z], me.to_y),
        ]

    def o_wait(i):
        kind, a, b = ITEMS[i]
        cp = pltpu.make_async_copy(own.at[kind, :, a:b], piece(i, z, x, y), own_sem.at[0])
        cp.start()
        cp.wait()

    def oz_sends(i):
        kind, a, b = ITEMS[i]
        src, dst = own.at[kind, :, a:b], piece(i, z, x, y)
        return [remote(src, dst, s_first.at[i], r_z.at[i, z], me.to_z[j]) for j in (1, 3, 2)]

    def q_wait(i, j):
        arrived(piece(i, zs[j], x, y), r_z.at[i, zs[j]])

    def q_sends(i, j):
        a, b = piece(i, zs[j], x, y, near), piece(i, zs[j], x, y, far)
        return [
            remote(a, a, s_first.at[i], r_x.at[i, zs[j]], me.to_x),
            remote(b, b, s_first.at[i], r_y.at[i, zs[j]], me.to_y),
        ]

    def ry_wait(i, j):
        arrived(piece(i, zs[j], xn, y, near), r_x.at[i, zs[j]])

    def ry_sends(i, j):
        u = x_pair(i, zs[j], y)
        return [remote(u, u, s_far.at[i], r_far.at[i], me.to_y)]

    def rx_wait(i, j):
        arrived(piece(i, zs[j], x, yn, far), r_y.at[i, zs[j]])

    def rx_sends(i, j):
        u = y_pair(i, zs[j], x)
        return [remote(u, u, s_far.at[i], r_far.at[i], me.to_x)]

    def fa_wait(i):
        kind, a, b = ITEMS[i]
        arrived(w.at[kind, yn, c, :, :, a:b], r_far.at[i])

    def fa_sends(i):
        kind, a, b = ITEMS[i]
        u = w.at[kind, :, c, :, :, a:b]
        return [remote(u, u, s_core.at[i], r_core.at[i], me.to_core)]

    def complete(i):
        kind, a, b = ITEMS[i]
        arrived(w.at[kind, :, cn, :, :, a:b], r_core.at[i])

    def sa_wait(n):
        if n == 1:
            for j in (1, 2, 3):
                arrived(sb.at[c, x, y, z], rs_small.at[zs[j]])
        if n == 2:
            arrived(sb.at[c, x, y], rs_small.at[4])
        if n == 3:
            arrived(sb.at[c, :, y], rs_small.at[5])

    def sa_sends(n):
        u = (sb.at[c, x, y, z], sb.at[c, x, y], sb.at[c, :, y], sb.at[c])[n]
        if n == 0:
            return [remote(u, u, ss_small.at[j], rs_small.at[z], me.to_z[j]) for j in (1, 3, 2)]
        return [remote(u, u, ss_small.at[3 + n], rs_small.at[3 + n], (me.to_x, me.to_y, me.to_core)[n - 1])]

    def grad(kind):
        return w.at[2] if kind == 0 else g12.at[kind - 1]

    def land(kind):
        return w.at[1] if kind == 0 else rb12.at[kind - 1]

    def pairs(zz):
        return pl.ds(2 * zz, 2)

    def y1(kind, zz):
        return land(kind).at[1, 0, pairs(zz), near]

    def x1(kind, zz):
        return land(kind).at[1, 0, pairs(zz), far]

    def x2(kind, zz):
        return land(kind).at[1, 1, zz, near]

    def y2(kind, zz):
        return land(kind).at[1, 1, zz, far]

    def zb(kind, j):
        return land(kind).at[1, 1, 3 + j]

    def ps_sends(kind, n):
        if kind == 2:
            zz = zx[n]
            return [
                remote(grad(2).at[:, cn, pairs(zz)], land(2).at[0, :, pairs(zz)], t_p.at[2], u_p.at[2, zz], me.to_core)
            ]
        yy = (yn, y)[n]
        return [remote(grad(kind).at[yy, cn], land(kind).at[0, yy], t_p.at[kind], u_p.at[kind, yy], me.to_core)]

    def y1_send(kind, j):
        src = grad(kind).at[yn, c, pairs(zx[j]), near]
        return remote(src, y1(kind, zx[j]), t_1.at[kind], u_y1.at[kind, zx[j]], me.to_y)

    def x1_send(kind, j):
        src = grad(kind).at[:, c, 2 * zx[j] + xn, far]
        return remote(src, x1(kind, zx[j]), t_1.at[kind], u_x1.at[kind, zx[j]], me.to_x)

    def pa_wait(kind, n):
        g = grad(kind)
        if kind == 2:
            zz = zx[n]
            arrived(land(2).at[0, :, pairs(zz)], u_p.at[2, zz])
            g[:, c, pairs(zz)] = g[:, c, pairs(zz)] + land(2)[0, :, pairs(zz)]
            return
        yy = (yn, y)[n]
        arrived(land(kind).at[0, yy], u_p.at[kind, yy])

        def add(i, _):
            d = pl.ds(2 * i, 2)
            g[yy, c, d] = g[yy, c, d] + land(kind)[0, yy, d]
            return 0

        lax.fori_loop(0, 4, add, 0)

    def near_send(kind):
        src = grad(kind).at[yn, c, pairs(zx[3]), near]
        return remote(src, y1(kind, zx[2]), t_1.at[kind], u_e.at[kind], me.to_zx[1])

    def far_send(kind):
        src = grad(kind).at[:, c, 2 * zx[3] + xn, far]
        return remote(src, x1(kind, zx[2]), t_1.at[kind], u_e.at[kind], me.to_zx[1])

    def pa_sends(kind, n):
        if kind == 2:
            return {0: [y1_send(2, 0), x1_send(2, 0)], 1: [y1_send(2, 1), x1_send(2, 1)], 2: [], 3: [near_send(2), far_send(2)]}[n]
        if kind == 1:
            return [(near_send, far_send)[n](1), (y1_send, x1_send)[n](1, 1)]
        return [(y1_send, x1_send)[n](kind, j) for j in ORDER[:AHEAD]]

    def ee_wait(kind):
        arrived(land(kind).at[1, 0, pairs(zx[3])], u_e.at[kind])
        u = grad(kind).at[yn, c, pairs(zx[2]), near]
        u[...] = u[...] + y1(kind, zx[3])[...]
        u = grad(kind).at[:, c, 2 * zx[2] + xn, far]
        u[...] = u[...] + x1(kind, zx[3])[...]

    def ee_sends(kind):
        return [y1_send(kind, 2), x1_send(kind, 2)]

    def later(kind, j, send):
        if kind == 2:
            return []
        if kind == 1:
            return [send(1, 0)] if j == 1 else []
        n = ORDER.index(j) + AHEAD
        return [send(kind, ORDER[n])] if n < 4 else []

    def by_wait(kind, j):
        if kind in PAIRED and j == 3:
            return
        arrived(y1(kind, zx[j]), u_y1.at[kind, zx[j]])
        u = grad(kind).at[y, c, pairs(zx[j]), near]
        u[...] = u[...] + y1(kind, zx[j])[...]

    def by_sends(kind, j):
        src = grad(kind).at[y, c, 2 * zx[j] + xn, near]
        return [
            remote(src, x2(kind, zx[j]), t_2.at[kind], u_2.at[kind, zx[j]], me.to_x)
        ] + later(kind, j, y1_send)

    def bx_wait(kind, j):
        if kind in PAIRED and j == 3:
            return
        arrived(x1(kind, zx[j]), u_x1.at[kind, zx[j]])
        u = grad(kind).at[:, c, 2 * zx[j] + x, far]
        u[...] = u[...] + x1(kind, zx[j])[...]

    def bx_sends(kind, j):
        src = grad(kind).at[yn, c, 2 * zx[j] + x, far]
        return [
            remote(src, y2(kind, zx[j]), t_2.at[kind], u_2.at[kind, zx[j]], me.to_y)
        ] + later(kind, j, x1_send)

    def cz_wait(kind, j):
        arrived(land(kind).at[1, 1, zx[j]], u_2.at[kind, zx[j]])
        u = grad(kind).at[y, c, 2 * zx[j] + x]
        add = land(kind).at[1, 1, zx[j]]
        if j:
            u[...] = u[...] + add[...]
        else:
            o_ref[kind] = u[...].astype(F32) + add[...].astype(F32)

    def cz_sends(kind, j):
        if not j:
            return []
        src = grad(kind).at[y, c, 2 * zx[j] + x]
        return [remote(src, zb(kind, j), t_2.at[kind], u_z.at[kind], me.to_zx[j])]

    def fz_wait(kind):
        arrived(land(kind).at[1, 1, 4:7], u_z.at[kind])
        o_ref[kind] = o_ref[kind] + sum(zb(kind, j)[...].astype(F32) for j in (1, 2, 3))
        save_grads[kind].start()

    save_grads = [pltpu.make_async_copy(o_ref.at[n], o_hbm.at[n], io_sem.at[4 + n]) for n in range(3)]
    save_small = pltpu.make_async_copy(so_ref, so_hbm, io_sem.at[7])

    def sb_wait(n):
        if n == 1:
            arrived(s1, rs_grad.at[4])
            sb[c] = sb[c] + s1[...]
        if n == 2:
            arrived(s2, rs_grad.at[5])
            sb[c, x] = sb[c, x] + s2[...]
        if n == 3:
            arrived(s3, rs_grad.at[6])
            sb[c, x, y] = sb[c, x, y] + s3[...]
        if n == 4:
            total = sb[c, x, y, z]
            for j in (1, 2, 3):
                arrived(s4.at[zs[j]], rs_grad.at[zs[j]])
                total = total + s4[zs[j]]
            so_ref[...] = total
            save_small.start()

    def sb_sends(n):
        if n == 3:
            return [
                remote(sb.at[c, x, y, zs[j]], s4.at[z], ss_grad.at[j], rs_grad.at[z], me.to_z[j]) for j in (1, 3, 2)
            ]
        if n == 4:
            return []
        src, dst = ((sb.at[cn], s1), (sb.at[c, xn], s2), (sb.at[c, x, yn], s3))[n]
        return [remote(src, dst, ss_grad.at[4 + n], rs_grad.at[4 + n], (me.to_core, me.to_x, me.to_y)[n])]

    waits = {
        "o": o_wait, "q": q_wait, "ry": ry_wait, "rx": rx_wait, "fa": fa_wait, "sa": sa_wait,
        "pa": pa_wait, "ee": ee_wait, "by": by_wait, "bx": bx_wait, "cz": cz_wait, "fz": fz_wait, "sb": sb_wait,
    }
    sends = {
        "o": o_sends, "oz": oz_sends, "q": q_sends, "ry": ry_sends, "rx": rx_sends, "fa": fa_sends, "sa": sa_sends,
        "ps": ps_sends, "pa": pa_sends, "ee": ee_sends, "by": by_sends, "bx": bx_sends, "cz": cz_sends, "sb": sb_sends,
    }

    def transfers(steps):
        for name, *args in steps:
            if name == "o":
                for cp in o_sends(*args):
                    cp.start()
            if name in waits:
                waits[name](*args)
            if name in sends and name != "o":
                for cp in sends[name](*args):
                    cp.start()

    def at(name, index=None, part=None):
        if index is None:
            transfers(STEPS.get((name,), ()))
            return
        for n in range(4):
            key = (name, n) if part is None else (name, n, part)
            if key in STEPS:
                pl.when(index == n)(functools.partial(transfers, STEPS[key]))

    def gather_sent():
        for i, (kind, a, b) in enumerate(ITEMS):
            arrived(w.at[kind, y, c, 0:7, :, a:b], s_first.at[i])
            arrived(w.at[kind, y, c, :, :, a:b], s_far.at[i])
            arrived(w.at[kind, :, c, :, :, a:b], s_core.at[i])
        for n in range(4):
            for cp in sa_sends(n):
                cp.wait_send()

    def grads_sent():
        for kind in range(3):
            arrived(grad(kind).at[:, cn], t_p.at[kind])
            arrived(grad(kind).at[y, c], t_1.at[kind])
            arrived(grad(kind).at[y, c, 0:7], t_2.at[kind])
        for n in range(4):
            for cp in sb_sends(n):
                cp.wait_send()

    eye = (iota((96, 96), 0) == iota((96, 96), 1)).astype(F32).astype(BF)
    for cp in loads:
        cp.wait()
    q, k, v = wq_ref[...], wk_ref[...], wv_ref[...]
    own[0, :, 0:128] = q[:, 0:128].astype(BF)
    own[0, :, 128:256] = k[:, 0:128].astype(BF)
    own[0, :, 256:384] = v[:, 0:128].astype(BF)
    own[0, :, 384:512] = jnp.concatenate([q[:, 128:192], v[:, 128:192]], axis=1).astype(BF)
    wo = wo_ref[...].astype(BF)
    o2 = dot(eye, wo[128:192], NT)
    own[0, :, 512:640] = jnp.concatenate([k[:, 128:192], o2], axis=1).astype(BF)
    own[0, :, 640:768] = dot(eye, wo[0:128], NT).astype(BF)
    small[...] = jnp.zeros_like(small)
    for i, ref in enumerate(vector_refs):
        small[i : i + 1, 0:96] = ref[...].astype(BF).astype(F32)
    small[7:10, 0:8] = bq_ref[...].astype(BF).astype(F32)
    small[10:13, 0:8] = bv_ref[...].astype(BF).astype(F32)
    sb[c, x, y, z] = small[...]
    pl.semaphore_wait(bar, len(me.peers))
    at("pack")
    own[1] = w1_ref[...].astype(BF)
    own[2] = w2_ref[...].astype(BF)
    at("mask")

    ends, total = [], jnp.int32(0)
    for i in range(4):
        total = total + lens_ref[me.t, i]
        ends.append(total)
    row, lane = iota((SEQ, 1), 0), iota((1, SEQ), 1)
    seg_q = sum((row >= e).astype(jnp.int32) for e in ends)
    seg_k = sum((lane >= e).astype(jnp.int32) for e in ends)
    valid = row < ends[3]
    same = jnp.where(valid, seg_q, row + 8) == jnp.where(lane < ends[3], seg_k, lane + 8)
    z1_s[:, 0:SEQ] = jnp.where(same, 0.0, NEGATIVE)
    load_c.wait()
    cot_s[...] = jnp.where(valid, cot_s[...].astype(F32), 0.0).astype(BF)
    load_x.wait()
    at("expand")
    arrived(sb.at[c], rs_small.at[6])

    vec_s[...] = jnp.zeros_like(vec_s)
    bqv_s[...] = jnp.zeros_like(bqv_s)

    def expand(d, _):
        vec, head = spread(d)
        zz, xx = lax.div(d, 2), lax.rem(d, 2)
        part = jnp.concatenate([sb[t % 2, xx, t // 2, zz] for t in range(4)], axis=0).astype(BF)
        vec_s[...] += dot(part, vec, NN)
        bqv_s[...] += dot(part, head, NN)
        return 0

    lax.fori_loop(0, 8, expand, 0)
    col = iota((1, D), 1)
    for t in range(4):
        bias = jnp.zeros((1, D), F32)
        for s, start in enumerate(SLOTS):
            keep = (col >= start) & (col < start + 64)
            bias = bias + jnp.where(keep, bqv_s[16 * t + 7 + s : 16 * t + 8 + s], 0.0)
        bqv_s[16 * t : 16 * t + 1] = bias
    bo, c2, g1, b1, g2, b2 = (vec_s[i : i + 1] for i in range(1, 7))

    low = iota((1, 128), 1) < 64
    acc[...] = x_s[...].astype(F32) + bo

    def tile(n):
        return slice(128 * n, 128 * n + 128)

    def half_of(values, upper):
        return jnp.where(low, 0.0, values) if upper else jnp.where(low, values, 0.0)

    def mixed_of(t):
        return jnp.concatenate(
            [half_of(a_s[t, :, tile(4)].astype(F32), 1).astype(BF), a_s[t, :, tile(5)]], axis=1
        )

    def block(kind, yy, cc, cols=slice(None)):
        value = w[kind, yy, cc, :, :, cols]
        return value.reshape(D, value.shape[-1])

    def attend(t, _):
        yy, cc = lax.div(t, 2), lax.rem(t, 2)
        at("att", t, 0)

        @pl.when(t == 0)
        def _():
            for i, item in enumerate(ITEMS):
                if item[0] == 0:
                    complete(i)

        pre = dot(x_s[...], block(0, yy, cc), NN) + bqv_s[pl.ds(pl.multiple_of(16 * t, 16), 1)]
        a_s[t] = pre.astype(BF)
        mix = [None] * 3
        for h, (qt, kt, vt, ot, qu, vu, ou) in enumerate(HEADS):
            at("att", t, h + 1)
            qh = (half_of(a_s[t, :, tile(qt)].astype(F32), qu) * 0.125).astype(BF)
            s = dot(qh, a_s[t, :, tile(kt)], NT) + z1_s[:, 0:SEQ]
            e = jnp.exp(s - jnp.max(s, axis=-1, keepdims=True))
            p = (e / jnp.sum(e, axis=-1, keepdims=True)).astype(BF)
            p_s[t, h] = p
            mix[h] = dot(p, a_s[t, :, tile(vt)], NN)
        a_s[t, :, tile(5)] = jnp.where(low, mix[0], mix[1]).astype(BF)
        a_s[t, :, tile(4)] = jnp.where(low, a_s[t, :, tile(4)].astype(F32), mix[2]).astype(BF)
        acc[...] += dot(mixed_of(t), block(0, yy, cc, slice(512, 768)), NT)
        return 0

    lax.fori_loop(0, 4, attend, 0)

    at("ln1")

    def norm1(i, _):
        rr = pl.ds(pl.multiple_of(i * 256, 256), 256)
        u = acc[rr]
        u = u - jnp.mean(u, axis=-1, keepdims=True)
        rs = lax.rsqrt(jnp.mean(u * u, axis=-1, keepdims=True) + EPS)
        n = u * rs
        z1_s[rr] = n
        rs1_s[rr] = jnp.broadcast_to(rs, (256, 128))
        n = n * g1 + b1
        nl_s[rr] = n.astype(BF)
        acc[rr] = n + c2
        return 0

    lax.fori_loop(0, 2, norm1, 0)

    def up(i, t, _):
        kind, a, b = ITEMS[i]
        at(f"up{a}", t)
        pl.when(t == 0)(functools.partial(complete, i))
        bias = vec_s[pl.ds(pl.multiple_of(16 * t, 16), 1), a:b]
        u = dot(nl_s[...], block(1, lax.div(t, 2), lax.rem(t, 2), slice(a, b)), NN) + bias
        phi = 0.5 + 0.5 * lax.erf(u * 0.7071067811865476)
        act_s[t, :, a:b] = (u * phi).astype(BF)
        gp_s[t, :, a:b] = (phi + u * (0.3989422804014327 * jnp.exp(-0.5 * u * u))).astype(BF)
        return 0

    def down(i, n, _):
        kind, a, b = ITEMS[i]
        at(f"down{a}", n)
        pl.when(n == 0)(functools.partial(complete, i))
        act = jnp.concatenate([act_s[2 * n, :, a:b], act_s[2 * n + 1, :, a:b]], axis=1)
        weight = jnp.concatenate([block(2, n, 0, slice(a, b)), block(2, n, 1, slice(a, b))], axis=1)
        acc[...] += dot(act, weight, NT)
        return 0

    for i, item in enumerate(ITEMS):
        if item[0]:
            lax.fori_loop(0, 6 - 2 * item[0], functools.partial((up, down)[item[0] - 1], i), 0)

    at("ln2")
    gv_s[...] = jnp.zeros_like(gv_s)

    def put(row, value):
        gv_s[0, row : row + 1] += value

    def norm2(i, sums):
        rr = pl.ds(pl.multiple_of(i * 256, 256), 256)
        u = acc[rr]
        u = u - jnp.mean(u, axis=-1, keepdims=True)
        rs = lax.rsqrt(jnp.mean(u * u, axis=-1, keepdims=True) + EPS)
        n = u * rs
        ag_s[rr] = (n * g2 + b2).astype(BF)
        ct = cot_s[rr].astype(F32)
        cg = ct * g2
        cgn = cg * n
        grad = rs * (cg - jnp.mean(cg, axis=-1, keepdims=True) - n * jnp.mean(cgn, axis=-1, keepdims=True))
        acc[rr] = grad
        grad = grad.astype(BF)
        dg_s[rr] = grad
        dgt_s[:, rr] = grad.T
        add = (ct * n, ct, grad.astype(F32))
        return tuple(a + jnp.sum(b, axis=0, keepdims=True) for a, b in zip(sums, add))

    sums = lax.fori_loop(0, 2, norm2, (jnp.zeros((1, D), F32),) * 3)
    for row, value in zip((5, 6, 2), sums):
        put(row, value)
    save_hid = pltpu.make_async_copy(ag_s, hid_hbm, io_sem.at[2])
    save_hid.start()


    def down_grad(n, cc):
        zz = zx[PIECES[n]]
        rr = pl.ds(pl.multiple_of(192 * zz, 64), 192)
        for yy in range(2):
            value = dot(dgt_s[rr], act_s[2 * yy + cc], NN).astype(BF)
            g12[1, yy, cc, pairs(zz)] = value.reshape(2, 96, D)

    for n in range(4):
        transfers(STEPS.get(("dw2", n, 0), ()))
        down_grad(n, cn)
        transfers(STEPS.get(("dw2", n, 1), ()))
        down_grad(n, c)

    def turn(n):
        return jnp.where(n < 2, yn, y), jnp.where(lax.rem(n, 2) == 0, cn, c)

    def up_grad(n, _):
        yy, cc = turn(n)
        t = 2 * yy + cc
        at("dw1", n, 0)
        ig = (dot(dg_s[...], block(2, yy, cc), NN) * gp_s[t].astype(F32)).astype(BF)
        ig_s[...] = ig
        gv_s[t, 0:1] = jnp.sum(ig.astype(F32), axis=0, keepdims=True)
        g12[0, yy, cc] = dot(nl_s[...], ig_s[...], TN).astype(BF).reshape(8, 96, D)
        at("dw1", n, 1)
        acc[...] += dot(ig_s[...], block(1, yy, cc), NT)
        return 0

    lax.fori_loop(0, 4, up_grad, 0)
    gather_sent()
    for peer in me.peers:
        pl.semaphore_signal(ready, inc=1, device_id=peer, device_id_type=MESH)

    at("ln1b")
    save_hid.wait()

    def norm1_back(i, _):
        rr = pl.ds(pl.multiple_of(i * 256, 256), 256)
        n, gr = z1_s[rr], acc[rr]
        put(3, jnp.sum(gr * n, axis=0, keepdims=True))
        put(4, jnp.sum(gr, axis=0, keepdims=True))
        cg = gr * g1
        grad = rs1_s[rr, 0:1] * (
            cg
            - jnp.mean(cg, axis=-1, keepdims=True)
            - n * jnp.mean(cg * n, axis=-1, keepdims=True)
        )
        acc[rr] = grad
        grad = grad.astype(BF)
        ag_s[rr] = grad
        put(1, jnp.sum(grad.astype(F32), axis=0, keepdims=True))
        return 0

    lax.fori_loop(0, 2, norm1_back, 0)

    def attend_back(n, _):
        yy, cc = turn(n)
        t = 2 * yy + cc
        at("dw0", n, 0)
        pl.when(n == 0)(functools.partial(pl.semaphore_wait, ready, len(me.peers)))
        mg = dot(ag_s[...], block(0, yy, cc, slice(512, 768)), NN)
        dq, dk, dv = [None] * 3, [None] * 3, [None] * 3
        for h, (qt, kt, vt, ot, qu, vu, ou) in enumerate(HEADS):
            if h:
                at("dw0", n, h)
            go = half_of(mg[:, 128:256] if ot == 5 else mg[:, 0:128], ou)
            inner = jnp.sum(go * a_s[t, :, tile(ot)].astype(F32), axis=-1, keepdims=True)
            go = go.astype(BF)
            p = p_s[t, h]
            dv[h] = dot(p, go, TN)
            ds = (p.astype(F32) * (dot(go, a_s[t, :, tile(vt)], NT) - inner)).astype(BF)
            dq[h] = dot(ds, a_s[t, :, tile(kt)], NN) * 0.125
            dk[h] = dot(ds, a_s[t, :, tile(qt)], TN) * 0.125
        da_s[:, tile(0)] = jnp.where(low, dq[0], dq[1]).astype(BF)
        da_s[:, tile(1)] = jnp.where(low, dk[0], dk[1]).astype(BF)
        da_s[:, tile(2)] = jnp.where(low, dv[0], dv[1]).astype(BF)
        da_s[:, tile(3)] = jnp.where(low, dq[2], dv[2]).astype(BF)
        da_s[:, tile(4)] = jnp.where(low, dk[2], 0.0).astype(BF)
        at("dw0", n, 3)
        sums = jnp.sum(da_s[...].astype(F32), axis=0, keepdims=True)
        for s, start in enumerate(SLOTS):
            m = start // 128
            gv_s[t, 7 + s : 8 + s, tile(m)] = half_of(sums[:, tile(m)], (start // 64) % 2)
        g0 = w.at[2, yy, cc]
        g0[:, :, 0:512] = dot(x_s[...], da_s[:, 0:512], TN).astype(BF).reshape(8, 96, 512)
        tail = dot(ag_s[...], mixed_of(t), TN)
        mixed = tail[:, 0:128] + dot(x_s[...], da_s[:, tile(4)], TN)
        g0[:, :, 512:640] = mixed.astype(BF).reshape(8, 96, 128)
        g0[:, :, 640:768] = tail[:, 128:256].astype(BF).reshape(8, 96, 128)
        at("dw0", n, 4)
        acc[...] += dot(da_s[...], block(0, yy, cc, slice(0, 640)), NT)
        return 0

    lax.fori_loop(0, 4, attend_back, 0)
    at("gx")
    dg_s[...] = acc[...].astype(BF)
    save_gx = pltpu.make_async_copy(dg_s, gx_hbm, io_sem.at[3])
    save_gx.start()
    at("small")

    for t in range(1, 4):
        gv_s[t, 1:7] = gv_s[0, 1:7]

    def collect(d, _):
        vec, head = spread(d)
        zz, xx = lax.div(d, 2), lax.rem(d, 2)
        val = gv_s[...].reshape(64, D)
        high = val.astype(BF)
        rest = (val - high.astype(F32)).astype(BF)
        is_vec = (iota((64, 1), 0) & 15) < 7
        got = jnp.where(is_vec, dot(high, vec, NT) + dot(rest, vec, NT), dot(high, head, NT) + dot(rest, head, NT))
        for t in range(4):
            sb[t % 2, xx, t // 2, zz] = got[16 * t : 16 * t + 16]
        return 0

    lax.fori_loop(0, 8, collect, 0)
    at("tail")
    grads_sent()
    for cp in [save_gx, save_small] + save_grads:
        cp.wait()


def run(r, *args):
    hbm, sm = pl.BlockSpec(memory_space=pl.ANY), pl.BlockSpec(memory_space=pltpu.SMEM)
    t = (SEQ, D)
    V = pltpu.VMEM
    items = len(ITEMS)
    gather = [DMA((items,))] * 3 + [DMA((items, 4))] * 3 + [DMA((items,))] * 2
    back = [DMA((3,))] * 3 + [DMA((3, 4))] * 4 + [DMA((3,))] * 2
    blocks = (2, 2, 8, 96, D)
    return pl.pallas_call(
        functools.partial(kernel, r),
        out_shape=(
            jax.ShapeDtypeStruct(t, BF),
            jax.ShapeDtypeStruct(t, BF),
            jax.ShapeDtypeStruct((3, 96, D), F32),
            jax.ShapeDtypeStruct((16, 128), F32),
        ),
        in_specs=[sm] + [hbm] * 17,
        out_specs=(hbm,) * 4,
        scratch_shapes=[V(i.shape, i.dtype) for i in args[3:]]
        + [DMA((15,)), V((3, 96, D), F32), V((16, 128), F32)]
        + [
            V((3, 96, D), BF), V((3,) + blocks, BF), V((2,) + blocks, BF), V((2,) + blocks, BF),
            V((16, 128), F32), V((2, 2, 2, 4, 16, 128), F32), V((64, D), F32), V((64, D), F32),
            V((4,) + t, BF), V((4, 3, SEQ, SEQ), BF), V(t, F32), V((SEQ, 128), F32), V(t, F32),
            V((4,) + t, BF), V((4,) + t, BF), V(t, BF),
            V(t, BF), V(t, BF), V(t, BF), V((D, SEQ), BF), V(t, BF), V(t, BF), V((SEQ, 640), BF), V((4, 16, D), F32),
            V((2, 2, 4, 16, 128), F32), V((2, 4, 16, 128), F32), V((4, 16, 128), F32), V((4, 16, 128), F32),
            DMA((8,)), DMA((1,)), *gather, DMA((7,)), DMA((7,)),
            *back, DMA((7,)), DMA((7,)), pltpu.SemaphoreType.REGULAR,
        ],
        compiler_params=pltpu.CompilerParams(
            collective_id=0, has_side_effects=True, vmem_limit_bytes=67043328
        ),
    )(*args)


FINAL = ((96, 192),) * 3 + ((192, 96), (96, D), (96, D), (3, 8), (3, 8)) + ((1, 96),) * 7


def finish_kernel(hid_hbm, gx_hbm, g_hbm, s_hbm, *refs):
    outs, scratch, sem = refs[:17], refs[17:-1], refs[-1]
    hid, gx, g, s = scratch[:4]
    wq, wk, wv, wo, w1, w2, bq, bv, *vectors = scratch[4:]

    def copy(n, src, dst):
        cp = pltpu.make_async_copy(src, dst, sem.at[n])
        cp.start()
        return cp

    get_g, get_s = copy(0, g_hbm, g), copy(1, s_hbm, s)
    get_hid, get_gx = copy(2, hid_hbm, hid), copy(3, gx_hbm, gx)
    get_g.wait()
    out = [copy(8, g.at[1], outs[6]), copy(9, g.at[2], outs[7])]
    a = g[0]
    for n, ref in enumerate((wq, wk, wv)):
        ref[:, 0:128] = a[:, 128 * n : 128 * n + 128]
    wq[:, 128:192] = a[:, 384:448]
    wk[:, 128:192] = a[:, 512:576]
    wv[:, 128:192] = a[:, 448:512]
    out += [copy(10 + n, ref, outs[2 + n]) for n, ref in enumerate((wq, wk, wv))]
    get_hid.wait()
    out.append(copy(4, hid, outs[0]))
    get_gx.wait()
    out.append(copy(5, gx, outs[1]))
    eye = (iota((96, 96), 0) == iota((96, 96), 1)).astype(F32)
    turned = lax.dot_general(
        a[:, 512:768], eye, (TN, ((), ())), preferred_element_type=F32, precision=lax.Precision.HIGHEST
    )
    wo[0:128] = turned[128:256]
    wo[128:192] = turned[64:128]
    out.append(copy(6, wo, outs[5]))
    get_s.wait()
    bq[...] = s[7:10, 0:8]
    bv[...] = s[10:13, 0:8]
    for n, ref in enumerate(vectors):
        ref[...] = s[n : n + 1, 0:96]
    out += [copy(13 + n, ref, outs[8 + n]) for n, ref in enumerate((bq, bv, *vectors))]
    for cp in out:
        cp.wait()


def finish(hidden, gx, grads, small):
    tokens = jax.ShapeDtypeStruct((SEQ, D), BF)
    hbm = pl.BlockSpec(memory_space=pl.ANY)
    out = pl.pallas_call(
        finish_kernel,
        out_shape=[tokens, tokens] + [jax.ShapeDtypeStruct(s, F32) for s in FINAL],
        in_specs=[hbm] * 4,
        out_specs=[hbm] * 17,
        scratch_shapes=[pltpu.VMEM((SEQ, D), BF)] * 2
        + [pltpu.VMEM((3, 96, D), F32), pltpu.VMEM((16, 128), F32)]
        + [pltpu.VMEM(s, F32) for s in FINAL]
        + [DMA((22,))],
    )(hidden, gx, grads, small)
    out = list(out)
    return out[:7] + [out[7].T] + out[8:11] + [i.reshape(96) for i in out[11:]]


def body(
    hidden_in, seq_lengths, out_grad, query_weight, key_weight, value_weight, output_weight, up_weight,
    down_weight, query_bias, value_bias, inner_bias, output_bias, down_bias, first_gain, first_shift,
    second_gain, second_shift,
):
    r = lax.axis_size("dp") // 8
    groups = [[g * r + i for i in range(r)] for g in range(8)]

    def whole(value, axis):
        if r == 1:
            return value
        value = value.astype(BF)
        return lax.all_gather(value, "dp", axis=axis, tiled=True, axis_index_groups=groups).astype(F32)

    def shard(value, axis):
        if r == 1:
            return value
        return lax.psum_scatter(value, "dp", scatter_dimension=axis, tiled=True, axis_index_groups=groups)

    vectors = (output_bias, down_bias, first_gain, first_shift, second_gain, second_shift)
    hidden, gx, gw, gs = run(
        r, seq_lengths, hidden_in, out_grad,
        whole(query_weight, 0), whole(key_weight, 0), whole(value_weight, 0), whole(output_weight, 1),
        whole(up_weight, 0), whole(down_weight.T, 0),
        whole(query_bias, 1), whole(value_bias, 1), whole(inner_bias, 1),
        *(whole(i.reshape(1, -1), 1) for i in vectors),
    )
    if r == 1:
        return tuple(finish(hidden, gx, gw, gs))
    gw = shard(gw, 1)
    gv = shard(gs[0:7, 0:96], 1)
    gh = shard(gs[7:13, 0:8], 1)
    a = gw[0]
    return (
        hidden,
        gx,
        jnp.concatenate([a[:, 0:128], a[:, 384:448]], axis=1),
        jnp.concatenate([a[:, 128:256], a[:, 512:576]], axis=1),
        jnp.concatenate([a[:, 256:384], a[:, 448:512]], axis=1),
        jnp.concatenate([a[:, 640:768], a[:, 576:640]], axis=1).T,
        gw[1],
        gw[2].T,
        gh[0:3],
        gh[3:6],
        gv[0:1],
        *(gv[i] for i in range(1, 7)),
    )


def solution(mesh):
    both, dp = P(("dp", "tensor"), None), P("dp")
    rows_first, columns_first = P("dp", "tensor"), P("tensor", "dp")
    weights = (rows_first,) * 3 + (columns_first, rows_first, columns_first)
    smalls = (columns_first,) * 3 + (dp,) * 6
    return jax.shard_map(
        body,
        mesh=mesh,
        in_specs=(P("dp", None),) * 3 + weights + smalls,
        out_specs=(both, both) + weights + smalls,
        check_vma=False,
    )
```

```python
import functools

import jax
import jax.numpy as jnp
from jax import lax
from jax.experimental import pallas as pl
from jax.experimental.pallas import tpu as pltpu
from jax.sharding import PartitionSpec as P

SEQ = 512
D = 768
EPS = 1e-12
NEGATIVE = -1000000000.0
MESH = pl.DeviceIdType.MESH
BF = jnp.bfloat16
F32 = jnp.float32
DMA = pltpu.SemaphoreType.DMA
NN, NT, TN = ((1,), (0,)), ((1,), (1,)), ((0,), (0,))
HEADS = ((0, 1, 2, 5, 0, 0, 0), (0, 1, 2, 5, 1, 1, 1), (3, 4, 3, 4, 0, 1, 1))
SLOTS = (0, 64, 384, 256, 320, 448)
ITEMS = ((0, 0, 768), (1, 0, 768), (2, 0, 512), (2, 512, 768))
PIECES = (3, 2, 1, 0)
ORDER = (2, 3, 1, 0)
AHEAD = 1
PAIRED = (1, 2)
STEPS = {
    ("pack",): (("sa", 0), ("o", 0), ("oz", 0)),
    ("mask",): (("o", 1), ("o", 2), ("o", 3)),
    ("expand",): (("ry", 0, 0), ("sa", 1), ("rx", 0, 0), ("rx", 1, 0), ("ry", 2, 0), ("ry", 1, 0), ("q", 0, 3),
        ("rx", 3, 0), ("rx", 2, 0), ("q", 0, 1), ("q", 0, 2), ("oz", 1), ("oz", 2), ("sa", 2), ("ry", 0, 3),
        ("rx", 0, 1), ("rx", 0, 3), ("rx", 0, 2), ("ry", 0, 1), ("sa", 3), ("ry", 3, 0), ("ry", 0, 2)),
    ("att", 0, 0): (("q", 1, 3), ("q", 1, 1), ("q", 1, 2), ("ry", 1, 3), ("fa", 0), ("rx", 1, 3), ("ry", 1, 1),
        ("rx", 1, 1), ("q", 2, 3), ("rx", 1, 2)),
    ("att", 0, 1): (("oz", 3),),
    ("att", 0, 3): (("ry", 1, 2),),
    ("att", 1, 2): (("q", 2, 1),),
    ("att", 1, 3): (("q", 2, 2),),
    ("att", 2, 0): (("ry", 2, 3), ("rx", 2, 3)),
    ("att", 2, 2): (("q", 3, 1),),
    ("att", 3, 0): (("q", 3, 2), ("q", 3, 3), ("fa", 1)),
    ("att", 3, 2): (("ry", 2, 2), ("rx", 2, 2)),
    ("ln1",): (("ry", 2, 1), ("rx", 2, 1)),
    ("up0", 0): (("rx", 3, 2), ("rx", 3, 1)),
    ("up0", 1): (("ry", 3, 3), ("ry", 3, 1), ("rx", 3, 3)),
    ("up0", 2): (("ry", 3, 2), ("fa", 2)),
    ("down0", 0): (("fa", 3),),
    ("dw2", 0, 1): (("ps", 2, 3),),
    ("dw2", 2, 1): (("pa", 2, 3), ("ps", 2, 1), ("bx", 2, 3)),
    ("dw2", 3, 1): (("ps", 2, 0), ("by", 2, 3)),
    ("dw1", 0, 0): (("pa", 2, 1),),
    ("dw1", 0, 1): (("ps", 1, 0),),
    ("dw1", 1, 0): (("pa", 2, 0), ("ps", 2, 2)),
    ("dw1", 2, 0): (("pa", 1, 0), ("cz", 2, 3)),
    ("dw1", 3, 0): (("pa", 2, 2), ("ps", 1, 1), ("ee", 2), ("by", 2, 1)),
    ("dw0", 0, 0): (("pa", 1, 1), ("bx", 2, 1), ("bx", 1, 3)),
    ("dw0", 0, 3): (("by", 1, 3),),
    ("dw0", 1, 0): (("by", 2, 0), ("bx", 2, 2)),
    ("dw0", 1, 1): (("ps", 0, 0), ("by", 2, 2), ("by", 1, 1)),
    ("dw0", 1, 4): (("cz", 2, 1), ("ee", 1)),
    ("dw0", 2, 0): (("cz", 1, 3),),
    ("dw0", 2, 2): (("bx", 2, 0),),
    ("dw0", 2, 3): (("bx", 1, 1),),
    ("dw0", 2, 4): (("ps", 0, 1), ("pa", 0, 0), ("cz", 2, 2)),
    ("dw0", 3, 1): (("bx", 1, 2), ("by", 1, 0), ("by", 1, 2)),
    ("dw0", 3, 4): (("pa", 0, 1),),
    ("small",): (("cz", 1, 1), ("cz", 2, 0)),
    ("tail",): (("by", 0, 2), ("cz", 1, 2), ("sb", 0), ("sb", 1), ("bx", 0, 2), ("bx", 1, 0), ("by", 0, 3),
        ("cz", 0, 2), ("sb", 2), ("bx", 0, 3), ("by", 0, 1), ("cz", 1, 0), ("fz", 1), ("sb", 3), ("cz", 0, 3),
        ("bx", 0, 1), ("fz", 2), ("sb", 4), ("by", 0, 0), ("cz", 0, 1), ("bx", 0, 0), ("cz", 0, 0), ("fz", 0)),
}


def dot(a, b, dims):
    return lax.dot_general(a, b, (dims, ((), ())), preferred_element_type=F32)


def iota(shape, axis):
    return lax.broadcasted_iota(jnp.int32, shape, axis)


class Place:
    def __init__(self, r):
        dp = lax.axis_index("dp")
        t = lax.axis_index("tensor")
        g = lax.div(dp, r)
        self.r, self.q, self.t = r, lax.rem(dp, r), t
        self.z, self.x = lax.div(g, 2), lax.rem(g, 2)
        self.y, self.c = lax.div(t, 2), lax.rem(t, 2)
        self.xn, self.yn, self.cn = 1 - self.x, 1 - self.y, 1 - self.c
        self.zs = [lax.rem(self.z + i, 4) for i in range(4)]
        self.to_x = self.dev(self.z, self.xn, self.y, self.c)
        self.to_y = self.dev(self.z, self.x, self.yn, self.c)
        self.to_core = self.dev(self.z, self.x, self.y, self.cn)
        self.to_z = [self.dev(self.zs[i], self.x, self.y, self.c) for i in range(4)]
        self.zx = [self.z, self.z + 1 - 2 * lax.rem(self.z, 2), self.zs[2], 3 - self.z]
        self.to_zx = [self.dev(i, self.x, self.y, self.c) for i in self.zx]
        self.peers = self.to_z[1:] + [self.to_x, self.to_y, self.to_core]

    def dev(self, z, x, y, c):
        return {"dp": (2 * z + x) * self.r + self.q, "tensor": 2 * y + c}


def remote(src, dst, ss, rs, to):
    return pltpu.make_async_remote_copy(
        src_ref=src, dst_ref=dst, send_sem=ss, recv_sem=rs, device_id=to, device_id_type=MESH
    )


def arrived(ref, sem):
    pltpu.make_async_copy(ref, ref, sem).wait()


def spread(d):
    lane, col = iota((128, D), 0), iota((128, D), 1)
    vec = (col == lane + 96 * d) & (lane < 96)
    head = ((col & 63) == lane + 8 * d) & (lane < 8)
    return vec.astype(F32).astype(BF), head.astype(F32).astype(BF)


def kernel(
    r,
    lens_ref, x_hbm, cot_hbm, *refs,
):
    shards_hbm, (hid_hbm, gx_hbm, o_hbm, so_hbm), refs = refs[:15], refs[15:19], refs[19:]
    shards, (load_sem, o_ref, so_ref, *refs) = refs[:15], refs[15:]
    work(
        r, lens_ref, x_hbm, cot_hbm, shards_hbm, shards, load_sem, hid_hbm, gx_hbm, o_hbm, so_hbm, o_ref, so_ref, *refs
    )


def work(
    r, lens_ref, x_hbm, cot_hbm, shards_hbm, shards, load_sem, hid_hbm, gx_hbm, o_hbm, so_hbm, o_ref, so_ref,
    own, w, g12, rb12, small, sb, vec_s, bqv_s, a_s, p_s, z1_s, rs1_s, acc, act_s, gp_s, nl_s,
    x_s, cot_s, dg_s, dgt_s, ig_s, ag_s, da_s, gv_s, s1, s2, s3, s4,
    io_sem, own_sem, s_first, s_far, s_core, r_z, r_x, r_y, r_far, r_core, ss_small, rs_small,
    t_p, t_1, t_2, u_p, u_y1, u_x1, u_2, u_z, u_e, ss_grad, rs_grad, ready,
):
    me = Place(r)
    z, x, y, c, xn, yn, cn, zs, zx = me.z, me.x, me.y, me.c, me.xn, me.yn, me.cn, me.zs, me.zx
    bar = pltpu.get_barrier_semaphore()
    for peer in me.peers:
        pl.semaphore_signal(bar, inc=1, device_id=peer, device_id_type=MESH)
    mine = pl.ds(pl.multiple_of(me.t * SEQ, SEQ), SEQ)
    load_x = pltpu.make_async_copy(x_hbm.at[mine], x_s, io_sem.at[0])
    load_c = pltpu.make_async_copy(cot_hbm.at[mine], cot_s, io_sem.at[1])
    loads = [pltpu.make_async_copy(a, b, load_sem.at[i]) for i, (a, b) in enumerate(zip(shards_hbm, shards))]
    for cp in loads:
        cp.start()
    load_x.start()
    load_c.start()
    wq_ref, wk_ref, wv_ref, wo_ref, w1_ref, w2_ref, bq_ref, bv_ref, *vector_refs = shards

    near, far = slice(0, 48), slice(48, 96)

    def piece(i, zz, xx, yy, rr=slice(None)):
        kind, a, b = ITEMS[i]
        return w.at[kind, yy, c, 2 * zz + xx, rr, a:b]

    def x_pair(i, zz, yy):
        kind, a, b = ITEMS[i]
        return w.at[kind, yy, c, pl.ds(2 * zz, 2), near, a:b]

    def y_pair(i, zz, xx):
        kind, a, b = ITEMS[i]
        return w.at[kind, :, c, 2 * zz + xx, far, a:b]

    def o_sends(i):
        kind, a, b = ITEMS[i]
        return [
            remote(own.at[kind, near, a:b], piece(i, z, x, y, near), s_first.at[i], r_x.at[i, z], me.to_x),
            remote(own.at[kind, far, a:b], piece(i, z, x, y, far), s_first.at[i], r_y.at[i, z], me.to_y),
        ]

    def o_wait(i):
        kind, a, b = ITEMS[i]
        cp = pltpu.make_async_copy(own.at[kind, :, a:b], piece(i, z, x, y), own_sem.at[0])
        cp.start()
        cp.wait()

    def oz_sends(i):
        kind, a, b = ITEMS[i]
        src, dst = own.at[kind, :, a:b], piece(i, z, x, y)
        return [remote(src, dst, s_first.at[i], r_z.at[i, z], me.to_z[j]) for j in (1, 3, 2)]

    def q_wait(i, j):
        arrived(piece(i, zs[j], x, y), r_z.at[i, zs[j]])

    def q_sends(i, j):
        a, b = piece(i, zs[j], x, y, near), piece(i, zs[j], x, y, far)
        return [
            remote(a, a, s_first.at[i], r_x.at[i, zs[j]], me.to_x),
            remote(b, b, s_first.at[i], r_y.at[i, zs[j]], me.to_y),
        ]

    def ry_wait(i, j):
        arrived(piece(i, zs[j], xn, y, near), r_x.at[i, zs[j]])

    def ry_sends(i, j):
        u = x_pair(i, zs[j], y)
        return [remote(u, u, s_far.at[i], r_far.at[i], me.to_y)]

    def rx_wait(i, j):
        arrived(piece(i, zs[j], x, yn, far), r_y.at[i, zs[j]])

    def rx_sends(i, j):
        u = y_pair(i, zs[j], x)
        return [remote(u, u, s_far.at[i], r_far.at[i], me.to_x)]

    def fa_wait(i):
        kind, a, b = ITEMS[i]
        arrived(w.at[kind, yn, c, :, :, a:b], r_far.at[i])

    def fa_sends(i):
        kind, a, b = ITEMS[i]
        u = w.at[kind, :, c, :, :, a:b]
        return [remote(u, u, s_core.at[i], r_core.at[i], me.to_core)]

    def complete(i):
        kind, a, b = ITEMS[i]
        arrived(w.at[kind, :, cn, :, :, a:b], r_core.at[i])

    def sa_wait(n):
        if n == 1:
            for j in (1, 2, 3):
                arrived(sb.at[c, x, y, z], rs_small.at[zs[j]])
        if n == 2:
            arrived(sb.at[c, x, y], rs_small.at[4])
        if n == 3:
            arrived(sb.at[c, :, y], rs_small.at[5])

    def sa_sends(n):
        u = (sb.at[c, x, y, z], sb.at[c, x, y], sb.at[c, :, y], sb.at[c])[n]
        if n == 0:
            return [remote(u, u, ss_small.at[j], rs_small.at[z], me.to_z[j]) for j in (1, 3, 2)]
        return [remote(u, u, ss_small.at[3 + n], rs_small.at[3 + n], (me.to_x, me.to_y, me.to_core)[n - 1])]

    def grad(kind):
        return w.at[2] if kind == 0 else g12.at[kind - 1]

    def land(kind):
        return w.at[1] if kind == 0 else rb12.at[kind - 1]

    def pairs(zz):
        return pl.ds(2 * zz, 2)

    def y1(kind, zz):
        return land(kind).at[1, 0, pairs(zz), near]

    def x1(kind, zz):
        return land(kind).at[1, 0, pairs(zz), far]

    def x2(kind, zz):
        return land(kind).at[1, 1, zz, near]

    def y2(kind, zz):
        return land(kind).at[1, 1, zz, far]

    def zb(kind, j):
        return land(kind).at[1, 1, 3 + j]

    def ps_sends(kind, n):
        if kind == 2:
            zz = zx[n]
            return [
                remote(grad(2).at[:, cn, pairs(zz)], land(2).at[0, :, pairs(zz)], t_p.at[2], u_p.at[2, zz], me.to_core)
            ]
        yy = (yn, y)[n]
        return [remote(grad(kind).at[yy, cn], land(kind).at[0, yy], t_p.at[kind], u_p.at[kind, yy], me.to_core)]

    def y1_send(kind, j):
        src = grad(kind).at[yn, c, pairs(zx[j]), near]
        return remote(src, y1(kind, zx[j]), t_1.at[kind], u_y1.at[kind, zx[j]], me.to_y)

    def x1_send(kind, j):
        src = grad(kind).at[:, c, 2 * zx[j] + xn, far]
        return remote(src, x1(kind, zx[j]), t_1.at[kind], u_x1.at[kind, zx[j]], me.to_x)

    def pa_wait(kind, n):
        g = grad(kind)
        if kind == 2:
            zz = zx[n]
            arrived(land(2).at[0, :, pairs(zz)], u_p.at[2, zz])
            g[:, c, pairs(zz)] = g[:, c, pairs(zz)] + land(2)[0, :, pairs(zz)]
            return
        yy = (yn, y)[n]
        arrived(land(kind).at[0, yy], u_p.at[kind, yy])

        def add(i, _):
            d = pl.ds(2 * i, 2)
            g[yy, c, d] = g[yy, c, d] + land(kind)[0, yy, d]
            return 0

        lax.fori_loop(0, 4, add, 0)

    def near_send(kind):
        src = grad(kind).at[yn, c, pairs(zx[3]), near]
        return remote(src, y1(kind, zx[2]), t_1.at[kind], u_e.at[kind], me.to_zx[1])

    def far_send(kind):
        src = grad(kind).at[:, c, 2 * zx[3] + xn, far]
        return remote(src, x1(kind, zx[2]), t_1.at[kind], u_e.at[kind], me.to_zx[1])

    def pa_sends(kind, n):
        if kind == 2:
            return {0: [y1_send(2, 0), x1_send(2, 0)], 1: [y1_send(2, 1), x1_send(2, 1)], 2: [], 3: [near_send(2), far_send(2)]}[n]
        if kind == 1:
            return [(near_send, far_send)[n](1), (y1_send, x1_send)[n](1, 1)]
        return [(y1_send, x1_send)[n](kind, j) for j in ORDER[:AHEAD]]

    def ee_wait(kind):
        arrived(land(kind).at[1, 0, pairs(zx[3])], u_e.at[kind])
        u = grad(kind).at[yn, c, pairs(zx[2]), near]
        u[...] = u[...] + y1(kind, zx[3])[...]
        u = grad(kind).at[:, c, 2 * zx[2] + xn, far]
        u[...] = u[...] + x1(kind, zx[3])[...]

    def ee_sends(kind):
        return [y1_send(kind, 2), x1_send(kind, 2)]

    def later(kind, j, send):
        if kind == 2:
            return []
        if kind == 1:
            return [send(1, 0)] if j == 1 else []
        n = ORDER.index(j) + AHEAD
        return [send(kind, ORDER[n])] if n < 4 else []

    def by_wait(kind, j):
        if kind in PAIRED and j == 3:
            return
        arrived(y1(kind, zx[j]), u_y1.at[kind, zx[j]])
        u = grad(kind).at[y, c, pairs(zx[j]), near]
        u[...] = u[...] + y1(kind, zx[j])[...]

    def by_sends(kind, j):
        src = grad(kind).at[y, c, 2 * zx[j] + xn, near]
        return [
            remote(src, x2(kind, zx[j]), t_2.at[kind], u_2.at[kind, zx[j]], me.to_x)
        ] + later(kind, j, y1_send)

    def bx_wait(kind, j):
        if kind in PAIRED and j == 3:
            return
        arrived(x1(kind, zx[j]), u_x1.at[kind, zx[j]])
        u = grad(kind).at[:, c, 2 * zx[j] + x, far]
        u[...] = u[...] + x1(kind, zx[j])[...]

    def bx_sends(kind, j):
        src = grad(kind).at[yn, c, 2 * zx[j] + x, far]
        return [
            remote(src, y2(kind, zx[j]), t_2.at[kind], u_2.at[kind, zx[j]], me.to_y)
        ] + later(kind, j, x1_send)

    def cz_wait(kind, j):
        arrived(land(kind).at[1, 1, zx[j]], u_2.at[kind, zx[j]])
        u = grad(kind).at[y, c, 2 * zx[j] + x]
        add = land(kind).at[1, 1, zx[j]]
        if j:
            u[...] = u[...] + add[...]
        else:
            o_ref[kind] = u[...].astype(F32) + add[...].astype(F32)

    def cz_sends(kind, j):
        if not j:
            return []
        src = grad(kind).at[y, c, 2 * zx[j] + x]
        return [remote(src, zb(kind, j), t_2.at[kind], u_z.at[kind], me.to_zx[j])]

    def fz_wait(kind):
        arrived(land(kind).at[1, 1, 4:7], u_z.at[kind])
        o_ref[kind] = o_ref[kind] + sum(zb(kind, j)[...].astype(F32) for j in (1, 2, 3))
        save_grads[kind].start()

    save_grads = [pltpu.make_async_copy(o_ref.at[n], o_hbm.at[n], io_sem.at[4 + n]) for n in range(3)]
    save_small = pltpu.make_async_copy(so_ref, so_hbm, io_sem.at[7])

    def sb_wait(n):
        if n == 1:
            arrived(s1, rs_grad.at[4])
            sb[c] = sb[c] + s1[...]
        if n == 2:
            arrived(s2, rs_grad.at[5])
            sb[c, x] = sb[c, x] + s2[...]
        if n == 3:
            arrived(s3, rs_grad.at[6])
            sb[c, x, y] = sb[c, x, y] + s3[...]
        if n == 4:
            total = sb[c, x, y, z]
            for j in (1, 2, 3):
                arrived(s4.at[zs[j]], rs_grad.at[zs[j]])
                total = total + s4[zs[j]]
            so_ref[...] = total
            save_small.start()

    def sb_sends(n):
        if n == 3:
            return [
                remote(sb.at[c, x, y, zs[j]], s4.at[z], ss_grad.at[j], rs_grad.at[z], me.to_z[j]) for j in (1, 3, 2)
            ]
        if n == 4:
            return []
        src, dst = ((sb.at[cn], s1), (sb.at[c, xn], s2), (sb.at[c, x, yn], s3))[n]
        return [remote(src, dst, ss_grad.at[4 + n], rs_grad.at[4 + n], (me.to_core, me.to_x, me.to_y)[n])]

    waits = {
        "o": o_wait, "q": q_wait, "ry": ry_wait, "rx": rx_wait, "fa": fa_wait, "sa": sa_wait,
        "pa": pa_wait, "ee": ee_wait, "by": by_wait, "bx": bx_wait, "cz": cz_wait, "fz": fz_wait, "sb": sb_wait,
    }
    sends = {
        "o": o_sends, "oz": oz_sends, "q": q_sends, "ry": ry_sends, "rx": rx_sends, "fa": fa_sends, "sa": sa_sends,
        "ps": ps_sends, "pa": pa_sends, "ee": ee_sends, "by": by_sends, "bx": bx_sends, "cz": cz_sends, "sb": sb_sends,
    }

    def transfers(steps):
        for name, *args in steps:
            if name == "o":
                for cp in o_sends(*args):
                    cp.start()
            if name in waits:
                waits[name](*args)
            if name in sends and name != "o":
                for cp in sends[name](*args):
                    cp.start()

    def at(name, index=None, part=None):
        if index is None:
            transfers(STEPS.get((name,), ()))
            return
        for n in range(4):
            key = (name, n) if part is None else (name, n, part)
            if key in STEPS:
                pl.when(index == n)(functools.partial(transfers, STEPS[key]))

    def gather_sent():
        for i, (kind, a, b) in enumerate(ITEMS):
            arrived(w.at[kind, y, c, 0:7, :, a:b], s_first.at[i])
            arrived(w.at[kind, y, c, :, :, a:b], s_far.at[i])
            arrived(w.at[kind, :, c, :, :, a:b], s_core.at[i])
        for n in range(4):
            for cp in sa_sends(n):
                cp.wait_send()

    def grads_sent():
        for kind in range(3):
            arrived(grad(kind).at[:, cn], t_p.at[kind])
            arrived(grad(kind).at[y, c], t_1.at[kind])
            arrived(grad(kind).at[y, c, 0:7], t_2.at[kind])
        for n in range(4):
            for cp in sb_sends(n):
                cp.wait_send()

    eye = (iota((96, 96), 0) == iota((96, 96), 1)).astype(F32).astype(BF)
    for cp in loads:
        cp.wait()
    q, k, v = wq_ref[...], wk_ref[...], wv_ref[...]
    own[0, :, 0:128] = q[:, 0:128].astype(BF)
    own[0, :, 128:256] = k[:, 0:128].astype(BF)
    own[0, :, 256:384] = v[:, 0:128].astype(BF)
    own[0, :, 384:512] = jnp.concatenate([q[:, 128:192], v[:, 128:192]], axis=1).astype(BF)
    wo = wo_ref[...].astype(BF)
    o2 = dot(eye, wo[128:192], NT)
    own[0, :, 512:640] = jnp.concatenate([k[:, 128:192], o2], axis=1).astype(BF)
    own[0, :, 640:768] = dot(eye, wo[0:128], NT).astype(BF)
    small[...] = jnp.zeros_like(small)
    for i, ref in enumerate(vector_refs):
        small[i : i + 1, 0:96] = ref[...].astype(BF).astype(F32)
    small[7:10, 0:8] = bq_ref[...].astype(BF).astype(F32)
    small[10:13, 0:8] = bv_ref[...].astype(BF).astype(F32)
    sb[c, x, y, z] = small[...]
    pl.semaphore_wait(bar, len(me.peers))
    at("pack")
    own[1] = w1_ref[...].astype(BF)
    own[2] = w2_ref[...].astype(BF)
    at("mask")

    ends, total = [], jnp.int32(0)
    for i in range(4):
        total = total + lens_ref[me.t, i]
        ends.append(total)
    row, lane = iota((SEQ, 1), 0), iota((1, SEQ), 1)
    seg_q = sum((row >= e).astype(jnp.int32) for e in ends)
    seg_k = sum((lane >= e).astype(jnp.int32) for e in ends)
    valid = row < ends[3]
    same = jnp.where(valid, seg_q, row + 8) == jnp.where(lane < ends[3], seg_k, lane + 8)
    z1_s[:, 0:SEQ] = jnp.where(same, 0.0, NEGATIVE)
    load_c.wait()
    cot_s[...] = jnp.where(valid, cot_s[...].astype(F32), 0.0).astype(BF)
    load_x.wait()
    at("expand")
    arrived(sb.at[c], rs_small.at[6])

    vec_s[...] = jnp.zeros_like(vec_s)
    bqv_s[...] = jnp.zeros_like(bqv_s)

    def expand(d, _):
        vec, head = spread(d)
        zz, xx = lax.div(d, 2), lax.rem(d, 2)
        part = jnp.concatenate([sb[t % 2, xx, t // 2, zz] for t in range(4)], axis=0).astype(BF)
        vec_s[...] += dot(part, vec, NN)
        bqv_s[...] += dot(part, head, NN)
        return 0

    lax.fori_loop(0, 8, expand, 0)
    col = iota((1, D), 1)
    for t in range(4):
        bias = jnp.zeros((1, D), F32)
        for s, start in enumerate(SLOTS):
            keep = (col >= start) & (col < start + 64)
            bias = bias + jnp.where(keep, bqv_s[16 * t + 7 + s : 16 * t + 8 + s], 0.0)
        bqv_s[16 * t : 16 * t + 1] = bias
    bo, c2, g1, b1, g2, b2 = (vec_s[i : i + 1] for i in range(1, 7))

    def cot_sums(i, total):
        rr = pl.ds(pl.multiple_of(i * 256, 256), 256)
        ct = cot_s[rr].astype(F32)
        rs1_s[rr, 64:128] = jnp.broadcast_to(jnp.mean(ct * g2, axis=-1, keepdims=True), (256, 64))
        return total + jnp.sum(ct, axis=0, keepdims=True)

    gv_s[...] = jnp.zeros_like(gv_s)
    gv_s[0, 6:7] = lax.fori_loop(0, 2, cot_sums, jnp.zeros((1, D), F32))

    low = iota((1, 128), 1) < 64
    acc[...] = x_s[...].astype(F32) + bo

    def tile(n):
        return slice(128 * n, 128 * n + 128)

    def half_of(values, upper):
        return jnp.where(low, 0.0, values) if upper else jnp.where(low, values, 0.0)

    def mixed_of(t):
        return jnp.concatenate(
            [half_of(a_s[t, :, tile(4)].astype(F32), 1).astype(BF), a_s[t, :, tile(5)]], axis=1
        )

    def block(kind, yy, cc, cols=slice(None)):
        value = w[kind, yy, cc, :, :, cols]
        return value.reshape(D, value.shape[-1])

    def attend(t, _):
        yy, cc = lax.div(t, 2), lax.rem(t, 2)
        at("att", t, 0)

        @pl.when(t == 0)
        def _():
            for i, item in enumerate(ITEMS):
                if item[0] == 0:
                    complete(i)

        pre = dot(x_s[...], block(0, yy, cc), NN) + bqv_s[pl.ds(pl.multiple_of(16 * t, 16), 1)]
        a_s[t] = pre.astype(BF)
        mix = [None] * 3
        for h, (qt, kt, vt, ot, qu, vu, ou) in enumerate(HEADS):
            at("att", t, h + 1)
            qh = (half_of(a_s[t, :, tile(qt)].astype(F32), qu) * 0.125).astype(BF)
            s = dot(qh, a_s[t, :, tile(kt)], NT) + z1_s[:, 0:SEQ]
            e = jnp.exp(s - jnp.max(s, axis=-1, keepdims=True))
            p = (e / jnp.sum(e, axis=-1, keepdims=True)).astype(BF)
            p_s[t, h] = p
            mix[h] = dot(p, a_s[t, :, tile(vt)], NN)
        a_s[t, :, tile(5)] = jnp.where(low, mix[0], mix[1]).astype(BF)
        a_s[t, :, tile(4)] = jnp.where(low, a_s[t, :, tile(4)].astype(F32), mix[2]).astype(BF)
        acc[...] += dot(mixed_of(t), block(0, yy, cc, slice(512, 768)), NT)
        return 0

    lax.fori_loop(0, 4, attend, 0)

    at("ln1")

    def norm1(i, _):
        rr = pl.ds(pl.multiple_of(i * 256, 256), 256)
        u = acc[rr]
        u = u - jnp.mean(u, axis=-1, keepdims=True)
        rs = lax.rsqrt(jnp.mean(u * u, axis=-1, keepdims=True) + EPS)
        n = u * rs
        z1_s[rr] = n
        rs1_s[rr, 0:64] = jnp.broadcast_to(rs, (256, 64))
        n = n * g1 + b1
        nl_s[rr] = n.astype(BF)
        acc[rr] = n + c2
        return 0

    lax.fori_loop(0, 2, norm1, 0)

    def up(i, t, _):
        kind, a, b = ITEMS[i]
        at(f"up{a}", t)
        pl.when(t == 0)(functools.partial(complete, i))
        bias = vec_s[pl.ds(pl.multiple_of(16 * t, 16), 1), a:b]
        u = dot(nl_s[...], block(1, lax.div(t, 2), lax.rem(t, 2), slice(a, b)), NN) + bias
        phi = 0.5 + 0.5 * lax.erf(u * 0.7071067811865476)
        act_s[t, :, a:b] = (u * phi).astype(BF)
        gp_s[t, :, a:b] = (phi + u * (0.3989422804014327 * jnp.exp(-0.5 * u * u))).astype(BF)
        return 0

    def down(i, n, _):
        kind, a, b = ITEMS[i]
        at(f"down{a}", n)
        pl.when(n == 0)(functools.partial(complete, i))
        act = jnp.concatenate([act_s[2 * n, :, a:b], act_s[2 * n + 1, :, a:b]], axis=1)
        weight = jnp.concatenate([block(2, n, 0, slice(a, b)), block(2, n, 1, slice(a, b))], axis=1)
        acc[...] += dot(act, weight, NT)
        return 0

    for i, item in enumerate(ITEMS):
        if item[0]:
            lax.fori_loop(0, 6 - 2 * item[0], functools.partial((up, down)[item[0] - 1], i), 0)

    at("ln2")

    def put(row, value):
        gv_s[0, row : row + 1] += value

    def norm2(i, sums):
        rr = pl.ds(pl.multiple_of(i * 256, 256), 256)
        u = acc[rr]
        u = u - jnp.mean(u, axis=-1, keepdims=True)
        rs = lax.rsqrt(jnp.mean(u * u, axis=-1, keepdims=True) + EPS)
        n = u * rs
        ag_s[rr] = (n * g2 + b2).astype(BF)
        ct = cot_s[rr].astype(F32)
        cg = ct * g2
        cgn = cg * n
        grad = rs * (cg - rs1_s[rr, 64:65] - n * jnp.mean(cgn, axis=-1, keepdims=True))
        acc[rr] = grad
        grad = grad.astype(BF)
        dg_s[rr] = grad
        dgt_s[:, rr] = grad.T
        add = (ct * n, grad.astype(F32))
        return tuple(a + jnp.sum(b, axis=0, keepdims=True) for a, b in zip(sums, add))

    sums = lax.fori_loop(0, 2, norm2, (jnp.zeros((1, D), F32),) * 2)
    for row, value in zip((5, 2), sums):
        put(row, value)
    save_hid = pltpu.make_async_copy(ag_s, hid_hbm, io_sem.at[2])
    save_hid.start()


    def down_grad(n, cc):
        zz = zx[PIECES[n]]
        rr = pl.ds(pl.multiple_of(192 * zz, 64), 192)
        for yy in range(2):
            value = dot(dgt_s[rr], act_s[2 * yy + cc], NN).astype(BF)
            g12[1, yy, cc, pairs(zz)] = value.reshape(2, 96, D)

    for n in range(4):
        transfers(STEPS.get(("dw2", n, 0), ()))
        down_grad(n, cn)
        transfers(STEPS.get(("dw2", n, 1), ()))
        down_grad(n, c)

    def turn(n):
        return jnp.where(n < 2, yn, y), jnp.where(lax.rem(n, 2) == 0, cn, c)

    def up_grad(n, _):
        yy, cc = turn(n)
        t = 2 * yy + cc
        at("dw1", n, 0)
        ig = (dot(dg_s[...], block(2, yy, cc), NN) * gp_s[t].astype(F32)).astype(BF)
        ig_s[...] = ig
        gv_s[t, 0:1] = jnp.sum(ig.astype(F32), axis=0, keepdims=True)
        g12[0, yy, cc] = dot(nl_s[...], ig_s[...], TN).astype(BF).reshape(8, 96, D)
        at("dw1", n, 1)
        acc[...] += dot(ig_s[...], block(1, yy, cc), NT)
        return 0

    lax.fori_loop(0, 4, up_grad, 0)
    gather_sent()
    for peer in me.peers:
        pl.semaphore_signal(ready, inc=1, device_id=peer, device_id_type=MESH)

    at("ln1b")
    save_hid.wait()

    def norm1_back(i, _):
        rr = pl.ds(pl.multiple_of(i * 256, 256), 256)
        n, gr = z1_s[rr], acc[rr]
        put(3, jnp.sum(gr * n, axis=0, keepdims=True))
        put(4, jnp.sum(gr, axis=0, keepdims=True))
        cg = gr * g1
        grad = rs1_s[rr, 0:1] * (
            cg
            - jnp.mean(cg, axis=-1, keepdims=True)
            - n * jnp.mean(cg * n, axis=-1, keepdims=True)
        )
        acc[rr] = grad
        grad = grad.astype(BF)
        ag_s[rr] = grad
        put(1, jnp.sum(grad.astype(F32), axis=0, keepdims=True))
        return 0

    lax.fori_loop(0, 2, norm1_back, 0)

    def attend_back(n, _):
        yy, cc = turn(n)
        t = 2 * yy + cc
        at("dw0", n, 0)
        pl.when(n == 0)(functools.partial(pl.semaphore_wait, ready, len(me.peers)))
        mg = dot(ag_s[...], block(0, yy, cc, slice(512, 768)), NN)
        dq, dk, dv = [None] * 3, [None] * 3, [None] * 3
        for h, (qt, kt, vt, ot, qu, vu, ou) in enumerate(HEADS):
            if h:
                at("dw0", n, h)
            go = half_of(mg[:, 128:256] if ot == 5 else mg[:, 0:128], ou)
            inner = jnp.sum(go * a_s[t, :, tile(ot)].astype(F32), axis=-1, keepdims=True)
            go = go.astype(BF)
            p = p_s[t, h]
            dv[h] = dot(p, go, TN)
            ds = (p.astype(F32) * (dot(go, a_s[t, :, tile(vt)], NT) - inner)).astype(BF)
            dq[h] = dot(ds, a_s[t, :, tile(kt)], NN) * 0.125
            dk[h] = dot(ds, a_s[t, :, tile(qt)], TN) * 0.125
        da_s[:, tile(0)] = jnp.where(low, dq[0], dq[1]).astype(BF)
        da_s[:, tile(1)] = jnp.where(low, dk[0], dk[1]).astype(BF)
        da_s[:, tile(2)] = jnp.where(low, dv[0], dv[1]).astype(BF)
        da_s[:, tile(3)] = jnp.where(low, dq[2], dv[2]).astype(BF)
        da_s[:, tile(4)] = jnp.where(low, dk[2], 0.0).astype(BF)
        at("dw0", n, 3)
        sums = jnp.sum(da_s[...].astype(F32), axis=0, keepdims=True)
        for s, start in enumerate(SLOTS):
            m = start // 128
            gv_s[t, 7 + s : 8 + s, tile(m)] = half_of(sums[:, tile(m)], (start // 64) % 2)
        g0 = w.at[2, yy, cc]
        g0[:, :, 0:512] = dot(x_s[...], da_s[:, 0:512], TN).astype(BF).reshape(8, 96, 512)
        tail = dot(ag_s[...], mixed_of(t), TN)
        mixed = tail[:, 0:128] + dot(x_s[...], da_s[:, tile(4)], TN)
        g0[:, :, 512:640] = mixed.astype(BF).reshape(8, 96, 128)
        g0[:, :, 640:768] = tail[:, 128:256].astype(BF).reshape(8, 96, 128)
        at("dw0", n, 4)
        acc[...] += dot(da_s[...], block(0, yy, cc, slice(0, 640)), NT)
        return 0

    lax.fori_loop(0, 4, attend_back, 0)
    at("gx")
    dg_s[...] = acc[...].astype(BF)
    save_gx = pltpu.make_async_copy(dg_s, gx_hbm, io_sem.at[3])
    save_gx.start()
    at("small")

    for t in range(1, 4):
        gv_s[t, 1:7] = gv_s[0, 1:7]

    def collect(d, _):
        vec, head = spread(d)
        zz, xx = lax.div(d, 2), lax.rem(d, 2)
        val = gv_s[...].reshape(64, D)
        high = val.astype(BF)
        rest = (val - high.astype(F32)).astype(BF)
        is_vec = (iota((64, 1), 0) & 15) < 7
        got = jnp.where(is_vec, dot(high, vec, NT) + dot(rest, vec, NT), dot(high, head, NT) + dot(rest, head, NT))
        for t in range(4):
            sb[t % 2, xx, t // 2, zz] = got[16 * t : 16 * t + 16]
        return 0

    lax.fori_loop(0, 8, collect, 0)
    at("tail")
    grads_sent()
    for cp in [save_gx, save_small] + save_grads:
        cp.wait()


def run(r, *args):
    hbm, sm = pl.BlockSpec(memory_space=pl.ANY), pl.BlockSpec(memory_space=pltpu.SMEM)
    t = (SEQ, D)
    V = pltpu.VMEM
    items = len(ITEMS)
    gather = [DMA((items,))] * 3 + [DMA((items, 4))] * 3 + [DMA((items,))] * 2
    back = [DMA((3,))] * 3 + [DMA((3, 4))] * 4 + [DMA((3,))] * 2
    blocks = (2, 2, 8, 96, D)
    return pl.pallas_call(
        functools.partial(kernel, r),
        out_shape=(
            jax.ShapeDtypeStruct(t, BF),
            jax.ShapeDtypeStruct(t, BF),
            jax.ShapeDtypeStruct((3, 96, D), F32),
            jax.ShapeDtypeStruct((16, 128), F32),
        ),
        in_specs=[sm] + [hbm] * 17,
        out_specs=(hbm,) * 4,
        scratch_shapes=[V(i.shape, i.dtype) for i in args[3:]]
        + [DMA((15,)), V((3, 96, D), F32), V((16, 128), F32)]
        + [
            V((3, 96, D), BF), V((3,) + blocks, BF), V((2,) + blocks, BF), V((2,) + blocks, BF),
            V((16, 128), F32), V((2, 2, 2, 4, 16, 128), F32), V((64, D), F32), V((64, D), F32),
            V((4,) + t, BF), V((4, 3, SEQ, SEQ), BF), V(t, F32), V((SEQ, 128), F32), V(t, F32),
            V((4,) + t, BF), V((4,) + t, BF), V(t, BF),
            V(t, BF), V(t, BF), V(t, BF), V((D, SEQ), BF), V(t, BF), V(t, BF), V((SEQ, 640), BF), V((4, 16, D), F32),
            V((2, 2, 4, 16, 128), F32), V((2, 4, 16, 128), F32), V((4, 16, 128), F32), V((4, 16, 128), F32),
            DMA((8,)), DMA((1,)), *gather, DMA((7,)), DMA((7,)),
            *back, DMA((7,)), DMA((7,)), pltpu.SemaphoreType.REGULAR,
        ],
        compiler_params=pltpu.CompilerParams(
            collective_id=0, has_side_effects=True, vmem_limit_bytes=67043328
        ),
    )(*args)


FINAL = ((96, 192),) * 3 + ((192, 96), (96, D), (96, D), (3, 8), (3, 8)) + ((1, 96),) * 7


def finish_kernel(hid_hbm, gx_hbm, g_hbm, s_hbm, *refs):
    outs, scratch, sem = refs[:17], refs[17:-1], refs[-1]
    hid, gx, g, s = scratch[:4]
    wq, wk, wv, wo, w1, w2, bq, bv, *vectors = scratch[4:]

    def copy(n, src, dst):
        cp = pltpu.make_async_copy(src, dst, sem.at[n])
        cp.start()
        return cp

    get_g, get_s = copy(0, g_hbm, g), copy(1, s_hbm, s)
    get_hid, get_gx = copy(2, hid_hbm, hid), copy(3, gx_hbm, gx)
    get_g.wait()
    out = [copy(8, g.at[1], outs[6]), copy(9, g.at[2], outs[7])]
    a = g[0]
    for n, ref in enumerate((wq, wk, wv)):
        ref[:, 0:128] = a[:, 128 * n : 128 * n + 128]
    wq[:, 128:192] = a[:, 384:448]
    wk[:, 128:192] = a[:, 512:576]
    wv[:, 128:192] = a[:, 448:512]
    out += [copy(10 + n, ref, outs[2 + n]) for n, ref in enumerate((wq, wk, wv))]
    get_hid.wait()
    out.append(copy(4, hid, outs[0]))
    get_gx.wait()
    out.append(copy(5, gx, outs[1]))
    eye = (iota((96, 96), 0) == iota((96, 96), 1)).astype(F32)
    turned = lax.dot_general(
        a[:, 512:768], eye, (TN, ((), ())), preferred_element_type=F32, precision=lax.Precision.HIGHEST
    )
    wo[0:128] = turned[128:256]
    wo[128:192] = turned[64:128]
    out.append(copy(6, wo, outs[5]))
    get_s.wait()
    bq[...] = s[7:10, 0:8]
    bv[...] = s[10:13, 0:8]
    for n, ref in enumerate(vectors):
        ref[...] = s[n : n + 1, 0:96]
    out += [copy(13 + n, ref, outs[8 + n]) for n, ref in enumerate((bq, bv, *vectors))]
    for cp in out:
        cp.wait()


def finish(hidden, gx, grads, small):
    tokens = jax.ShapeDtypeStruct((SEQ, D), BF)
    hbm = pl.BlockSpec(memory_space=pl.ANY)
    out = pl.pallas_call(
        finish_kernel,
        out_shape=[tokens, tokens] + [jax.ShapeDtypeStruct(s, F32) for s in FINAL],
        in_specs=[hbm] * 4,
        out_specs=[hbm] * 17,
        scratch_shapes=[pltpu.VMEM((SEQ, D), BF)] * 2
        + [pltpu.VMEM((3, 96, D), F32), pltpu.VMEM((16, 128), F32)]
        + [pltpu.VMEM(s, F32) for s in FINAL]
        + [DMA((22,))],
    )(hidden, gx, grads, small)
    out = list(out)
    return out[:7] + [out[7].T] + out[8:11] + [i.reshape(96) for i in out[11:]]


def body(
    hidden_in, seq_lengths, out_grad, query_weight, key_weight, value_weight, output_weight, up_weight,
    down_weight, query_bias, value_bias, inner_bias, output_bias, down_bias, first_gain, first_shift,
    second_gain, second_shift,
):
    r = lax.axis_size("dp") // 8
    groups = [[g * r + i for i in range(r)] for g in range(8)]

    def whole(value, axis):
        if r == 1:
            return value
        value = value.astype(BF)
        return lax.all_gather(value, "dp", axis=axis, tiled=True, axis_index_groups=groups).astype(F32)

    def shard(value, axis):
        if r == 1:
            return value
        return lax.psum_scatter(value, "dp", scatter_dimension=axis, tiled=True, axis_index_groups=groups)

    vectors = (output_bias, down_bias, first_gain, first_shift, second_gain, second_shift)
    hidden, gx, gw, gs = run(
        r, seq_lengths, hidden_in, out_grad,
        whole(query_weight, 0), whole(key_weight, 0), whole(value_weight, 0), whole(output_weight, 1),
        whole(up_weight, 0), whole(down_weight.T, 0),
        whole(query_bias, 1), whole(value_bias, 1), whole(inner_bias, 1),
        *(whole(i.reshape(1, -1), 1) for i in vectors),
    )
    if r == 1:
        return tuple(finish(hidden, gx, gw, gs))
    gw = shard(gw, 1)
    gv = shard(gs[0:7, 0:96], 1)
    gh = shard(gs[7:13, 0:8], 1)
    a = gw[0]
    return (
        hidden,
        gx,
        jnp.concatenate([a[:, 0:128], a[:, 384:448]], axis=1),
        jnp.concatenate([a[:, 128:256], a[:, 512:576]], axis=1),
        jnp.concatenate([a[:, 256:384], a[:, 448:512]], axis=1),
        jnp.concatenate([a[:, 640:768], a[:, 576:640]], axis=1).T,
        gw[1],
        gw[2].T,
        gh[0:3],
        gh[3:6],
        gv[0:1],
        *(gv[i] for i in range(1, 7)),
    )


def solution(mesh):
    both, dp = P(("dp", "tensor"), None), P("dp")
    rows_first, columns_first = P("dp", "tensor"), P("tensor", "dp")
    weights = (rows_first,) * 3 + (columns_first, rows_first, columns_first)
    smalls = (columns_first,) * 3 + (dp,) * 6
    return jax.shard_map(
        body,
        mesh=mesh,
        in_specs=(P("dp", None),) * 3 + weights + smalls,
        out_specs=(both, both) + weights + smalls,
        check_vma=False,
    )
```

```python
import functools

import jax
import jax.numpy as jnp
from jax import lax
from jax.experimental import pallas as pl
from jax.experimental.pallas import tpu as pltpu
from jax.sharding import PartitionSpec as P

SEQ = 512
D = 768
EPS = 1e-12
NEGATIVE = -1000000000.0
MESH = pl.DeviceIdType.MESH
BF = jnp.bfloat16
F32 = jnp.float32
DMA = pltpu.SemaphoreType.DMA
NN, NT, TN = ((1,), (0,)), ((1,), (1,)), ((0,), (0,))
HEADS = ((0, 1, 2, 5, 0, 0, 0), (0, 1, 2, 5, 1, 1, 1), (3, 4, 3, 4, 0, 1, 1))
SLOTS = (0, 64, 384, 256, 320, 448)
ITEMS = ((0, 0, 768), (1, 0, 768), (2, 0, 512), (2, 512, 768))
PIECES = (3, 2, 1, 0)
ORDER = (2, 3, 1, 0)
AHEAD = 1
PAIRED = (1, 2)
STEPS = {
    ("pack",): (("sa", 0), ("o", 0), ("oz", 0)),
    ("mask",): (("o", 1), ("o", 2), ("o", 3)),
    ("expand",): (("ry", 0, 0), ("sa", 1), ("rx", 0, 0), ("rx", 1, 0), ("ry", 2, 0), ("ry", 1, 0), ("q", 0, 3),
        ("rx", 3, 0), ("rx", 2, 0), ("q", 0, 1), ("q", 0, 2), ("oz", 1), ("oz", 2), ("sa", 2), ("ry", 0, 3),
        ("rx", 0, 1), ("rx", 0, 3), ("rx", 0, 2), ("ry", 0, 1), ("sa", 3), ("ry", 3, 0), ("ry", 0, 2)),
    ("att", 0, 0): (("q", 1, 3), ("q", 1, 1), ("q", 1, 2), ("ry", 1, 3), ("fa", 0), ("rx", 1, 3), ("ry", 1, 1),
        ("rx", 1, 1), ("q", 2, 3), ("rx", 1, 2)),
    ("att", 0, 1): (("oz", 3),),
    ("att", 0, 3): (("ry", 1, 2),),
    ("att", 1, 2): (("q", 2, 1),),
    ("att", 1, 3): (("q", 2, 2),),
    ("att", 2, 0): (("ry", 2, 3), ("rx", 2, 3)),
    ("att", 2, 2): (("q", 3, 1),),
    ("att", 3, 0): (("q", 3, 2), ("q", 3, 3), ("fa", 1)),
    ("att", 3, 2): (("ry", 2, 2), ("rx", 2, 2)),
    ("ln1",): (("ry", 2, 1), ("rx", 2, 1)),
    ("up0", 0): (("rx", 3, 2), ("rx", 3, 1)),
    ("up0", 1): (("ry", 3, 3), ("ry", 3, 1), ("rx", 3, 3)),
    ("up0", 2): (("ry", 3, 2), ("fa", 2)),
    ("down0", 0): (("fa", 3),),
    ("dw2", 0, 1): (("ps", 2, 3),),
    ("dw2", 2, 1): (("pa", 2, 3), ("ps", 2, 1), ("bx", 2, 3)),
    ("dw2", 3, 1): (("ps", 2, 0), ("by", 2, 3)),
    ("dw1", 0, 0): (("pa", 2, 1),),
    ("dw1", 0, 1): (("ps", 1, 0),),
    ("dw1", 1, 0): (("pa", 2, 0), ("ps", 2, 2)),
    ("dw1", 2, 0): (("pa", 1, 0), ("cz", 2, 3)),
    ("dw1", 3, 0): (("pa", 2, 2), ("ps", 1, 1), ("ee", 2), ("by", 2, 1)),
    ("dw0", 0, 0): (("pa", 1, 1), ("bx", 2, 1), ("bx", 1, 3)),
    ("dw0", 0, 3): (("by", 1, 3),),
    ("dw0", 1, 0): (("by", 2, 0), ("bx", 2, 2)),
    ("dw0", 1, 1): (("ps", 0, 0), ("by", 2, 2), ("by", 1, 1)),
    ("dw0", 1, 4): (("cz", 2, 1), ("ee", 1)),
    ("dw0", 2, 0): (("cz", 1, 3),),
    ("dw0", 2, 2): (("bx", 2, 0),),
    ("dw0", 2, 3): (("bx", 1, 1),),
    ("dw0", 2, 4): (("ps", 0, 1), ("pa", 0, 0), ("cz", 2, 2)),
    ("dw0", 3, 1): (("bx", 1, 2), ("by", 1, 0), ("by", 1, 2)),
    ("dw0", 3, 4): (("pa", 0, 1),),
    ("small",): (("cz", 1, 1), ("cz", 2, 0)),
    ("tail",): (("by", 0, 2), ("cz", 1, 2), ("sb", 0), ("sb", 1), ("bx", 0, 2), ("bx", 1, 0), ("by", 0, 3),
        ("cz", 0, 2), ("sb", 2), ("bx", 0, 3), ("by", 0, 1), ("cz", 1, 0), ("fz", 1), ("sb", 3), ("cz", 0, 3),
        ("bx", 0, 1), ("fz", 2), ("sb", 4), ("by", 0, 0), ("cz", 0, 1), ("bx", 0, 0), ("cz", 0, 0), ("fz", 0)),
}


def dot(a, b, dims):
    return lax.dot_general(a, b, (dims, ((), ())), preferred_element_type=F32)


def iota(shape, axis):
    return lax.broadcasted_iota(jnp.int32, shape, axis)


class Place:
    def __init__(self, r):
        dp = lax.axis_index("dp")
        t = lax.axis_index("tensor")
        g = lax.div(dp, r)
        self.r, self.q, self.t = r, lax.rem(dp, r), t
        self.z, self.x = lax.div(g, 2), lax.rem(g, 2)
        self.y, self.c = lax.div(t, 2), lax.rem(t, 2)
        self.xn, self.yn, self.cn = 1 - self.x, 1 - self.y, 1 - self.c
        self.zs = [lax.rem(self.z + i, 4) for i in range(4)]
        self.to_x = self.dev(self.z, self.xn, self.y, self.c)
        self.to_y = self.dev(self.z, self.x, self.yn, self.c)
        self.to_core = self.dev(self.z, self.x, self.y, self.cn)
        self.to_z = [self.dev(self.zs[i], self.x, self.y, self.c) for i in range(4)]
        self.zx = [self.z, self.z + 1 - 2 * lax.rem(self.z, 2), self.zs[2], 3 - self.z]
        self.to_zx = [self.dev(i, self.x, self.y, self.c) for i in self.zx]
        self.peers = self.to_z[1:] + [self.to_x, self.to_y, self.to_core]

    def dev(self, z, x, y, c):
        return {"dp": (2 * z + x) * self.r + self.q, "tensor": 2 * y + c}


def remote(src, dst, ss, rs, to):
    return pltpu.make_async_remote_copy(
        src_ref=src, dst_ref=dst, send_sem=ss, recv_sem=rs, device_id=to, device_id_type=MESH
    )


def arrived(ref, sem):
    pltpu.make_async_copy(ref, ref, sem).wait()


def spread(d):
    lane, col = iota((128, D), 0), iota((128, D), 1)
    vec = (col == lane + 96 * d) & (lane < 96)
    head = ((col & 63) == lane + 8 * d) & (lane < 8)
    return vec.astype(F32).astype(BF), head.astype(F32).astype(BF)


def kernel(
    r,
    lens_ref, x_hbm, cot_hbm, *refs,
):
    shards_hbm, (hid_hbm, gx_hbm, o_hbm, so_hbm), refs = refs[:15], refs[15:19], refs[19:]
    shards, (load_sem, o_ref, so_ref, *refs) = refs[:15], refs[15:]
    work(
        r, lens_ref, x_hbm, cot_hbm, shards_hbm, shards, load_sem, hid_hbm, gx_hbm, o_hbm, so_hbm, o_ref, so_ref, *refs
    )


def work(
    r, lens_ref, x_hbm, cot_hbm, shards_hbm, shards, load_sem, hid_hbm, gx_hbm, o_hbm, so_hbm, o_ref, so_ref,
    own, w, g12, rb12, small, sb, vec_s, bqv_s, a_s, p_s, z1_s, rs1_s, acc, act_s, gp_s, nl_s,
    x_s, cot_s, dg_s, dgt_s, ig_s, ag_s, da_s, gv_s, s1, s2, s3, s4,
    io_sem, own_sem, s_first, s_far, s_core, r_z, r_x, r_y, r_far, r_core, ss_small, rs_small,
    t_p, t_1, t_2, u_p, u_y1, u_x1, u_2, u_z, u_e, ss_grad, rs_grad, ready,
):
    me = Place(r)
    z, x, y, c, xn, yn, cn, zs, zx = me.z, me.x, me.y, me.c, me.xn, me.yn, me.cn, me.zs, me.zx
    bar = pltpu.get_barrier_semaphore()
    for peer in me.peers:
        pl.semaphore_signal(bar, inc=1, device_id=peer, device_id_type=MESH)
    mine = pl.ds(pl.multiple_of(me.t * SEQ, SEQ), SEQ)
    load_x = pltpu.make_async_copy(x_hbm.at[mine], x_s, io_sem.at[0])
    load_c = pltpu.make_async_copy(cot_hbm.at[mine], cot_s, io_sem.at[1])
    loads = [pltpu.make_async_copy(a, b, load_sem.at[i]) for i, (a, b) in enumerate(zip(shards_hbm, shards))]
    for cp in loads:
        cp.start()
    load_x.start()
    load_c.start()
    wq_ref, wk_ref, wv_ref, wo_ref, w1_ref, w2_ref, bq_ref, bv_ref, *vector_refs = shards

    near, far = slice(0, 48), slice(48, 96)

    def piece(i, zz, xx, yy, rr=slice(None)):
        kind, a, b = ITEMS[i]
        return w.at[kind, yy, c, 2 * zz + xx, rr, a:b]

    def x_pair(i, zz, yy):
        kind, a, b = ITEMS[i]
        return w.at[kind, yy, c, pl.ds(2 * zz, 2), near, a:b]

    def y_pair(i, zz, xx):
        kind, a, b = ITEMS[i]
        return w.at[kind, :, c, 2 * zz + xx, far, a:b]

    def o_sends(i):
        kind, a, b = ITEMS[i]
        return [
            remote(own.at[kind, near, a:b], piece(i, z, x, y, near), s_first.at[i], r_x.at[i, z], me.to_x),
            remote(own.at[kind, far, a:b], piece(i, z, x, y, far), s_first.at[i], r_y.at[i, z], me.to_y),
        ]

    def o_wait(i):
        kind, a, b = ITEMS[i]
        cp = pltpu.make_async_copy(own.at[kind, :, a:b], piece(i, z, x, y), own_sem.at[0])
        cp.start()
        cp.wait()

    def oz_sends(i):
        kind, a, b = ITEMS[i]
        src, dst = own.at[kind, :, a:b], piece(i, z, x, y)
        return [remote(src, dst, s_first.at[i], r_z.at[i, z], me.to_z[j]) for j in (1, 3, 2)]

    def q_wait(i, j):
        arrived(piece(i, zs[j], x, y), r_z.at[i, zs[j]])

    def q_sends(i, j):
        a, b = piece(i, zs[j], x, y, near), piece(i, zs[j], x, y, far)
        return [
            remote(a, a, s_first.at[i], r_x.at[i, zs[j]], me.to_x),
            remote(b, b, s_first.at[i], r_y.at[i, zs[j]], me.to_y),
        ]

    def ry_wait(i, j):
        arrived(piece(i, zs[j], xn, y, near), r_x.at[i, zs[j]])

    def ry_sends(i, j):
        u = x_pair(i, zs[j], y)
        return [remote(u, u, s_far.at[i], r_far.at[i], me.to_y)]

    def rx_wait(i, j):
        arrived(piece(i, zs[j], x, yn, far), r_y.at[i, zs[j]])

    def rx_sends(i, j):
        u = y_pair(i, zs[j], x)
        return [remote(u, u, s_far.at[i], r_far.at[i], me.to_x)]

    def fa_wait(i):
        kind, a, b = ITEMS[i]
        arrived(w.at[kind, yn, c, :, :, a:b], r_far.at[i])

    def fa_sends(i):
        kind, a, b = ITEMS[i]
        u = w.at[kind, :, c, :, :, a:b]
        return [remote(u, u, s_core.at[i], r_core.at[i], me.to_core)]

    def complete(i):
        kind, a, b = ITEMS[i]
        arrived(w.at[kind, :, cn, :, :, a:b], r_core.at[i])

    def sa_wait(n):
        if n == 1:
            for j in (1, 2, 3):
                arrived(sb.at[c, x, y, z], rs_small.at[zs[j]])
        if n == 2:
            arrived(sb.at[c, x, y], rs_small.at[4])
        if n == 3:
            arrived(sb.at[c, :, y], rs_small.at[5])

    def sa_sends(n):
        u = (sb.at[c, x, y, z], sb.at[c, x, y], sb.at[c, :, y], sb.at[c])[n]
        if n == 0:
            return [remote(u, u, ss_small.at[j], rs_small.at[z], me.to_z[j]) for j in (1, 3, 2)]
        return [remote(u, u, ss_small.at[3 + n], rs_small.at[3 + n], (me.to_x, me.to_y, me.to_core)[n - 1])]

    def grad(kind):
        return w.at[2] if kind == 0 else g12.at[kind - 1]

    def land(kind):
        return w.at[1] if kind == 0 else rb12.at[kind - 1]

    def pairs(zz):
        return pl.ds(2 * zz, 2)

    def y1(kind, zz):
        return land(kind).at[1, 0, pairs(zz), near]

    def x1(kind, zz):
        return land(kind).at[1, 0, pairs(zz), far]

    def x2(kind, zz):
        return land(kind).at[1, 1, zz, near]

    def y2(kind, zz):
        return land(kind).at[1, 1, zz, far]

    def zb(kind, j):
        return land(kind).at[1, 1, 3 + j]

    def ps_sends(kind, n):
        if kind == 2:
            zz = zx[n]
            return [
                remote(grad(2).at[:, cn, pairs(zz)], land(2).at[0, :, pairs(zz)], t_p.at[2], u_p.at[2, zz], me.to_core)
            ]
        yy = (yn, y)[n]
        return [remote(grad(kind).at[yy, cn], land(kind).at[0, yy], t_p.at[kind], u_p.at[kind, yy], me.to_core)]

    def y1_send(kind, j):
        src = grad(kind).at[yn, c, pairs(zx[j]), near]
        return remote(src, y1(kind, zx[j]), t_1.at[kind], u_y1.at[kind, zx[j]], me.to_y)

    def x1_send(kind, j):
        src = grad(kind).at[:, c, 2 * zx[j] + xn, far]
        return remote(src, x1(kind, zx[j]), t_1.at[kind], u_x1.at[kind, zx[j]], me.to_x)

    def pa_wait(kind, n):
        g = grad(kind)
        if kind == 2:
            zz = zx[n]
            arrived(land(2).at[0, :, pairs(zz)], u_p.at[2, zz])
            g[:, c, pairs(zz)] = g[:, c, pairs(zz)] + land(2)[0, :, pairs(zz)]
            return
        yy = (yn, y)[n]
        arrived(land(kind).at[0, yy], u_p.at[kind, yy])

        def add(i, _):
            d = pl.ds(2 * i, 2)
            g[yy, c, d] = g[yy, c, d] + land(kind)[0, yy, d]
            return 0

        lax.fori_loop(0, 4, add, 0)

    def near_send(kind):
        src = grad(kind).at[yn, c, pairs(zx[3]), near]
        return remote(src, y1(kind, zx[2]), t_1.at[kind], u_e.at[kind], me.to_zx[1])

    def far_send(kind):
        src = grad(kind).at[:, c, 2 * zx[3] + xn, far]
        return remote(src, x1(kind, zx[2]), t_1.at[kind], u_e.at[kind], me.to_zx[1])

    def pa_sends(kind, n):
        if kind == 2:
            return {0: [y1_send(2, 0), x1_send(2, 0)], 1: [y1_send(2, 1), x1_send(2, 1)], 2: [], 3: [near_send(2), far_send(2)]}[n]
        if kind == 1:
            return [(near_send, far_send)[n](1), (y1_send, x1_send)[n](1, 1)]
        return [(y1_send, x1_send)[n](kind, j) for j in ORDER[:AHEAD]]

    def ee_wait(kind):
        arrived(land(kind).at[1, 0, pairs(zx[3])], u_e.at[kind])
        u = grad(kind).at[yn, c, pairs(zx[2]), near]
        u[...] = u[...] + y1(kind, zx[3])[...]
        u = grad(kind).at[:, c, 2 * zx[2] + xn, far]
        u[...] = u[...] + x1(kind, zx[3])[...]

    def ee_sends(kind):
        return [y1_send(kind, 2), x1_send(kind, 2)]

    def later(kind, j, send):
        if kind == 2:
            return []
        if kind == 1:
            return [send(1, 0)] if j == 1 else []
        n = ORDER.index(j) + AHEAD
        return [send(kind, ORDER[n])] if n < 4 else []

    def by_wait(kind, j):
        if kind in PAIRED and j == 3:
            return
        arrived(y1(kind, zx[j]), u_y1.at[kind, zx[j]])
        u = grad(kind).at[y, c, pairs(zx[j]), near]
        u[...] = u[...] + y1(kind, zx[j])[...]

    def by_sends(kind, j):
        src = grad(kind).at[y, c, 2 * zx[j] + xn, near]
        return [
            remote(src, x2(kind, zx[j]), t_2.at[kind], u_2.at[kind, zx[j]], me.to_x)
        ] + later(kind, j, y1_send)

    def bx_wait(kind, j):
        if kind in PAIRED and j == 3:
            return
        arrived(x1(kind, zx[j]), u_x1.at[kind, zx[j]])
        u = grad(kind).at[:, c, 2 * zx[j] + x, far]
        u[...] = u[...] + x1(kind, zx[j])[...]

    def bx_sends(kind, j):
        src = grad(kind).at[yn, c, 2 * zx[j] + x, far]
        return [
            remote(src, y2(kind, zx[j]), t_2.at[kind], u_2.at[kind, zx[j]], me.to_y)
        ] + later(kind, j, x1_send)

    def cz_wait(kind, j):
        arrived(land(kind).at[1, 1, zx[j]], u_2.at[kind, zx[j]])
        u = grad(kind).at[y, c, 2 * zx[j] + x]
        add = land(kind).at[1, 1, zx[j]]
        if j:
            u[...] = u[...] + add[...]
        else:
            o_ref[kind] = u[...].astype(F32) + add[...].astype(F32)

    def cz_sends(kind, j):
        if not j:
            return []
        src = grad(kind).at[y, c, 2 * zx[j] + x]
        return [remote(src, zb(kind, j), t_2.at[kind], u_z.at[kind], me.to_zx[j])]

    def fz_wait(kind):
        arrived(land(kind).at[1, 1, 4:7], u_z.at[kind])
        o_ref[kind] = o_ref[kind] + sum(zb(kind, j)[...].astype(F32) for j in (1, 2, 3))
        save_grads[kind].start()

    save_grads = [pltpu.make_async_copy(o_ref.at[n], o_hbm.at[n], io_sem.at[4 + n]) for n in range(3)]
    save_small = pltpu.make_async_copy(so_ref, so_hbm, io_sem.at[7])

    def sb_wait(n):
        if n == 1:
            arrived(s1, rs_grad.at[4])
            sb[c] = sb[c] + s1[...]
        if n == 2:
            arrived(s2, rs_grad.at[5])
            sb[c, x] = sb[c, x] + s2[...]
        if n == 3:
            arrived(s3, rs_grad.at[6])
            sb[c, x, y] = sb[c, x, y] + s3[...]
        if n == 4:
            total = sb[c, x, y, z]
            for j in (1, 2, 3):
                arrived(s4.at[zs[j]], rs_grad.at[zs[j]])
                total = total + s4[zs[j]]
            so_ref[...] = total
            save_small.start()

    def sb_sends(n):
        if n == 3:
            return [
                remote(sb.at[c, x, y, zs[j]], s4.at[z], ss_grad.at[j], rs_grad.at[z], me.to_z[j]) for j in (1, 3, 2)
            ]
        if n == 4:
            return []
        src, dst = ((sb.at[cn], s1), (sb.at[c, xn], s2), (sb.at[c, x, yn], s3))[n]
        return [remote(src, dst, ss_grad.at[4 + n], rs_grad.at[4 + n], (me.to_core, me.to_x, me.to_y)[n])]

    waits = {
        "o": o_wait, "q": q_wait, "ry": ry_wait, "rx": rx_wait, "fa": fa_wait, "sa": sa_wait,
        "pa": pa_wait, "ee": ee_wait, "by": by_wait, "bx": bx_wait, "cz": cz_wait, "fz": fz_wait, "sb": sb_wait,
    }
    sends = {
        "o": o_sends, "oz": oz_sends, "q": q_sends, "ry": ry_sends, "rx": rx_sends, "fa": fa_sends, "sa": sa_sends,
        "ps": ps_sends, "pa": pa_sends, "ee": ee_sends, "by": by_sends, "bx": bx_sends, "cz": cz_sends, "sb": sb_sends,
    }

    def transfers(steps):
        for name, *args in steps:
            if name == "o":
                for cp in o_sends(*args):
                    cp.start()
            if name in waits:
                waits[name](*args)
            if name in sends and name != "o":
                for cp in sends[name](*args):
                    cp.start()

    def at(name, index=None, part=None):
        if index is None:
            transfers(STEPS.get((name,), ()))
            return
        for n in range(4):
            key = (name, n) if part is None else (name, n, part)
            if key in STEPS:
                pl.when(index == n)(functools.partial(transfers, STEPS[key]))

    def gather_sent():
        for i, (kind, a, b) in enumerate(ITEMS):
            arrived(w.at[kind, y, c, 0:7, :, a:b], s_first.at[i])
            arrived(w.at[kind, y, c, :, :, a:b], s_far.at[i])
            arrived(w.at[kind, :, c, :, :, a:b], s_core.at[i])
        for n in range(4):
            for cp in sa_sends(n):
                cp.wait_send()

    def grads_sent():
        for kind in range(3):
            arrived(grad(kind).at[:, cn], t_p.at[kind])
            arrived(grad(kind).at[y, c], t_1.at[kind])
            arrived(grad(kind).at[y, c, 0:7], t_2.at[kind])
        for n in range(4):
            for cp in sb_sends(n):
                cp.wait_send()

    eye = (iota((96, 96), 0) == iota((96, 96), 1)).astype(F32).astype(BF)
    for cp in loads:
        cp.wait()
    q, k, v = wq_ref[...], wk_ref[...], wv_ref[...]
    own[0, :, 0:128] = q[:, 0:128].astype(BF)
    own[0, :, 128:256] = k[:, 0:128].astype(BF)
    own[0, :, 256:384] = v[:, 0:128].astype(BF)
    own[0, :, 384:512] = jnp.concatenate([q[:, 128:192], v[:, 128:192]], axis=1).astype(BF)
    wo = wo_ref[...].astype(BF)
    o2 = dot(eye, wo[128:192], NT)
    own[0, :, 512:640] = jnp.concatenate([k[:, 128:192], o2], axis=1).astype(BF)
    own[0, :, 640:768] = dot(eye, wo[0:128], NT).astype(BF)
    small[...] = jnp.zeros_like(small)
    for i, ref in enumerate(vector_refs):
        small[i : i + 1, 0:96] = ref[...].astype(BF).astype(F32)
    small[7:10, 0:8] = bq_ref[...].astype(BF).astype(F32)
    small[10:13, 0:8] = bv_ref[...].astype(BF).astype(F32)
    sb[c, x, y, z] = small[...]
    pl.semaphore_wait(bar, len(me.peers))
    at("pack")
    own[1] = w1_ref[...].astype(BF)
    own[2] = w2_ref[...].astype(BF)
    at("mask")

    ends, total = [], jnp.int32(0)
    for i in range(4):
        total = total + lens_ref[me.t, i]
        ends.append(total)
    row, lane = iota((SEQ, 1), 0), iota((1, SEQ), 1)
    seg_q = sum((row >= e).astype(jnp.int32) for e in ends)
    seg_k = sum((lane >= e).astype(jnp.int32) for e in ends)
    valid = row < ends[3]
    same = jnp.where(valid, seg_q, row + 8) == jnp.where(lane < ends[3], seg_k, lane + 8)
    z1_s[:, 0:SEQ] = jnp.where(same, 0.0, NEGATIVE)
    load_c.wait()
    cot_s[...] = jnp.where(valid, cot_s[...].astype(F32), 0.0).astype(BF)
    load_x.wait()
    at("expand")
    arrived(sb.at[c], rs_small.at[6])

    vec_s[...] = jnp.zeros_like(vec_s)
    bqv_s[...] = jnp.zeros_like(bqv_s)

    def expand(d, _):
        vec, head = spread(d)
        zz, xx = lax.div(d, 2), lax.rem(d, 2)
        part = jnp.concatenate([sb[t % 2, xx, t // 2, zz] for t in range(4)], axis=0).astype(BF)
        vec_s[...] += dot(part, vec, NN)
        bqv_s[...] += dot(part, head, NN)
        return 0

    lax.fori_loop(0, 8, expand, 0)
    col = iota((1, D), 1)
    for t in range(4):
        bias = jnp.zeros((1, D), F32)
        for s, start in enumerate(SLOTS):
            keep = (col >= start) & (col < start + 64)
            bias = bias + jnp.where(keep, bqv_s[16 * t + 7 + s : 16 * t + 8 + s], 0.0)
        bqv_s[16 * t : 16 * t + 1] = bias
    bo, c2, g1, b1, g2, b2 = (vec_s[i : i + 1] for i in range(1, 7))

    low = iota((1, 128), 1) < 64
    acc[...] = x_s[...].astype(F32) + bo

    def tile(n):
        return slice(128 * n, 128 * n + 128)

    def half_of(values, upper):
        return jnp.where(low, 0.0, values) if upper else jnp.where(low, values, 0.0)

    def mixed_of(t):
        return jnp.concatenate(
            [half_of(a_s[t, :, tile(4)].astype(F32), 1).astype(BF), a_s[t, :, tile(5)]], axis=1
        )

    def block(kind, yy, cc, cols=slice(None)):
        value = w[kind, yy, cc, :, :, cols]
        return value.reshape(D, value.shape[-1])

    def attend(t, _):
        yy, cc = lax.div(t, 2), lax.rem(t, 2)
        at("att", t, 0)

        @pl.when(t == 0)
        def _():
            for i, item in enumerate(ITEMS):
                if item[0] == 0:
                    complete(i)

        pre = dot(x_s[...], block(0, yy, cc), NN) + bqv_s[pl.ds(pl.multiple_of(16 * t, 16), 1)]
        a_s[t] = pre.astype(BF)
        mix = [None] * 3
        for h, (qt, kt, vt, ot, qu, vu, ou) in enumerate(HEADS):
            at("att", t, h + 1)
            qh = (half_of(a_s[t, :, tile(qt)].astype(F32), qu) * 0.125).astype(BF)
            s = dot(qh, a_s[t, :, tile(kt)], NT) + z1_s[:, 0:SEQ]
            e = jnp.exp(s - jnp.max(s, axis=-1, keepdims=True))
            p = (e / jnp.sum(e, axis=-1, keepdims=True)).astype(BF)
            p_s[t, h] = p
            mix[h] = dot(p, a_s[t, :, tile(vt)], NN)
        a_s[t, :, tile(5)] = jnp.where(low, mix[0], mix[1]).astype(BF)
        a_s[t, :, tile(4)] = jnp.where(low, a_s[t, :, tile(4)].astype(F32), mix[2]).astype(BF)
        acc[...] += dot(mixed_of(t), block(0, yy, cc, slice(512, 768)), NT)
        return 0

    lax.fori_loop(0, 4, attend, 0)

    at("ln1")

    def norm1(i, _):
        rr = pl.ds(pl.multiple_of(i * 256, 256), 256)
        u = acc[rr]
        u = u - jnp.mean(u, axis=-1, keepdims=True)
        rs = lax.rsqrt(jnp.mean(u * u, axis=-1, keepdims=True) + EPS)
        n = u * rs
        z1_s[rr] = n
        rs1_s[rr] = jnp.broadcast_to(rs, (256, 128))
        n = n * g1 + b1
        nl_s[rr] = n.astype(BF)
        acc[rr] = n + c2
        return 0

    lax.fori_loop(0, 2, norm1, 0)

    def up(i, t, _):
        kind, a, b = ITEMS[i]
        at(f"up{a}", t)
        pl.when(t == 0)(functools.partial(complete, i))
        bias = vec_s[pl.ds(pl.multiple_of(16 * t, 16), 1), a:b]
        u = dot(nl_s[...], block(1, lax.div(t, 2), lax.rem(t, 2), slice(a, b)), NN) + bias
        phi = 0.5 + 0.5 * lax.erf(u * 0.7071067811865476)
        act_s[t, :, a:b] = (u * phi).astype(BF)
        gp_s[t, :, a:b] = (phi + u * (0.3989422804014327 * jnp.exp(-0.5 * u * u))).astype(BF)
        return 0

    def down(i, n, _):
        kind, a, b = ITEMS[i]
        at(f"down{a}", n)
        pl.when(n == 0)(functools.partial(complete, i))
        act = jnp.concatenate([act_s[2 * n, :, a:b], act_s[2 * n + 1, :, a:b]], axis=1)
        weight = jnp.concatenate([block(2, n, 0, slice(a, b)), block(2, n, 1, slice(a, b))], axis=1)
        acc[...] += dot(act, weight, NT)
        return 0

    for i, item in enumerate(ITEMS):
        if item[0]:
            lax.fori_loop(0, 6 - 2 * item[0], functools.partial((up, down)[item[0] - 1], i), 0)

    at("ln2")
    gv_s[...] = jnp.zeros_like(gv_s)

    def put(row, value):
        gv_s[0, row : row + 1] += value

    def norm2(i, sums):
        rr = pl.ds(pl.multiple_of(i * 256, 256), 256)
        u = acc[rr]
        u = u - jnp.mean(u, axis=-1, keepdims=True)
        rs = lax.rsqrt(jnp.mean(u * u, axis=-1, keepdims=True) + EPS)
        n = u * rs
        ag_s[rr] = (n * g2 + b2).astype(BF)
        ct = cot_s[rr].astype(F32)
        cg = ct * g2
        cgn = cg * n
        grad = rs * (cg - jnp.mean(cg, axis=-1, keepdims=True) - n * jnp.mean(cgn, axis=-1, keepdims=True))
        acc[rr] = grad
        grad = grad.astype(BF)
        dg_s[rr] = grad
        dgt_s[:, rr] = grad.T
        add = (ct * n, ct, grad.astype(F32))
        return tuple(a + jnp.sum(b, axis=0, keepdims=True) for a, b in zip(sums, add))

    sums = lax.fori_loop(0, 2, norm2, (jnp.zeros((1, D), F32),) * 3)
    for row, value in zip((5, 6, 2), sums):
        put(row, value)
    save_hid = pltpu.make_async_copy(ag_s, hid_hbm, io_sem.at[2])
    save_hid.start()


    def down_grad(n, cc):
        zz = zx[PIECES[n]]
        rr = pl.ds(pl.multiple_of(192 * zz, 64), 192)
        for yy in range(2):
            value = dot(dgt_s[rr], act_s[2 * yy + cc], NN).astype(BF)
            g12[1, yy, cc, pairs(zz)] = value.reshape(2, 96, D)

    for n in range(4):
        transfers(STEPS.get(("dw2", n, 0), ()))
        down_grad(n, cn)
        transfers(STEPS.get(("dw2", n, 1), ()))
        down_grad(n, c)

    def turn(n):
        return jnp.where(n < 2, yn, y), jnp.where(lax.rem(n, 2) == 0, cn, c)

    def up_grad(n, _):
        yy, cc = turn(n)
        t = 2 * yy + cc
        at("dw1", n, 0)
        ig = (dot(dg_s[...], block(2, yy, cc), NN) * gp_s[t].astype(F32)).astype(BF)
        ig_s[...] = ig
        gv_s[t, 0:1] = jnp.sum(ig.astype(F32), axis=0, keepdims=True)
        g12[0, yy, cc] = dot(nl_s[...], ig_s[...], TN).astype(BF).reshape(8, 96, D)
        at("dw1", n, 1)
        acc[...] += dot(ig_s[...], block(1, yy, cc), NT)
        return 0

    lax.fori_loop(0, 4, up_grad, 0)
    gather_sent()
    for peer in me.peers:
        pl.semaphore_signal(ready, inc=1, device_id=peer, device_id_type=MESH)

    at("ln1b")
    save_hid.wait()

    def norm1_back(i, _):
        rr = pl.ds(pl.multiple_of(i * 256, 256), 256)
        n, gr = z1_s[rr], acc[rr]
        put(3, jnp.sum(gr * n, axis=0, keepdims=True))
        put(4, jnp.sum(gr, axis=0, keepdims=True))
        cg = gr * g1
        grad = rs1_s[rr, 0:1] * (
            cg
            - jnp.mean(cg, axis=-1, keepdims=True)
            - n * jnp.mean(cg * n, axis=-1, keepdims=True)
        )
        acc[rr] = grad
        grad = grad.astype(BF)
        ag_s[rr] = grad
        put(1, jnp.sum(grad.astype(F32), axis=0, keepdims=True))
        return 0

    lax.fori_loop(0, 2, norm1_back, 0)

    def attend_back(n, _):
        yy, cc = turn(n)
        t = 2 * yy + cc
        at("dw0", n, 0)
        pl.when(n == 0)(functools.partial(pl.semaphore_wait, ready, len(me.peers)))
        mg = dot(ag_s[...], block(0, yy, cc, slice(512, 768)), NN)
        dq, dk, dv = [None] * 3, [None] * 3, [None] * 3
        for h, (qt, kt, vt, ot, qu, vu, ou) in enumerate(HEADS):
            if h:
                at("dw0", n, h)
            go = half_of(mg[:, 128:256] if ot == 5 else mg[:, 0:128], ou)
            inner = jnp.sum(go * a_s[t, :, tile(ot)].astype(F32), axis=-1, keepdims=True)
            go = go.astype(BF)
            p = p_s[t, h]
            dv[h] = dot(p, go, TN)
            ds = (p.astype(F32) * (dot(go, a_s[t, :, tile(vt)], NT) - inner)).astype(BF)
            dq[h] = dot(ds, a_s[t, :, tile(kt)], NN) * 0.125
            dk[h] = dot(ds, a_s[t, :, tile(qt)], TN) * 0.125
        da_s[:, tile(0)] = jnp.where(low, dq[0], dq[1]).astype(BF)
        da_s[:, tile(1)] = jnp.where(low, dk[0], dk[1]).astype(BF)
        da_s[:, tile(2)] = jnp.where(low, dv[0], dv[1]).astype(BF)
        da_s[:, tile(3)] = jnp.where(low, dq[2], dv[2]).astype(BF)
        da_s[:, tile(4)] = jnp.where(low, dk[2], 0.0).astype(BF)
        at("dw0", n, 3)
        sums = jnp.sum(da_s[...].astype(F32), axis=0, keepdims=True)
        for s, start in enumerate(SLOTS):
            m = start // 128
            gv_s[t, 7 + s : 8 + s, tile(m)] = half_of(sums[:, tile(m)], (start // 64) % 2)
        g0 = w.at[2, yy, cc]
        g0[:, :, 0:512] = dot(x_s[...], da_s[:, 0:512], TN).astype(BF).reshape(8, 96, 512)
        tail = dot(ag_s[...], mixed_of(t), TN)
        mixed = tail[:, 0:128] + dot(x_s[...], da_s[:, tile(4)], TN)
        g0[:, :, 512:640] = mixed.astype(BF).reshape(8, 96, 128)
        g0[:, :, 640:768] = tail[:, 128:256].astype(BF).reshape(8, 96, 128)
        at("dw0", n, 4)
        acc[...] += dot(da_s[...], block(0, yy, cc, slice(0, 640)), NT)
        return 0

    lax.fori_loop(0, 4, attend_back, 0)
    at("gx")
    dg_s[...] = acc[...].astype(BF)
    save_gx = pltpu.make_async_copy(dg_s, gx_hbm, io_sem.at[3])
    save_gx.start()
    at("small")

    for t in range(1, 4):
        gv_s[t, 1:7] = gv_s[0, 1:7]

    def collect(d, _):
        vec, head = spread(d)
        zz, xx = lax.div(d, 2), lax.rem(d, 2)
        val = gv_s[...].reshape(64, D)
        high = val.astype(BF)
        rest = (val - high.astype(F32)).astype(BF)
        is_vec = (iota((64, 1), 0) & 15) < 7
        got = jnp.where(is_vec, dot(high, vec, NT) + dot(rest, vec, NT), dot(high, head, NT) + dot(rest, head, NT))
        for t in range(4):
            sb[t % 2, xx, t // 2, zz] = got[16 * t : 16 * t + 16]
        return 0

    lax.fori_loop(0, 8, collect, 0)
    at("tail")
    grads_sent()
    for cp in [save_gx, save_small] + save_grads:
        cp.wait()


def run(r, *args):
    hbm, sm = pl.BlockSpec(memory_space=pl.ANY), pl.BlockSpec(memory_space=pltpu.SMEM)
    t = (SEQ, D)
    V = pltpu.VMEM
    items = len(ITEMS)
    gather = [DMA((items,))] * 3 + [DMA((items, 4))] * 3 + [DMA((items,))] * 2
    back = [DMA((3,))] * 3 + [DMA((3, 4))] * 4 + [DMA((3,))] * 2
    blocks = (2, 2, 8, 96, D)
    return pl.pallas_call(
        functools.partial(kernel, r),
        out_shape=(
            jax.ShapeDtypeStruct(t, BF),
            jax.ShapeDtypeStruct(t, BF),
            jax.ShapeDtypeStruct((3, 96, D), F32),
            jax.ShapeDtypeStruct((16, 128), F32),
        ),
        in_specs=[sm] + [hbm] * 17,
        out_specs=(hbm,) * 4,
        scratch_shapes=[V(i.shape, i.dtype) for i in args[3:]]
        + [DMA((15,)), V((3, 96, D), F32), V((16, 128), F32)]
        + [
            V((3, 96, D), BF), V((3,) + blocks, BF), V((2,) + blocks, BF), V((2,) + blocks, BF),
            V((16, 128), F32), V((2, 2, 2, 4, 16, 128), F32), V((64, D), F32), V((64, D), F32),
            V((4,) + t, BF), V((4, 3, SEQ, SEQ), BF), V(t, F32), V((SEQ, 128), F32), V(t, F32),
            V((4,) + t, BF), V((4,) + t, BF), V(t, BF),
            V(t, BF), V(t, BF), V(t, BF), V((D, SEQ), BF), V(t, BF), V(t, BF), V((SEQ, 640), BF), V((4, 16, D), F32),
            V((2, 2, 4, 16, 128), F32), V((2, 4, 16, 128), F32), V((4, 16, 128), F32), V((4, 16, 128), F32),
            DMA((8,)), DMA((1,)), *gather, DMA((7,)), DMA((7,)),
            *back, DMA((7,)), DMA((7,)), pltpu.SemaphoreType.REGULAR,
        ],
        compiler_params=pltpu.CompilerParams(
            collective_id=0, has_side_effects=True, vmem_limit_bytes=67043328
        ),
    )(*args)


FINAL = ((96, 192),) * 3 + ((192, 96), (96, D), (96, D), (3, 8), (3, 8)) + ((1, 96),) * 7


def finish_kernel(hid_hbm, gx_hbm, g_hbm, s_hbm, *refs):
    outs, scratch, sem = refs[:17], refs[17:-1], refs[-1]
    hid, gx, g, s = scratch[:4]
    wq, wk, wv, wo, w1, w2, bq, bv, *vectors = scratch[4:]

    def copy(n, src, dst):
        cp = pltpu.make_async_copy(src, dst, sem.at[n])
        cp.start()
        return cp

    get_g, get_s = copy(0, g_hbm, g), copy(1, s_hbm, s)
    get_hid, get_gx = copy(2, hid_hbm, hid), copy(3, gx_hbm, gx)
    get_g.wait()
    out = [copy(8, g.at[1], outs[6]), copy(9, g.at[2], outs[7])]
    a = g[0]
    for n, ref in enumerate((wq, wk, wv)):
        ref[:, 0:128] = a[:, 128 * n : 128 * n + 128]
    wq[:, 128:192] = a[:, 384:448]
    wk[:, 128:192] = a[:, 512:576]
    wv[:, 128:192] = a[:, 448:512]
    out += [copy(10 + n, ref, outs[2 + n]) for n, ref in enumerate((wq, wk, wv))]
    get_hid.wait()
    out.append(copy(4, hid, outs[0]))
    get_gx.wait()
    out.append(copy(5, gx, outs[1]))
    eye = (iota((96, 96), 0) == iota((96, 96), 1)).astype(F32)
    turned = lax.dot_general(
        a[:, 512:768], eye, (TN, ((), ())), preferred_element_type=F32, precision=lax.Precision.HIGHEST
    )
    wo[0:128] = turned[128:256]
    wo[128:192] = turned[64:128]
    out.append(copy(6, wo, outs[5]))
    get_s.wait()
    bq[...] = s[7:10, 0:8]
    bv[...] = s[10:13, 0:8]
    for n, ref in enumerate(vectors):
        ref[...] = s[n : n + 1, 0:96]
    out += [copy(13 + n, ref, outs[8 + n]) for n, ref in enumerate((bq, bv, *vectors))]
    for cp in out:
        cp.wait()


def finish(hidden, gx, grads, small):
    tokens = jax.ShapeDtypeStruct((SEQ, D), BF)
    hbm = pl.BlockSpec(memory_space=pl.ANY)
    out = pl.pallas_call(
        finish_kernel,
        out_shape=[tokens, tokens] + [jax.ShapeDtypeStruct(s, F32) for s in FINAL],
        in_specs=[hbm] * 4,
        out_specs=[hbm] * 17,
        scratch_shapes=[pltpu.VMEM((SEQ, D), BF)] * 2
        + [pltpu.VMEM((3, 96, D), F32), pltpu.VMEM((16, 128), F32)]
        + [pltpu.VMEM(s, F32) for s in FINAL]
        + [DMA((22,))],
    )(hidden, gx, grads, small)
    out = list(out)
    return out[:7] + [out[7].T] + out[8:11] + [i.reshape(96) for i in out[11:]]


def body(
    hidden_in, seq_lengths, out_grad, query_weight, key_weight, value_weight, output_weight, up_weight,
    down_weight, query_bias, value_bias, inner_bias, output_bias, down_bias, first_gain, first_shift,
    second_gain, second_shift,
):
    r = lax.axis_size("dp") // 8
    groups = [[g * r + i for i in range(r)] for g in range(8)]

    def whole(value, axis):
        if r == 1:
            return value
        value = value.astype(BF)
        return lax.all_gather(value, "dp", axis=axis, tiled=True, axis_index_groups=groups).astype(F32)

    def shard(value, axis):
        if r == 1:
            return value
        return lax.psum_scatter(value, "dp", scatter_dimension=axis, tiled=True, axis_index_groups=groups)

    vectors = (output_bias, down_bias, first_gain, first_shift, second_gain, second_shift)
    hidden, gx, gw, gs = run(
        r, seq_lengths, hidden_in, out_grad,
        whole(query_weight, 0), whole(key_weight, 0), whole(value_weight, 0), whole(output_weight, 1),
        whole(up_weight, 0), whole(down_weight.T, 0),
        whole(query_bias, 1), whole(value_bias, 1), whole(inner_bias, 1),
        *(whole(i.reshape(1, -1), 1) for i in vectors),
    )
    if r == 1:
        return tuple(finish(hidden, gx, gw, gs))
    gw = shard(gw, 1)
    gv = shard(gs[0:7, 0:96], 1)
    gh = shard(gs[7:13, 0:8], 1)
    a = gw[0]
    return (
        hidden,
        gx,
        jnp.concatenate([a[:, 0:128], a[:, 384:448]], axis=1),
        jnp.concatenate([a[:, 128:256], a[:, 512:576]], axis=1),
        jnp.concatenate([a[:, 256:384], a[:, 448:512]], axis=1),
        jnp.concatenate([a[:, 640:768], a[:, 576:640]], axis=1).T,
        gw[1],
        gw[2].T,
        gh[0:3],
        gh[3:6],
        gv[0:1],
        *(gv[i] for i in range(1, 7)),
    )


def solution(mesh):
    both, dp = P(("dp", "tensor"), None), P("dp")
    rows_first, columns_first = P("dp", "tensor"), P("tensor", "dp")
    weights = (rows_first,) * 3 + (columns_first, rows_first, columns_first)
    smalls = (columns_first,) * 3 + (dp,) * 6
    return jax.shard_map(
        body,
        mesh=mesh,
        in_specs=(P("dp", None),) * 3 + weights + smalls,
        out_specs=(both, both) + weights + smalls,
        check_vma=False,
    )
```
